128 devices in a mesh: body: 2 (over core), dom: 64 (over z, x, y).
Axes of the slice: x: 4, y: 4, z: 4, core: 2. Of those that a mesh axis runs over, the one named last changes fastest.
Arguments:
- displacement: float32 [2, 3, 262144], P('body', None, 'dom'), may hold values from -6 to 6
- connectivity: int32 [2, 8, 262144], P('body', None, 'dom'), may hold values from 0 to 4096
- plastic_strain: float32 [2, 6, 262144], P('body', None, 'dom'), may hold values from -4 to 4
- element_size: float32 [2, 262144], P('body', 'dom'), may hold values from 0.5 to 2
- yield_stress: float32 [2, 262144], P('body', 'dom'), may hold values from 0.3 to 3
- external_force: float32 [2, 3, 262144], P('body', None, 'dom'), may hold values from -12 to 12
- slave_disp: bfloat16 [2, 8192, 3, 128], P('body', 'dom'), may hold values from -6 to 6
- pair_owner: int32 [2, 8192, 2], P('body', 'dom'), may hold values from 0 to 63, all different within a row; in each aligned block of 128 rows (0 to 127, 128 to 255, ..., all dimensions but the last counted through in order) at most 8 rows name the same one
- pair_local: int32 [2, 8192, 2], P('body', 'dom'), may hold values from 0 to 127
- active: int32 [2, 8192], P('body', 'dom'), may hold values 0 or 1
- master_gap: float32 [2, 8192, 128], P('body', 'dom'), may hold values from -6 to 6
- master_normal: float32 [2, 8192, 3, 128], P('body', 'dom'), may hold values from -4 to 4
- master_disp: bfloat16 [2, 8192, 3, 128], P('body', 'dom'), may hold values from -6 to 6
- coupling: bfloat16 [128, 128], replicated, may hold values from -0.25 to 0.25
- quad_weight: float32 [128], replicated, may hold values from 0.1 to 1.9
Outputs:
- residual: float32 [2, 3, 262144], P('body', None, 'dom')
- slave_force: float32 [2, 8192, 3, 128], P('body', 'dom')
- master_force: float32 [2, 8192, 3, 128], P('body', 'dom')
The draws below stay inside these ranges and needn't reach their ends.
Inputs may be any that keep to these rules, and one draw needn't show every extreme that they name: `pair_owner`: among the rows of one device, at most 8 pairings name the same owner, a bound that some block reaches; a segment's two pairings name different owners.
All inputs are finite; a program needn't handle non-finite values. No bound on the sum of `active` on one device may be relied on, other than what follows from the above.
Results may differ from the reference program's by a relative error of at most 0.0055.
Values may be sent and summed in bfloat16 or wider, within the bound.
No kernel may reach another device: no remote copies, remote signals or barrier semaphores. Data moves between devices by JAX's collectives and lax.ppermute only.
A program may use at most 128 MiB of HBM per device.

```python
import math
import jax
import jax.numpy as jnp
import numpy as np
from jax import lax

PTS = 128
SEG_DEV = 128
GHOST = 2048
CAP = 8
SEGS = 8192
NODES = 262144
N_BODY = 2
N_DOM = 64


def draw_connectivity(key, part):
    nodes = jax.random.randint(key, (N_BODY, 8, NODES), 0, 2 * GHOST + 1)
    nodes = nodes.at[:, 0, 0].set(0)
    nodes = nodes.at[:, 7, NODES - 1].set(2 * GHOST)
    return nodes.astype(jnp.int32)


def touch_ends(entries, key, least, top_value):
    place = [jax.random.randint(jax.random.fold_in(key, axis), (), 0, length) for axis, length in enumerate(entries.shape)]
    widest = entries.shape.index(max(entries.shape))
    next_to = place[:widest] + [(place[widest] + 1) % entries.shape[widest]] + place[widest + 1:]
    return entries.at[tuple(place)].set(least).at[tuple(next_to)].set(top_value)


def block_levels(key, extent, shards, least, largest):
    factor_of, own = 1.0, jax.random.fold_in(key, 6)
    for axis_at, blocks in shards:
        draws = jnp.exp(jax.random.uniform(jax.random.fold_in(own, axis_at), (blocks,), jnp.float32, least / len(shards), largest / len(shards)))
        factor_of = factor_of * jnp.repeat(draws, extent[axis_at] // blocks).reshape([-1 if axis == axis_at else 1 for axis in range(len(extent))])
    return factor_of


def assign_block(key, own, number, rows, count, top, bound, skew):
    ranking = jax.random.permutation(key, count)
    crowded, common = load_shares(count, rows * top, bound, skew, True), load_shares(count, rows * top, bound, skew, False)
    places = jnp.arange(count)

    def named(tallies, turn):
        used = int((tallies > 0).sum())
        fixed = max(1, used // 4)
        shifted = fixed + (places - fixed + turn * (used - fixed)) % max(1, count - fixed)
        return jnp.zeros((count,), jnp.int32).at[ranking[jnp.where(places < fixed, places, shifted)]].set(jnp.asarray(tallies, jnp.int32))

    tallies = jnp.where(number % 4 == 0, named(crowded, number // 4), named(common, number - number // 4 - 1))
    mixed = jax.random.permutation(jax.random.fold_in(own, 3), count)
    source_of, sink = mixed[0:count // 2 * 2:2], mixed[1:count // 2 * 2:2]
    room = jnp.minimum(tallies[source_of] - 1, bound - tallies[sink]) // 2
    room = jnp.where((source_of == ranking[0]) | (sink == ranking[0]) | (tallies[sink] == 0), 0, jnp.maximum(room, 0))
    shifted = jax.random.randint(jax.random.fold_in(own, 4), (count // 2,), 0, 1 << 20) % (room + 1)
    tallies = tallies.at[source_of].add(-shifted).at[sink].add(shifted)
    labels = jnp.searchsorted(jnp.cumsum(tallies), jnp.arange(rows * top), side="right").astype(jnp.int32)
    listing = labels.reshape(top, rows).T
    listing = listing[jax.random.permutation(jax.random.fold_in(own, 1), rows)]
    turn = jax.random.randint(jax.random.fold_in(own, 2), (rows, 1), 0, top)
    return jnp.take_along_axis(listing, (jnp.arange(top)[None, :] + turn) % top, axis=1)


def load_shares(number_of, total, limit, skew, full):
    loads = [(1 << 20) // math.isqrt(standing ** skew) + 1 for standing in range(1, number_of + 1)]
    largest = limit if full else min(limit, max(-(-total // number_of), total * loads[0] // sum(loads)))
    least = 1 if total - largest >= number_of - 1 else 0
    holding, surplus = [largest] + [least] * (number_of - 1), total - largest - least * (number_of - 1)
    while surplus > 0:
        candidates = [i for i in range(1, number_of) if holding[i] < largest] or [i for i in range(1, number_of) if holding[i] < limit]
        mass, budget = sum([loads[i] for i in candidates]), surplus
        for i in candidates:
            addition = min(limit - holding[i], max(1, budget * loads[i] // mass), surplus)
            holding[i] = holding[i] + addition
            surplus = surplus - addition
    return np.array(holding)


def normal_values(rng, shape, scale, most, split=(), kind=jnp.bfloat16):
    result = scale * jax.random.normal(rng, shape, jnp.float32)
    if split:
        result = result * block_levels(rng, shape, split, -0.22, 0.18)
    return jnp.clip(result, -most, most).astype(kind)


def setup_inputs(seed: int = 0) -> dict:
    key_list = jax.random.split(jax.random.key(seed), 16)
    displacement = normal_values(key_list[0], (N_BODY, 3, NODES), 1.0, 6.0, ((0, 2), (2, 64)), jnp.float32)
    connectivity = draw_connectivity(jax.random.fold_in(key_list[15], 71), 0)
    plastic_strain = normal_values(key_list[2], (N_BODY, 6, NODES), 0.3, 4.0, ((0, 2), (2, 64)), jnp.float32)
    element_size = jnp.clip(jnp.exp(math.log(2.0) - 1.3862944 * jax.random.uniform(key_list[3], (N_BODY, NODES), jnp.float32) ** block_levels(key_list[3], (N_BODY, NODES), ((0, 2), (1, 64)), -0.2, 0.2)), 0.5, 2.0)
    yield_stress = jnp.clip(jnp.exp(math.log(3.0) - 2.3025851 * jax.random.uniform(key_list[4], (N_BODY, NODES), jnp.float32) ** block_levels(key_list[4], (N_BODY, NODES), ((0, 2), (1, 64)), -0.2, 0.2)), 0.3, 3.0)
    external_force = normal_values(key_list[5], (N_BODY, 3, NODES), 2.0, 12.0, ((0, 2), (2, 64)), jnp.float32)
    slave_disp = normal_values(key_list[6], (N_BODY, SEGS, 3, PTS), 1.0, 6.0, ((0, 2), (1, 64)))
    pair_owner_keys = jax.random.split(jax.random.fold_in(key_list[7], 1), N_BODY * SEGS // SEG_DEV)
    pair_owner_turns = jax.random.permutation(jax.random.fold_in(key_list[7], 3), N_BODY * SEGS // SEG_DEV)
    pair_owner = jax.vmap(lambda own, number: assign_block(jax.random.fold_in(key_list[7], 2), own, number, SEG_DEV, N_DOM, 2, CAP, 2))(pair_owner_keys, pair_owner_turns).reshape((N_BODY, SEGS, 2))
    pair_local = touch_ends(jax.random.randint(key_list[8], (N_BODY, SEGS, 2), 0, SEG_DEV), jax.random.fold_in(key_list[8], 1), 0, SEG_DEV - 1).astype(jnp.int32)
    active = touch_ends((jax.random.randint(key_list[9], (N_BODY, SEGS), 0, 4) < 3).astype(jnp.int32), jax.random.fold_in(key_list[9], 1), 0, 1)
    master_gap = normal_values(key_list[10], (N_BODY, SEGS, PTS), 1.0, 6.0, ((0, 2), (1, 64)), jnp.float32)
    master_normal = normal_values(key_list[11], (N_BODY, SEGS, 3, PTS), 0.6, 4.0, ((0, 2), (1, 64)), jnp.float32)
    master_disp = normal_values(key_list[12], (N_BODY, SEGS, 3, PTS), 1.0, 6.0, ((0, 2), (1, 64)))
    coupling = normal_values(key_list[13], (PTS, PTS), (4 * PTS) ** -0.5, 0.25)
    quad_weight = jnp.clip(1.0 + 0.18 * jax.random.normal(key_list[14], (PTS,), jnp.float32), 0.1, 1.9)
    return {"displacement": displacement, "connectivity": connectivity, "plastic_strain": plastic_strain, "element_size": element_size, "yield_stress": yield_stress, "external_force": external_force, "slave_disp": slave_disp, "pair_owner": pair_owner, "pair_local": pair_local, "active": active, "master_gap": master_gap, "master_normal": master_normal, "master_disp": master_disp, "coupling": coupling, "quad_weight": quad_weight}


LAME_A = 1.0
LAME_B = 0.5
PENALTY = 2.0

def corner_table():
    rows = [[(2.0 * (a >> j & 1) - 1.0) / 4.0 for j in range(3)] for a in range(8)]
    return jnp.asarray(np.array(rows, dtype=np.float32))

def element_forces(nodal, strain_old, edge, yield_val):
    table = corner_table().astype(nodal.dtype)
    grad = jnp.einsum('iae,aj->ije', nodal, table, precision=lax.Precision.HIGHEST) / edge
    exx = grad[0, 0] - strain_old[0]
    eyy = grad[1, 1] - strain_old[1]
    ezz = grad[2, 2] - strain_old[2]
    exy = 0.5 * (grad[0, 1] + grad[1, 0]) - strain_old[3]
    eyz = 0.5 * (grad[1, 2] + grad[2, 1]) - strain_old[4]
    ezx = 0.5 * (grad[2, 0] + grad[0, 2]) - strain_old[5]
    trace = exx + eyy + ezz
    sxx = LAME_A * trace + 2.0 * LAME_B * exx
    syy = LAME_A * trace + 2.0 * LAME_B * eyy
    szz = LAME_A * trace + 2.0 * LAME_B * ezz
    sxy = 2.0 * LAME_B * exy
    syz = 2.0 * LAME_B * eyz
    szx = 2.0 * LAME_B * ezx
    mean = (sxx + syy + szz) / 3.0
    dxx, dyy, dzz = (sxx - mean, syy - mean, szz - mean)
    norm_dev = jnp.sqrt(dxx * dxx + dyy * dyy + dzz * dzz + 2.0 * (sxy * sxy + syz * syz + szx * szx))
    radius = jnp.sqrt(2.0 / 3.0) * yield_val
    factor = radius / jnp.maximum(norm_dev, radius)
    row_x = jnp.stack([mean + factor * dxx, factor * sxy, factor * szx])
    row_y = jnp.stack([factor * sxy, mean + factor * dyy, factor * syz])
    row_z = jnp.stack([factor * szx, factor * syz, mean + factor * dzz])
    stress = jnp.stack([row_x, row_y, row_z])
    return edge * edge * jnp.einsum('ije,aj->iae', stress, table, precision=lax.Precision.HIGHEST)

def reference(displacement, connectivity, plastic_strain, element_size, yield_stress, external_force, slave_disp, pair_owner, pair_local, active, master_gap, master_normal, master_disp, coupling, quad_weight):
    mortar = (jnp.eye(PTS, dtype=jnp.float32) + coupling.astype(jnp.float32)).astype(jnp.bfloat16)
    mortar_wide = mortar.astype(jnp.float32)
    residuals = []
    slave_out = []
    master_out = [None, None]
    for which in range(2):
        element_pos = jnp.arange(NODES, dtype=jnp.int32)
        glob = (element_pos[None, :] + connectivity[which] - GHOST).astype(jnp.int32)
        valid = ((glob >= 0) & (glob < NODES)).astype(displacement.dtype)
        index = jnp.clip(glob, 0, NODES - 1)
        nodal = displacement[which][:, index] * valid[None]
        forces = element_forces(nodal, plastic_strain[which], element_size[which], yield_stress[which])
        total = jnp.zeros((3, NODES), displacement.dtype).at[:, index].add(forces * valid[None])
        residuals.append(total - external_force[which])
    for which in range(2):
        other = 1 - which
        proj = jnp.einsum('scp,pq->scq', slave_disp[which].astype(jnp.float32), mortar_wide)
        rows = pair_owner[which] * SEG_DEV + pair_local[which]
        gap0 = master_gap[other][rows]
        normal = master_normal[other][rows]
        mdisp = master_disp[other][rows].astype(jnp.float32)
        gap = gap0 - lax.optimization_barrier(jnp.sum(normal * (proj[:, None] - mdisp), axis=2))
        act = active[which].astype(jnp.float32)[:, None, None]
        press = PENALTY * jnp.maximum(gap, 0.0) * act
        traction = quad_weight * press[:, :, None, :] * normal
        pair_sum = lax.optimization_barrier(jnp.sum(traction, axis=1)).astype(jnp.bfloat16)
        pair_sum = lax.optimization_barrier(pair_sum).astype(jnp.float32)
        slave_out.append(jnp.einsum('scq,pq->scp', pair_sum, mortar_wide))
        master_out[other] = jnp.zeros((SEGS, 3, PTS), traction.dtype).at[rows.reshape(-1)].add(-traction.reshape(-1, 3, PTS))
    return (jnp.stack(residuals), jnp.stack(slave_out), jnp.stack(master_out))
```

```python
import functools

import jax
import jax.numpy as jnp
import numpy as np
from jax import lax
from jax.experimental import pallas as pl
from jax.experimental.pallas import tpu as pltpu
from jax.sharding import PartitionSpec as P

LANES = 128
WINDOW = 40
HALO = 16
BLOCKS = 32
SLOTS = 8
PEERS = 64
SEG = 128
F32 = jnp.float32
BF16 = jnp.bfloat16
NT = (((1,), (1,)), ((), ()))
TN = (((0,), (0,)), ((), ()))
NN = (((1,), (0,)), ((), ()))


def dot(a, b, dims=NN):
    return lax.dot_general(a, b, dims, preferred_element_type=F32)


def iota(shape, dim, dtype=jnp.int32):
    return lax.broadcasted_iota(jnp.int32, shape, dim).astype(dtype)


def element_kernel(low, own, high, links, strain, edge_ref, yield_ref, ext, prev_out, next_out, own_out,
                   disp, lo_s, hi_s, force_s, acc):
    disp[:, 0:HALO, :] = low[...]
    disp[:, HALO : HALO + BLOCKS, :] = own[...]
    disp[:, HALO + BLOCKS : 2 * HALO + BLOCKS, :] = high[...]
    acc[...] = jnp.zeros_like(acc)
    lane = iota((8, LANES), 1)
    for m in range(BLOCKS // 8):
        nodal = []
        for a in range(8):
            reach = links[pl.ds(64 * m + a, 8, stride=8), :] + lane
            hi = reach >> 7
            lo = reach & 127
            lo_s[a * BLOCKS + 8 * m : a * BLOCKS + 8 * m + 8, :] = lo
            hi_s[a * BLOCKS + 8 * m : a * BLOCKS + 8 * m + 8, :] = hi
            got = [jnp.zeros((8, LANES), F32)] * 3
            for h in range(33):
                here = hi == h
                for i in range(3):
                    rows = disp[i, 8 * m + h : 8 * m + h + 8, :]
                    got[i] = jnp.where(here, jnp.take_along_axis(rows, lo, axis=1), got[i])
            nodal.append(got)
        edge = edge_ref[8 * m : 8 * m + 8, :]
        scale = 0.25 / edge
        grad = [[None] * 3 for _ in range(3)]
        for i in range(3):
            u = [nodal[a][i] for a in range(8)]
            for j in range(3):
                plus = [u[a] for a in range(8) if a >> j & 1]
                minus = [u[a] for a in range(8) if not a >> j & 1]
                total = sum(p - q for p, q in zip(plus, minus))
                grad[i][j] = total * scale
        old = [strain[c, 8 * m : 8 * m + 8, :] for c in range(6)]
        exx = grad[0][0] - old[0]
        eyy = grad[1][1] - old[1]
        ezz = grad[2][2] - old[2]
        exy = 0.5 * (grad[0][1] + grad[1][0]) - old[3]
        eyz = 0.5 * (grad[1][2] + grad[2][1]) - old[4]
        ezx = 0.5 * (grad[2][0] + grad[0][2]) - old[5]
        trace = exx + eyy + ezz
        sxx = trace + exx
        syy = trace + eyy
        szz = trace + ezz
        mean = (sxx + syy + szz) / 3.0
        dxx, dyy, dzz = sxx - mean, syy - mean, szz - mean
        size = jnp.sqrt(dxx * dxx + dyy * dyy + dzz * dzz + 2.0 * (exy * exy + eyz * eyz + ezx * ezx))
        radius = np.float32(np.sqrt(2.0 / 3.0)) * yield_ref[8 * m : 8 * m + 8, :]
        factor = radius / jnp.maximum(size, radius)
        area = 0.25 * edge * edge
        xy, yz, zx = area * factor * exy, area * factor * eyz, area * factor * ezx
        xx = area * (mean + factor * dxx)
        yy = area * (mean + factor * dyy)
        zz = area * (mean + factor * dzz)
        for i, (tx, ty, tz) in enumerate(((xx, xy, zx), (xy, yy, yz), (zx, yz, zz))):
            four = [tx + ty, ty - tx, tx - ty, -tx - ty]
            for a in range(8):
                pick = four[(0 if a & 1 else 1) if a & 2 else (2 if a & 1 else 3)]
                f = pick + tz if a & 4 else pick - tz
                force_s[i, a * BLOCKS + 8 * m : a * BLOCKS + 8 * m + 8, :] = f
    row = iota((WINDOW, LANES), 0)
    row_lane = iota((LANES, LANES), 0)
    for k in range(BLOCKS):
        left, right = [], []
        for a in range(8):
            r = a * BLOCKS + k
            hi = jnp.broadcast_to(hi_s[r : r + 1, :], (WINDOW, LANES))
            lo = jnp.broadcast_to(lo_s[r : r + 1, :], (LANES, LANES))
            here = hi == row
            parts = [
                jnp.where(here, jnp.broadcast_to(force_s[i, r : r + 1, :], (WINDOW, LANES)), 0.0) for i in range(3)
            ]
            left.append(jnp.concatenate(parts, axis=0).astype(BF16))
            right.append(jnp.where(lo == row_lane, 1.0, 0.0).astype(BF16))
        sums = dot(jnp.concatenate(left, axis=1), jnp.concatenate(right, axis=1), NT)
        for i in range(3):
            acc[i, k : k + WINDOW, :] += sums[i * WINDOW : (i + 1) * WINDOW]
    prev_out[...] = acc[:, 0:HALO, :]
    next_out[...] = acc[:, HALO + BLOCKS : 2 * HALO + BLOCKS, :]
    own_out[...] = acc[:, HALO : HALO + BLOCKS, :] - ext[...]


def finish_kernel(own, from_prev, from_next, out):
    out[:, 0:HALO, :] = own[:, 0:HALO, :] + from_prev[...]
    out[:, HALO:BLOCKS, :] = own[:, HALO:BLOCKS, :] + from_next[...]


def pack_kernel(owner, where, active, disp, send, place):
    names = iota((PEERS, SEG), 0)
    earlier = jnp.where(iota((SEG, SEG), 0) < iota((SEG, SEG), 1), 1.0, 0.0).astype(BF16)
    ones = jnp.ones((SEG, SEG), BF16)
    hot = [owner[k : k + 1, :] == names for k in range(2)]
    hot16 = [jnp.where(h, 1.0, 0.0).astype(BF16) for h in hot]
    before = [dot(hot16[0], earlier), dot(hot16[1], earlier) + dot(hot16[0], ones)]
    slots = iota((PEERS * SLOTS, SEG), 0)
    sent = jnp.zeros((PEERS * SLOTS, SEG), F32)
    meta = jnp.zeros((PEERS * SLOTS, SEG), F32)
    for k in range(2):
        rank = jnp.sum(jnp.where(hot[k], before[k], 0.0), axis=0, keepdims=True)
        slot = owner[k : k + 1, :] * SLOTS + rank.astype(jnp.int32)
        mark = ((where[k : k + 1, :] + 1) * active[...]).astype(F32)
        here = slot == slots
        sent = jnp.where(here, 1.0, sent)
        meta = jnp.where(here, mark, meta)
    sent = sent.astype(BF16)
    place[...] = sent
    for c in range(3):
        send[:, c * LANES : (c + 1) * LANES] = dot(sent, disp[c]).astype(BF16)
    send[:, 3 * LANES :] = dot(meta.astype(BF16), ones).astype(BF16)


def rows_kernel(gap, normal, mdisp, out):
    total = gap[...]
    for c in range(3):
        n = normal[c]
        total = total + n * mdisp[c].astype(F32)
        out[1 + c] = n
    out[0] = total


def mortar_of(coupling):
    eye = jnp.where(iota((LANES, LANES), 0) == iota((LANES, LANES), 1), 1.0, 0.0)
    return (eye + coupling[...].astype(F32)).astype(BF16)


def split(x):
    top = x.astype(BF16)
    return top, (x - top.astype(F32)).astype(BF16)


def master_kernel(got, rows, coupling, weight, back, force):
    mortar = mortar_of(coupling)
    table = [split(rows[c]) for c in range(4)]
    name = iota((SEG, LANES), 1, F32) + 1.0
    totals = [jnp.zeros((SEG, LANES), F32)] * 3
    for part in range(PEERS * SLOTS // SEG):
        span = slice(part * SEG, (part + 1) * SEG)
        hot = jnp.where(got[span, 3 * LANES :].astype(F32) == name, 1.0, 0.0).astype(BF16)
        gap, n0, n1, n2 = (dot(hot, t) + dot(hot, b) for t, b in table)
        normal = (n0, n1, n2)
        for c in range(3):
            gap = gap - normal[c] * dot(got[span, c * LANES : (c + 1) * LANES], mortar)
        press = weight[...] * (2.0 * jnp.maximum(gap, 0.0))
        for c in range(3):
            top, low = split(press * normal[c])
            back[span, c * LANES : (c + 1) * LANES] = top
            totals[c] = totals[c] + dot(hot, top, TN) + dot(hot, low, TN)
    for c in range(3):
        force[c] = -totals[c]


def slave_kernel(got, place, coupling, out):
    mortar = mortar_of(coupling)
    for c in range(3):
        pair = dot(place[...], got[:, c * LANES : (c + 1) * LANES], TN).astype(BF16)
        out[c] = dot(pair, mortar, NT)


def shape(*dims, dtype=F32):
    return jax.ShapeDtypeStruct(dims, dtype)


def call(kernel, outs, cost, scratch=()):
    return pl.pallas_call(
        kernel,
        out_shape=outs,
        scratch_shapes=scratch,
        cost_estimate=pl.CostEstimate(flops=cost, bytes_accessed=1 << 20, transcendentals=0),
        name=kernel.__name__,
    )


def shifted(block, distance):
    devices = range(PEERS)
    return lax.ppermute(block, "dom", [(i - distance, i) for i in devices if i - distance in devices])


def swapped(block):
    return lax.ppermute(block, "body", [(0, 1), (1, 0)])


def exchanged(block):
    return lax.all_to_all(block, "dom", split_axis=0, concat_axis=0, tiled=True)


def local(
    displacement,
    connectivity,
    plastic_strain,
    element_size,
    yield_stress,
    external_force,
    slave_disp,
    pair_owner,
    pair_local,
    active,
    master_gap,
    master_normal,
    master_disp,
    coupling,
    quad_weight,
):
    seg_major = lambda x: jnp.transpose(x[0], (1, 0, 2))
    send, place = call(
        pack_kernel,
        (shape(PEERS * SLOTS, 4 * LANES, dtype=BF16), shape(PEERS * SLOTS, SEG, dtype=BF16)),
        1 << 27,
    )(pair_owner[0].T, pair_local[0].T, active, seg_major(slave_disp))
    got = exchanged(send)

    own = displacement[0].reshape(3, BLOCKS, LANES)
    low = shifted(own[:, BLOCKS - HALO :], 1)
    high = shifted(own[:, :HALO], -1)
    rows = call(rows_kernel, shape(4, SEG, LANES), 1 << 20)(
        master_gap[0], seg_major(master_normal), seg_major(master_disp)
    )
    rows = swapped(rows)
    links = jnp.transpose(connectivity[0].reshape(8, BLOCKS, LANES), (1, 0, 2)).reshape(8 * BLOCKS, LANES)
    to_prev, to_next, own_force = call(
        element_kernel,
        (shape(3, HALO, LANES), shape(3, HALO, LANES), shape(3, BLOCKS, LANES)),
        1 << 32,
        (
            pltpu.VMEM((3, 2 * HALO + BLOCKS + 8, LANES), F32),
            pltpu.VMEM((8 * BLOCKS, LANES), jnp.int32),
            pltpu.VMEM((8 * BLOCKS, LANES), jnp.int32),
            pltpu.VMEM((3, 8 * BLOCKS, LANES), F32),
            pltpu.VMEM((3, 2 * HALO + BLOCKS + 8, LANES), F32),
        ),
    )(
        low,
        own,
        high,
        links,
        plastic_strain[0].reshape(6, BLOCKS, LANES),
        element_size.reshape(BLOCKS, LANES),
        yield_stress.reshape(BLOCKS, LANES),
        external_force[0].reshape(3, BLOCKS, LANES),
    )

    back, force = call(
        master_kernel, (shape(PEERS * SLOTS, 3 * LANES, dtype=BF16), shape(3, SEG, LANES)), 1 << 28
    )(got, rows, coupling, quad_weight.reshape(1, LANES))
    returned = exchanged(back)
    master_force = swapped(force)

    residual = call(finish_kernel, shape(3, BLOCKS, LANES), 1 << 20)(
        own_force, shifted(to_next, 1), shifted(to_prev, -1)
    )
    slave_force = call(slave_kernel, shape(3, SEG, LANES), 1 << 27)(returned, place, coupling)
    return (
        residual.reshape(1, 3, BLOCKS * LANES),
        jnp.transpose(slave_force, (1, 0, 2))[None],
        jnp.transpose(master_force, (1, 0, 2))[None],
    )


def solution(mesh):
    return jax.shard_map(
        local,
        mesh=mesh,
        in_specs=(
            P("body", None, "dom"),
            P("body", None, "dom"),
            P("body", None, "dom"),
            P("body", "dom"),
            P("body", "dom"),
            P("body", None, "dom"),
            P("body", "dom", None, None),
            P("body", "dom", None),
            P("body", "dom", None),
            P("body", "dom"),
            P("body", "dom", None),
            P("body", "dom", None, None),
            P("body", "dom", None, None),
            P(),
            P(),
        ),
        out_specs=(
            P("body", None, "dom"),
            P("body", "dom", None, None),
            P("body", "dom", None, None),
        ),
        check_vma=False,
    )
```

```python
import functools

import jax
import jax.numpy as jnp
import numpy as np
from jax import lax
from jax.experimental import pallas as pl
from jax.experimental.pallas import tpu as pltpu
from jax.sharding import PartitionSpec as P

LANES = 128
WINDOW = 48
HALO = 16
BLOCKS = 32
SLOTS = 8
PEERS = 64
SEG = 128
F32 = jnp.float32
BF16 = jnp.bfloat16
NT = (((1,), (1,)), ((), ()))
TN = (((0,), (0,)), ((), ()))
NN = (((1,), (0,)), ((), ()))


def dot(a, b, dims=NN):
    return lax.dot_general(a, b, dims, preferred_element_type=F32)


def iota(shape, dim, dtype=jnp.int32):
    return lax.broadcasted_iota(jnp.int32, shape, dim).astype(dtype)


def element_kernel(low, own, high, links, strain, edge_ref, yield_ref, ext, prev_out, next_out, own_out,
                   disp, lo_s, hi_s, force_s, acc):
    disp[:, 0:HALO, :] = low[...]
    disp[:, HALO : HALO + BLOCKS, :] = own[...]
    disp[:, HALO + BLOCKS : 2 * HALO + BLOCKS, :] = high[...]
    acc[...] = jnp.zeros_like(acc)
    lane = iota((8, LANES), 1)
    block = iota((8, LANES), 0)
    for m in range(BLOCKS // 8):
        nodal = []
        for a in range(8):
            reach = links[pl.ds(64 * m + a, 8, stride=8), :] + lane
            hi = reach >> 7
            lo = reach & 127
            lo_s[a * BLOCKS + 8 * m : a * BLOCKS + 8 * m + 8, :] = lo.astype(F32)
            hi_s[a * BLOCKS + 8 * m : a * BLOCKS + 8 * m + 8, :] = (hi + block).astype(F32)
            got = [jnp.zeros((8, LANES), F32)] * 3
            for h in range(33):
                here = hi == h
                for i in range(3):
                    rows = disp[i, 8 * m + h : 8 * m + h + 8, :]
                    got[i] = jnp.where(here, jnp.take_along_axis(rows, lo, axis=1), got[i])
            nodal.append(got)
        edge = edge_ref[8 * m : 8 * m + 8, :]
        scale = 0.25 / edge
        grad = [[None] * 3 for _ in range(3)]
        for i in range(3):
            u = [nodal[a][i] for a in range(8)]
            for j in range(3):
                plus = [u[a] for a in range(8) if a >> j & 1]
                minus = [u[a] for a in range(8) if not a >> j & 1]
                total = sum(p - q for p, q in zip(plus, minus))
                grad[i][j] = total * scale
        old = [strain[c, 8 * m : 8 * m + 8, :] for c in range(6)]
        exx = grad[0][0] - old[0]
        eyy = grad[1][1] - old[1]
        ezz = grad[2][2] - old[2]
        exy = 0.5 * (grad[0][1] + grad[1][0]) - old[3]
        eyz = 0.5 * (grad[1][2] + grad[2][1]) - old[4]
        ezx = 0.5 * (grad[2][0] + grad[0][2]) - old[5]
        trace = exx + eyy + ezz
        sxx = trace + exx
        syy = trace + eyy
        szz = trace + ezz
        mean = (sxx + syy + szz) / 3.0
        dxx, dyy, dzz = sxx - mean, syy - mean, szz - mean
        size = jnp.sqrt(dxx * dxx + dyy * dyy + dzz * dzz + 2.0 * (exy * exy + eyz * eyz + ezx * ezx))
        radius = np.float32(np.sqrt(2.0 / 3.0)) * yield_ref[8 * m : 8 * m + 8, :]
        factor = radius / jnp.maximum(size, radius)
        area = 0.25 * edge * edge
        xy, yz, zx = area * factor * exy, area * factor * eyz, area * factor * ezx
        xx = area * (mean + factor * dxx)
        yy = area * (mean + factor * dyy)
        zz = area * (mean + factor * dzz)
        for i, (tx, ty, tz) in enumerate(((xx, xy, zx), (xy, yy, yz), (zx, yz, zz))):
            four = [tx + ty, ty - tx, tx - ty, -tx - ty]
            for a in range(8):
                pick = four[(0 if a & 1 else 1) if a & 2 else (2 if a & 1 else 3)]
                f = pick + tz if a & 4 else pick - tz
                force_s[i, a * BLOCKS + 8 * m : a * BLOCKS + 8 * m + 8, :] = f
    row = iota((16, LANES), 0, F32)
    rows = [(row + 16.0 * t).astype(BF16) for t in range(8)]
    zero = jnp.zeros((16, LANES), BF16)
    one = jnp.ones((16, LANES), BF16)

    def wide(ref, *at):
        return jnp.broadcast_to(ref[at], (16, LANES)).astype(BF16)

    for m in range(BLOCKS // 8):
        sums = jnp.zeros((3 * WINDOW, LANES), F32)
        for s in range(8):
            left, right = [], []
            for a in range(8):
                at = slice(a * BLOCKS + 8 * m + s, a * BLOCKS + 8 * m + s + 1)
                hi = wide(hi_s, at, slice(None))
                lo = wide(lo_s, at, slice(None))
                here = [hi == rows[t] for t in range(WINDOW // 16)]
                parts = []
                for i in range(3):
                    f = wide(force_s, i, at, slice(None))
                    parts += [jnp.where(h, f, zero) for h in here]
                left.append(jnp.concatenate(parts, axis=0))
                right.append(jnp.concatenate([jnp.where(lo == r, one, zero) for r in rows], axis=0))
            sums = sums + dot(jnp.concatenate(left, axis=1), jnp.concatenate(right, axis=1), NT)
        for i in range(3):
            acc[i, 8 * m : 8 * m + WINDOW, :] += sums[i * WINDOW : (i + 1) * WINDOW]
    prev_out[...] = acc[:, 0:HALO, :]
    next_out[...] = acc[:, HALO + BLOCKS : 2 * HALO + BLOCKS, :]
    own_out[...] = acc[:, HALO : HALO + BLOCKS, :] - ext[...]


def finish_kernel(own, from_prev, from_next, force, out, force_out):
    force_out[...] = force[...]
    out[:, 0:HALO, :] = own[:, 0:HALO, :] + from_prev[...]
    out[:, HALO:BLOCKS, :] = own[:, HALO:BLOCKS, :] + from_next[...]


def pack_kernel(owner, where, active, disp, gap, normal, mdisp, send, place, rows):
    names = iota((PEERS, SEG), 0)
    earlier = jnp.where(iota((SEG, SEG), 0) < iota((SEG, SEG), 1), 1.0, 0.0).astype(BF16)
    ones = jnp.ones((SEG, SEG), BF16)
    hot = [owner[k : k + 1, :] == names for k in range(2)]
    hot16 = [jnp.where(h, 1.0, 0.0).astype(BF16) for h in hot]
    before = [dot(hot16[0], earlier), dot(hot16[1], earlier) + dot(hot16[0], ones)]
    slots = iota((PEERS * SLOTS, SEG), 0)
    sent = jnp.zeros((PEERS * SLOTS, SEG), F32)
    meta = jnp.zeros((PEERS * SLOTS, SEG), F32)
    for k in range(2):
        rank = jnp.sum(jnp.where(hot[k], before[k], 0.0), axis=0, keepdims=True)
        slot = owner[k : k + 1, :] * SLOTS + rank.astype(jnp.int32)
        mark = ((where[k : k + 1, :] + 1) * active[...]).astype(F32)
        here = slot == slots
        sent = jnp.where(here, 1.0, sent)
        meta = jnp.where(here, mark, meta)
    sent = sent.astype(BF16)
    place[...] = sent
    for c in range(3):
        send[:, c * LANES : (c + 1) * LANES] = dot(sent, disp[c]).astype(BF16)
    send[:, 3 * LANES :] = dot(meta.astype(BF16), ones).astype(BF16)
    total = gap[...]
    for c in range(3):
        n = normal[c]
        total = total + n * mdisp[c].astype(F32)
        rows[1 + c] = n
    rows[0] = total


def mortar_of(coupling):
    eye = jnp.where(iota((LANES, LANES), 0) == iota((LANES, LANES), 1), 1.0, 0.0)
    return (eye + coupling[...].astype(F32)).astype(BF16)


def split(x):
    top = x.astype(BF16)
    return top, (x - top.astype(F32)).astype(BF16)


def master_kernel(got, rows, coupling, weight, back, force):
    mortar = mortar_of(coupling)
    table = [split(rows[c]) for c in range(4)]
    name = iota((SEG, LANES), 1, F32) + 1.0
    totals = [jnp.zeros((SEG, LANES), F32)] * 3
    for part in range(PEERS * SLOTS // SEG):
        span = slice(part * SEG, (part + 1) * SEG)
        hot = jnp.where(got[span, 3 * LANES :].astype(F32) == name, 1.0, 0.0).astype(BF16)
        gap, n0, n1, n2 = (dot(hot, t) + dot(hot, b) for t, b in table)
        normal = (n0, n1, n2)
        for c in range(3):
            gap = gap - normal[c] * dot(got[span, c * LANES : (c + 1) * LANES], mortar)
        press = weight[...] * (2.0 * jnp.maximum(gap, 0.0))
        for c in range(3):
            top, low = split(press * normal[c])
            back[span, c * LANES : (c + 1) * LANES] = top
            totals[c] = totals[c] + dot(hot, top, TN) + dot(hot, low, TN)
    for c in range(3):
        force[c] = -totals[c]


def slave_kernel(got, place, coupling, out):
    mortar = mortar_of(coupling)
    for c in range(3):
        pair = dot(place[...], got[:, c * LANES : (c + 1) * LANES], TN).astype(BF16)
        out[c] = dot(pair, mortar, NT)


def shape(*dims, dtype=F32):
    return jax.ShapeDtypeStruct(dims, dtype)


VMEM = pl.BlockSpec(memory_space=pltpu.VMEM)


def call(kernel, ins, outs, cost, scratch=()):
    return pl.pallas_call(
        kernel,
        out_shape=outs,
        in_specs=[VMEM] * ins,
        out_specs=jax.tree.map(lambda _: VMEM, outs),
        scratch_shapes=scratch,
        compiler_params=pltpu.CompilerParams(vmem_limit_bytes=8 << 20),
        cost_estimate=pl.CostEstimate(flops=cost, bytes_accessed=1 << 20, transcendentals=0),
        name=kernel.__name__,
    )


def shifted(block, distance):
    devices = range(PEERS)
    return lax.ppermute(block, "dom", [(i - distance, i) for i in devices if i - distance in devices])


def swapped(block):
    return lax.ppermute(block, "body", [(0, 1), (1, 0)])


def exchanged(block):
    return lax.all_to_all(block, "dom", split_axis=0, concat_axis=0, tiled=True)


def local(
    displacement,
    connectivity,
    plastic_strain,
    element_size,
    yield_stress,
    external_force,
    slave_disp,
    pair_owner,
    pair_local,
    active,
    master_gap,
    master_normal,
    master_disp,
    coupling,
    quad_weight,
):
    seg_major = lambda x: jnp.transpose(x[0], (1, 0, 2))
    send, place, rows = call(
        pack_kernel,
        7,
        (
            shape(PEERS * SLOTS, 4 * LANES, dtype=BF16),
            shape(PEERS * SLOTS, SEG, dtype=BF16),
            shape(4, SEG, LANES),
        ),
        1 << 27,
    )(
        pair_owner[0].T,
        pair_local[0].T,
        active,
        seg_major(slave_disp),
        master_gap[0],
        seg_major(master_normal),
        seg_major(master_disp),
    )
    got = exchanged(send)

    own = displacement[0].reshape(3, BLOCKS, LANES)
    low = shifted(own[:, BLOCKS - HALO :], 1)
    high = shifted(own[:, :HALO], -1)
    rows = swapped(rows)
    links = jnp.transpose(connectivity[0].reshape(8, BLOCKS, LANES), (1, 0, 2)).reshape(8 * BLOCKS, LANES)
    to_prev, to_next, own_force = call(
        element_kernel,
        8,
        (shape(3, HALO, LANES), shape(3, HALO, LANES), shape(3, BLOCKS, LANES)),
        1 << 32,
        (
            pltpu.VMEM((3, 2 * HALO + BLOCKS + 16, LANES), F32),
            pltpu.VMEM((8 * BLOCKS, LANES), F32),
            pltpu.VMEM((8 * BLOCKS, LANES), F32),
            pltpu.VMEM((3, 8 * BLOCKS, LANES), F32),
            pltpu.VMEM((3, 2 * HALO + BLOCKS + 16, LANES), F32),
        ),
    )(
        low,
        own,
        high,
        links,
        plastic_strain[0].reshape(6, BLOCKS, LANES),
        element_size.reshape(BLOCKS, LANES),
        yield_stress.reshape(BLOCKS, LANES),
        external_force[0].reshape(3, BLOCKS, LANES),
    )

    got, to_prev, to_next = lax.optimization_barrier((got, to_prev, to_next))
    back, force = call(
        master_kernel, 4, (shape(PEERS * SLOTS, 3 * LANES, dtype=BF16), shape(3, SEG, LANES)), 1 << 28
    )(got, rows, coupling, quad_weight.reshape(1, LANES))
    returned = exchanged(back)
    residual, master_force = call(finish_kernel, 4, (shape(3, BLOCKS, LANES), shape(3, SEG, LANES)), 1 << 20)(
        own_force, shifted(to_next, 1), shifted(to_prev, -1), swapped(force)
    )
    slave_force = call(slave_kernel, 3, shape(3, SEG, LANES), 1 << 27)(returned, place, coupling)
    return (
        residual.reshape(1, 3, BLOCKS * LANES),
        jnp.transpose(slave_force, (1, 0, 2))[None],
        jnp.transpose(master_force, (1, 0, 2))[None],
    )


def solution(mesh):
    return jax.shard_map(
        local,
        mesh=mesh,
        in_specs=(
            P("body", None, "dom"),
            P("body", None, "dom"),
            P("body", None, "dom"),
            P("body", "dom"),
            P("body", "dom"),
            P("body", None, "dom"),
            P("body", "dom", None, None),
            P("body", "dom", None),
            P("body", "dom", None),
            P("body", "dom"),
            P("body", "dom", None),
            P("body", "dom", None, None),
            P("body", "dom", None, None),
            P(),
            P(),
        ),
        out_specs=(
            P("body", None, "dom"),
            P("body", "dom", None, None),
            P("body", "dom", None, None),
        ),
        check_vma=False,
    )
```

```python
import jax
import jax.numpy as jnp
import numpy as np
from jax import lax
from jax.experimental import pallas as pl
from jax.experimental.pallas import tpu as pltpu
from jax.sharding import PartitionSpec as P


LANES = 128
WINDOW = 48
HALO = 16
BLOCKS = 32
SLOTS = 8
PEERS = 64
SEG = 128
F32 = jnp.float32
BF16 = jnp.bfloat16
NT = (((1,), (1,)), ((), ()))
TN = (((0,), (0,)), ((), ()))
NN = (((1,), (0,)), ((), ()))


def dot(a, b, dims=NN):
    return lax.dot_general(a, b, dims, preferred_element_type=F32)


def iota(shape, dim, dtype=jnp.int32):
    return lax.broadcasted_iota(jnp.int32, shape, dim).astype(dtype)


def element_kernel(parity, far, near, own, links, strain, edge_ref, yield_ref, ext, far_out, near_out, own_out,
                   disp, lo_s, hi_s, force_s, acc):
    odd = parity[0:1, :] == 1
    disp[:, 0:HALO, :] = jnp.where(odd, near[...], far[...])
    disp[:, HALO : HALO + BLOCKS, :] = own[...]
    disp[:, HALO + BLOCKS : 2 * HALO + BLOCKS, :] = jnp.where(odd, far[...], near[...])
    acc[...] = jnp.zeros_like(acc)
    lane = iota((8, LANES), 1)
    block = iota((8, LANES), 0)
    for m in range(BLOCKS // 8):
        nodal = []
        for a in range(8):
            reach = links[pl.ds(64 * m + a, 8, stride=8), :] + lane
            hi = reach >> 7
            lo = reach & 127
            lo_s[a * BLOCKS + 8 * m : a * BLOCKS + 8 * m + 8, :] = lo.astype(F32)
            hi_s[a * BLOCKS + 8 * m : a * BLOCKS + 8 * m + 8, :] = (hi + block).astype(F32)
            got = [jnp.zeros((8, LANES), F32)] * 3
            for h in range(33):
                here = hi == h
                for i in range(3):
                    rows = disp[i, 8 * m + h : 8 * m + h + 8, :]
                    got[i] = jnp.where(here, jnp.take_along_axis(rows, lo, axis=1), got[i])
            nodal.append(got)
        edge = edge_ref[8 * m : 8 * m + 8, :]
        scale = 0.25 / edge
        grad = [[None] * 3 for _ in range(3)]
        for i in range(3):
            u = [nodal[a][i] for a in range(8)]
            for j in range(3):
                plus = [u[a] for a in range(8) if a >> j & 1]
                minus = [u[a] for a in range(8) if not a >> j & 1]
                total = sum(p - q for p, q in zip(plus, minus))
                grad[i][j] = total * scale
        old = [strain[c, 8 * m : 8 * m + 8, :] for c in range(6)]
        exx = grad[0][0] - old[0]
        eyy = grad[1][1] - old[1]
        ezz = grad[2][2] - old[2]
        exy = 0.5 * (grad[0][1] + grad[1][0]) - old[3]
        eyz = 0.5 * (grad[1][2] + grad[2][1]) - old[4]
        ezx = 0.5 * (grad[2][0] + grad[0][2]) - old[5]
        trace = exx + eyy + ezz
        sxx = trace + exx
        syy = trace + eyy
        szz = trace + ezz
        mean = (sxx + syy + szz) / 3.0
        dxx, dyy, dzz = sxx - mean, syy - mean, szz - mean
        size = jnp.sqrt(dxx * dxx + dyy * dyy + dzz * dzz + 2.0 * (exy * exy + eyz * eyz + ezx * ezx))
        radius = np.float32(np.sqrt(2.0 / 3.0)) * yield_ref[8 * m : 8 * m + 8, :]
        factor = radius / jnp.maximum(size, radius)
        area = 0.25 * edge * edge
        xy, yz, zx = area * factor * exy, area * factor * eyz, area * factor * ezx
        xx = area * (mean + factor * dxx)
        yy = area * (mean + factor * dyy)
        zz = area * (mean + factor * dzz)
        for i, (tx, ty, tz) in enumerate(((xx, xy, zx), (xy, yy, yz), (zx, yz, zz))):
            four = [tx + ty, ty - tx, tx - ty, -tx - ty]
            for a in range(8):
                pick = four[(0 if a & 1 else 1) if a & 2 else (2 if a & 1 else 3)]
                f = pick + tz if a & 4 else pick - tz
                force_s[i, a * BLOCKS + 8 * m : a * BLOCKS + 8 * m + 8, :] = f
    row = iota((16, LANES), 0, F32)
    rows = [(row + 16.0 * t).astype(BF16) for t in range(8)]
    zero = jnp.zeros((16, LANES), BF16)
    one = jnp.ones((16, LANES), BF16)

    def wide(ref, *at):
        return jnp.broadcast_to(ref[at], (16, LANES)).astype(BF16)

    for m in range(BLOCKS // 8):
        sums = jnp.zeros((3 * WINDOW, LANES), F32)
        for s in range(8):
            left, right = [], []
            for a in range(8):
                at = slice(a * BLOCKS + 8 * m + s, a * BLOCKS + 8 * m + s + 1)
                hi = wide(hi_s, at, slice(None))
                lo = wide(lo_s, at, slice(None))
                here = [hi == rows[t] for t in range(WINDOW // 16)]
                parts = []
                for i in range(3):
                    f = wide(force_s, i, at, slice(None))
                    parts += [jnp.where(h, f, zero) for h in here]
                left.append(jnp.concatenate(parts, axis=0))
                right.append(jnp.concatenate([jnp.where(lo == r, one, zero) for r in rows], axis=0))
            sums = sums + dot(jnp.concatenate(left, axis=1), jnp.concatenate(right, axis=1), NT)
        for i in range(3):
            acc[i, 8 * m : 8 * m + WINDOW, :] += sums[i * WINDOW : (i + 1) * WINDOW]
    low, high = acc[:, 0:HALO, :], acc[:, HALO + BLOCKS : 2 * HALO + BLOCKS, :]
    far_out[...] = jnp.where(odd, high, low)
    near_out[...] = jnp.where(odd, low, high)
    own_out[...] = acc[:, HALO : HALO + BLOCKS, :] - ext[...]


def finish_kernel(parity, own, far, near, force, out, force_out):
    odd = parity[0:1, :] == 1
    force_out[...] = force[...]
    out[:, 0:HALO, :] = own[:, 0:HALO, :] + jnp.where(odd, near[...], far[...])
    out[:, HALO:BLOCKS, :] = own[:, HALO:BLOCKS, :] + jnp.where(odd, far[...], near[...])


def pack_kernel(owner, where, active, disp, send, place):
    names = iota((PEERS, SEG), 0)
    earlier = jnp.where(iota((SEG, SEG), 0) < iota((SEG, SEG), 1), 1.0, 0.0).astype(BF16)
    ones = jnp.ones((SEG, SEG), BF16)
    hot = [owner[k : k + 1, :] == names for k in range(2)]
    hot16 = [jnp.where(h, 1.0, 0.0).astype(BF16) for h in hot]
    before = [dot(hot16[0], earlier), dot(hot16[1], earlier) + dot(hot16[0], ones)]
    slots = iota((PEERS * SLOTS, SEG), 0)
    sent = jnp.zeros((PEERS * SLOTS, SEG), F32)
    meta = jnp.zeros((PEERS * SLOTS, SEG), F32)
    for k in range(2):
        rank = jnp.sum(jnp.where(hot[k], before[k], 0.0), axis=0, keepdims=True)
        slot = owner[k : k + 1, :] * SLOTS + rank.astype(jnp.int32)
        mark = ((where[k : k + 1, :] + 1) * active[...]).astype(F32)
        here = slot == slots
        sent = jnp.where(here, 1.0, sent)
        meta = jnp.where(here, mark, meta)
    sent = sent.astype(BF16)
    place[...] = sent
    for c in range(3):
        send[:, c * LANES : (c + 1) * LANES] = dot(sent, disp[c]).astype(BF16)
    send[:, 3 * LANES :] = dot(meta.astype(BF16), ones).astype(BF16)


def rows_kernel(gap, normal, mdisp, rows):
    total = gap[...]
    for c in range(3):
        n = normal[c]
        total = total + n * mdisp[c].astype(F32)
        rows[1 + c] = n
    rows[0] = total


def mortar_of(coupling):
    eye = jnp.where(iota((LANES, LANES), 0) == iota((LANES, LANES), 1), 1.0, 0.0)
    return (eye + coupling[...].astype(F32)).astype(BF16)


def split(x):
    top = x.astype(BF16)
    return top, (x - top.astype(F32)).astype(BF16)


def master_kernel(got, rows, coupling, weight, back, force):
    mortar = mortar_of(coupling)
    table = [split(rows[c]) for c in range(4)]
    name = iota((SEG, LANES), 1, F32) + 1.0
    totals = [jnp.zeros((SEG, LANES), F32)] * 3
    for part in range(PEERS * SLOTS // SEG):
        span = slice(part * SEG, (part + 1) * SEG)
        hot = jnp.where(got[span, 3 * LANES :].astype(F32) == name, 1.0, 0.0).astype(BF16)
        gap, n0, n1, n2 = (dot(hot, t) + dot(hot, b) for t, b in table)
        normal = (n0, n1, n2)
        for c in range(3):
            gap = gap - normal[c] * dot(got[span, c * LANES : (c + 1) * LANES], mortar)
        press = weight[...] * (2.0 * jnp.maximum(gap, 0.0))
        for c in range(3):
            top, low = split(press * normal[c])
            back[span, c * LANES : (c + 1) * LANES] = top
            totals[c] = totals[c] + dot(hot, top, TN) + dot(hot, low, TN)
    for c in range(3):
        force[c] = -totals[c]


def slave_kernel(got, place, coupling, out):
    mortar = mortar_of(coupling)
    for c in range(3):
        pair = dot(place[...], got[:, c * LANES : (c + 1) * LANES], TN).astype(BF16)
        out[c] = dot(pair, mortar, NT)


def shape(*dims, dtype=F32):
    return jax.ShapeDtypeStruct(dims, dtype)


VMEM = pl.BlockSpec(memory_space=pltpu.VMEM)


def call(kernel, ins, outs, cost, scratch=(), grant=8 << 20):
    return pl.pallas_call(
        kernel,
        out_shape=outs,
        in_specs=[VMEM] * ins if ins > 0 else [pl.BlockSpec()] * -ins,
        out_specs=jax.tree.map(lambda _: VMEM if ins > 0 else pl.BlockSpec(), outs),
        scratch_shapes=scratch,
        compiler_params=pltpu.CompilerParams(vmem_limit_bytes=grant),
        cost_estimate=pl.CostEstimate(flops=cost, bytes_accessed=1 << 20, transcendentals=0),
    )


def paired(block, first):
    route = [(i, i + 1) for i in range(first, PEERS - 1, 2)]
    return lax.ppermute(block, "dom", route + [(j, i) for i, j in route])


def swapped(block):
    return lax.ppermute(block, "body", [(0, 1), (1, 0)])


def exchanged(block):
    return lax.all_to_all(block, "dom", split_axis=0, concat_axis=0, tiled=True)


def local(
    displacement,
    connectivity,
    plastic_strain,
    element_size,
    yield_stress,
    external_force,
    slave_disp,
    pair_owner,
    pair_local,
    active,
    master_gap,
    master_normal,
    master_disp,
    coupling,
    quad_weight,
):
    seg_major = lambda x: jnp.transpose(x[0], (1, 0, 2))
    send, place = call(
        pack_kernel,
        -4,
        (shape(PEERS * SLOTS, 4 * LANES, dtype=BF16), shape(PEERS * SLOTS, SEG, dtype=BF16)),
        1 << 27,
        grant=60 << 20,
    )(pair_owner[0].T, pair_local[0].T, active, seg_major(slave_disp))
    got = exchanged(send)

    own = displacement[0].reshape(3, BLOCKS, LANES)
    odd = lax.axis_index("dom") & 1
    parity = jnp.full((8, LANES), odd, jnp.int32)
    first, last = own[:, :HALO], own[:, BLOCKS - HALO :]
    far = paired(jnp.where(odd == 1, last, first), 1)
    near = paired(jnp.where(odd == 1, first, last), 0)
    rows = call(rows_kernel, 3, shape(4, SEG, LANES), 1 << 20)(
        master_gap[0], seg_major(master_normal), seg_major(master_disp)
    )
    rows = swapped(rows)
    links = jnp.transpose(connectivity[0].reshape(8, BLOCKS, LANES), (1, 0, 2)).reshape(8 * BLOCKS, LANES)
    far_force, near_force, own_force = call(
        element_kernel,
        9,
        (shape(3, HALO, LANES), shape(3, HALO, LANES), shape(3, BLOCKS, LANES)),
        1 << 32,
        (
            pltpu.VMEM((3, 2 * HALO + BLOCKS + 16, LANES), F32),
            pltpu.VMEM((8 * BLOCKS, LANES), F32),
            pltpu.VMEM((8 * BLOCKS, LANES), F32),
            pltpu.VMEM((3, 8 * BLOCKS, LANES), F32),
            pltpu.VMEM((3, 2 * HALO + BLOCKS + 16, LANES), F32),
        ),
    )(
        parity,
        far,
        near,
        own,
        links,
        plastic_strain[0].reshape(6, BLOCKS, LANES),
        element_size.reshape(BLOCKS, LANES),
        yield_stress.reshape(BLOCKS, LANES),
        external_force[0].reshape(3, BLOCKS, LANES),
    )

    got, far_force, near_force = lax.optimization_barrier((got, far_force, near_force))
    back, force = call(
        master_kernel, 4, (shape(PEERS * SLOTS, 3 * LANES, dtype=BF16), shape(3, SEG, LANES)), 1 << 28
    )(got, rows, coupling, quad_weight.reshape(1, LANES))
    returned = exchanged(back)
    residual, master_force = call(finish_kernel, 5, (shape(3, BLOCKS, LANES), shape(3, SEG, LANES)), 1 << 20)(
        parity, own_force, paired(far_force, 1), paired(near_force, 0), swapped(force)
    )
    slave_force = call(slave_kernel, 3, shape(3, SEG, LANES), 1 << 27)(returned, place, coupling)
    return (
        residual.reshape(1, 3, BLOCKS * LANES),
        jnp.transpose(slave_force, (1, 0, 2))[None],
        jnp.transpose(master_force, (1, 0, 2))[None],
    )


def solution(mesh):
    return jax.shard_map(
        local,
        mesh=mesh,
        in_specs=(
            P("body", None, "dom"),
            P("body", None, "dom"),
            P("body", None, "dom"),
            P("body", "dom"),
            P("body", "dom"),
            P("body", None, "dom"),
            P("body", "dom", None, None),
            P("body", "dom", None),
            P("body", "dom", None),
            P("body", "dom"),
            P("body", "dom", None),
            P("body", "dom", None, None),
            P("body", "dom", None, None),
            P(),
            P(),
        ),
        out_specs=(
            P("body", None, "dom"),
            P("body", "dom", None, None),
            P("body", "dom", None, None),
        ),
        check_vma=False,
    )
```

```python
import jax
import jax.numpy as jnp
import numpy as np
from jax import lax
from jax.experimental import pallas as pl
from jax.experimental.pallas import tpu as pltpu
from jax.sharding import PartitionSpec as P


LANES = 128
WINDOW = 48
HALO = 16
BLOCKS = 32
SLOTS = 8
PEERS = 64
SEG = 128
F32 = jnp.float32
BF16 = jnp.bfloat16
NT = (((1,), (1,)), ((), ()))
TN = (((0,), (0,)), ((), ()))
NN = (((1,), (0,)), ((), ()))


def dot(a, b, dims=NN):
    return lax.dot_general(a, b, dims, preferred_element_type=F32)


def iota(shape, dim, dtype=jnp.int32):
    return lax.broadcasted_iota(jnp.int32, shape, dim).astype(dtype)


def element_kernel(parity, far, near, own, links, strain, edge_ref, yield_ref, ext, far_out, near_out, own_out,
                   disp, lo_s, hi_s, force_s, acc):
    odd = parity[0:1, :] == 1
    disp[:, 0:HALO, :] = jnp.where(odd, near[...], far[...])
    disp[:, HALO : HALO + BLOCKS, :] = own[...]
    disp[:, HALO + BLOCKS : 2 * HALO + BLOCKS, :] = jnp.where(odd, far[...], near[...])
    acc[...] = jnp.zeros_like(acc)
    lane = iota((8, LANES), 1)
    block = iota((8, LANES), 0)
    for m in range(BLOCKS // 8):
        nodal = []
        for a in range(8):
            reach = links[pl.ds(64 * m + a, 8, stride=8), :] + lane
            hi = reach >> 7
            lo = reach & 127
            lo_s[a * BLOCKS + 8 * m : a * BLOCKS + 8 * m + 8, :] = lo.astype(F32)
            hi_s[a * BLOCKS + 8 * m : a * BLOCKS + 8 * m + 8, :] = (hi + block).astype(F32)
            got = [jnp.zeros((8, LANES), F32)] * 3
            for h in range(33):
                here = hi == h
                for i in range(3):
                    rows = disp[i, 8 * m + h : 8 * m + h + 8, :]
                    got[i] = jnp.where(here, jnp.take_along_axis(rows, lo, axis=1), got[i])
            nodal.append(got)
        edge = edge_ref[8 * m : 8 * m + 8, :]
        scale = 0.25 / edge
        grad = [[None] * 3 for _ in range(3)]
        for i in range(3):
            u = [nodal[a][i] for a in range(8)]
            for j in range(3):
                plus = [u[a] for a in range(8) if a >> j & 1]
                minus = [u[a] for a in range(8) if not a >> j & 1]
                total = sum(p - q for p, q in zip(plus, minus))
                grad[i][j] = total * scale
        old = [strain[c, 8 * m : 8 * m + 8, :] for c in range(6)]
        exx = grad[0][0] - old[0]
        eyy = grad[1][1] - old[1]
        ezz = grad[2][2] - old[2]
        exy = 0.5 * (grad[0][1] + grad[1][0]) - old[3]
        eyz = 0.5 * (grad[1][2] + grad[2][1]) - old[4]
        ezx = 0.5 * (grad[2][0] + grad[0][2]) - old[5]
        trace = exx + eyy + ezz
        sxx = trace + exx
        syy = trace + eyy
        szz = trace + ezz
        mean = (sxx + syy + szz) / 3.0
        dxx, dyy, dzz = sxx - mean, syy - mean, szz - mean
        size = jnp.sqrt(dxx * dxx + dyy * dyy + dzz * dzz + 2.0 * (exy * exy + eyz * eyz + ezx * ezx))
        radius = np.float32(np.sqrt(2.0 / 3.0)) * yield_ref[8 * m : 8 * m + 8, :]
        factor = radius / jnp.maximum(size, radius)
        area = 0.25 * edge * edge
        xy, yz, zx = area * factor * exy, area * factor * eyz, area * factor * ezx
        xx = area * (mean + factor * dxx)
        yy = area * (mean + factor * dyy)
        zz = area * (mean + factor * dzz)
        for i, (tx, ty, tz) in enumerate(((xx, xy, zx), (xy, yy, yz), (zx, yz, zz))):
            four = [tx + ty, ty - tx, tx - ty, -tx - ty]
            for a in range(8):
                pick = four[(0 if a & 1 else 1) if a & 2 else (2 if a & 1 else 3)]
                f = pick + tz if a & 4 else pick - tz
                force_s[i, a * BLOCKS + 8 * m : a * BLOCKS + 8 * m + 8, :] = f
    row = iota((16, LANES), 0, F32)
    rows = [(row + 16.0 * t).astype(BF16) for t in range(8)]
    zero = jnp.zeros((16, LANES), BF16)
    one = jnp.ones((16, LANES), BF16)

    def wide(ref, *at):
        return jnp.broadcast_to(ref[at], (16, LANES)).astype(BF16)

    for m in range(BLOCKS // 8):
        sums = jnp.zeros((3 * WINDOW, LANES), F32)
        for s in range(8):
            left, right = [], []
            for a in range(8):
                at = slice(a * BLOCKS + 8 * m + s, a * BLOCKS + 8 * m + s + 1)
                hi = wide(hi_s, at, slice(None))
                lo = wide(lo_s, at, slice(None))
                here = [hi == rows[t] for t in range(WINDOW // 16)]
                parts = []
                for i in range(3):
                    f = wide(force_s, i, at, slice(None))
                    parts += [jnp.where(h, f, zero) for h in here]
                left.append(jnp.concatenate(parts, axis=0))
                right.append(jnp.concatenate([jnp.where(lo == r, one, zero) for r in rows], axis=0))
            sums = sums + dot(jnp.concatenate(left, axis=1), jnp.concatenate(right, axis=1), NT)
        for i in range(3):
            acc[i, 8 * m : 8 * m + WINDOW, :] += sums[i * WINDOW : (i + 1) * WINDOW]
    low, high = acc[:, 0:HALO, :], acc[:, HALO + BLOCKS : 2 * HALO + BLOCKS, :]
    far_out[...] = jnp.where(odd, high, low)
    near_out[...] = jnp.where(odd, low, high)
    own_out[...] = acc[:, HALO : HALO + BLOCKS, :] - ext[...]


def finish_kernel(parity, own, far, near, force, out, force_out):
    odd = parity[0:1, :] == 1
    force_out[...] = force[...]
    out[:, 0:HALO, :] = own[:, 0:HALO, :] + jnp.where(odd, near[...], far[...])
    out[:, HALO:BLOCKS, :] = own[:, HALO:BLOCKS, :] + jnp.where(odd, far[...], near[...])


def pack_kernel(owner, where, active, disp, send, place):
    names = iota((PEERS, SEG), 0)
    earlier = jnp.where(iota((SEG, SEG), 0) < iota((SEG, SEG), 1), 1.0, 0.0).astype(BF16)
    ones = jnp.ones((SEG, SEG), BF16)
    hot = [owner[k : k + 1, :] == names for k in range(2)]
    hot16 = [jnp.where(h, 1.0, 0.0).astype(BF16) for h in hot]
    before = [dot(hot16[0], earlier), dot(hot16[1], earlier) + dot(hot16[0], ones)]
    slots = iota((PEERS * SLOTS, SEG), 0)
    sent = jnp.zeros((PEERS * SLOTS, SEG), F32)
    meta = jnp.zeros((PEERS * SLOTS, SEG), F32)
    for k in range(2):
        rank = jnp.sum(jnp.where(hot[k], before[k], 0.0), axis=0, keepdims=True)
        slot = owner[k : k + 1, :] * SLOTS + rank.astype(jnp.int32)
        mark = ((where[k : k + 1, :] + 1) * active[...]).astype(F32)
        here = slot == slots
        sent = jnp.where(here, 1.0, sent)
        meta = jnp.where(here, mark, meta)
    sent = sent.astype(BF16)
    place[...] = sent
    for c in range(3):
        send[:, c * LANES : (c + 1) * LANES] = dot(sent, disp[c]).astype(BF16)
    send[:, 3 * LANES :] = dot(meta.astype(BF16), ones).astype(BF16)


def rows_kernel(gap, normal, mdisp, coupling, quad_weight, rows, mortar, weight):
    mortar[...] = mortar_of(coupling)
    weight[...] = jnp.broadcast_to(quad_weight[...], weight.shape)
    total = gap[...]
    for c in range(3):
        n = normal[c]
        total = total + n * mdisp[c].astype(F32)
        rows[1 + c] = n
    rows[0] = total


def mortar_of(coupling):
    eye = jnp.where(iota((LANES, LANES), 0) == iota((LANES, LANES), 1), 1.0, 0.0)
    return (eye + coupling[...].astype(F32)).astype(BF16)


def split(x):
    top = x.astype(BF16)
    return top, (x - top.astype(F32)).astype(BF16)


def master_kernel(got, rows, mortar_ref, weight, back, force):
    mortar = mortar_ref[...]
    table = [split(rows[c]) for c in range(4)]
    name = iota((SEG, LANES), 1, F32) + 1.0
    totals = [jnp.zeros((SEG, LANES), F32)] * 3
    for part in range(PEERS * SLOTS // SEG):
        span = slice(part * SEG, (part + 1) * SEG)
        hot = jnp.where(got[span, 3 * LANES :].astype(F32) == name, 1.0, 0.0).astype(BF16)
        gap, n0, n1, n2 = (dot(hot, t) + dot(hot, b) for t, b in table)
        normal = (n0, n1, n2)
        for c in range(3):
            gap = gap - normal[c] * dot(got[span, c * LANES : (c + 1) * LANES], mortar)
        press = weight[0:1, :] * (2.0 * jnp.maximum(gap, 0.0))
        for c in range(3):
            top, low = split(press * normal[c])
            back[span, c * LANES : (c + 1) * LANES] = top
            totals[c] = totals[c] + dot(hot, top, TN) + dot(hot, low, TN)
    for c in range(3):
        force[c] = -totals[c]


def slave_kernel(got, place, mortar_ref, out):
    mortar = mortar_ref[...]
    for c in range(3):
        pair = dot(place[...], got[:, c * LANES : (c + 1) * LANES], TN).astype(BF16)
        out[c] = dot(pair, mortar, NT)


def shape(*dims, dtype=F32):
    return jax.ShapeDtypeStruct(dims, dtype)


VMEM = pl.BlockSpec(memory_space=pltpu.VMEM)


def call(kernel, ins, outs, cost, scratch=(), grant=8 << 20):
    return pl.pallas_call(
        kernel,
        out_shape=outs,
        in_specs=[VMEM] * ins if ins > 0 else [pl.BlockSpec()] * -ins,
        out_specs=jax.tree.map(lambda _: VMEM if ins > 0 else pl.BlockSpec(), outs),
        scratch_shapes=scratch,
        compiler_params=pltpu.CompilerParams(vmem_limit_bytes=grant),
        cost_estimate=pl.CostEstimate(flops=cost, bytes_accessed=1 << 20, transcendentals=0),
    )


def paired(block, first):
    route = [(i, i + 1) for i in range(first, PEERS - 1, 2)]
    return lax.ppermute(block, "dom", route + [(j, i) for i, j in route])


def swapped(block):
    return lax.ppermute(block, "body", [(0, 1), (1, 0)])


def exchanged(block):
    return lax.all_to_all(block, "dom", split_axis=0, concat_axis=0, tiled=True)


def local(
    displacement,
    connectivity,
    plastic_strain,
    element_size,
    yield_stress,
    external_force,
    slave_disp,
    pair_owner,
    pair_local,
    active,
    master_gap,
    master_normal,
    master_disp,
    coupling,
    quad_weight,
):
    seg_major = lambda x: jnp.transpose(x[0], (1, 0, 2))
    send, place = call(
        pack_kernel,
        -4,
        (shape(PEERS * SLOTS, 4 * LANES, dtype=BF16), shape(PEERS * SLOTS, SEG, dtype=BF16)),
        1 << 27,
        grant=60 << 20,
    )(pair_owner[0].T, pair_local[0].T, active, seg_major(slave_disp))
    got = exchanged(send)

    own = displacement[0].reshape(3, BLOCKS, LANES)
    odd = lax.axis_index("dom") & 1
    parity = jnp.full((8, LANES), odd, jnp.int32)
    first, last = own[:, :HALO], own[:, BLOCKS - HALO :]
    far = paired(jnp.where(odd == 1, last, first), 1)
    near = paired(jnp.where(odd == 1, first, last), 0)
    rows, mortar, weight = call(
        rows_kernel, 5, (shape(4, SEG, LANES), shape(LANES, LANES, dtype=BF16), shape(8, LANES)), 1 << 20
    )(master_gap[0], seg_major(master_normal), seg_major(master_disp), coupling, quad_weight.reshape(1, LANES))
    rows = swapped(rows)
    links = jnp.transpose(connectivity[0].reshape(8, BLOCKS, LANES), (1, 0, 2)).reshape(8 * BLOCKS, LANES)
    far_force, near_force, own_force = call(
        element_kernel,
        9,
        (shape(3, HALO, LANES), shape(3, HALO, LANES), shape(3, BLOCKS, LANES)),
        1 << 32,
        (
            pltpu.VMEM((3, 2 * HALO + BLOCKS + 16, LANES), F32),
            pltpu.VMEM((8 * BLOCKS, LANES), F32),
            pltpu.VMEM((8 * BLOCKS, LANES), F32),
            pltpu.VMEM((3, 8 * BLOCKS, LANES), F32),
            pltpu.VMEM((3, 2 * HALO + BLOCKS + 16, LANES), F32),
        ),
    )(
        parity,
        far,
        near,
        own,
        links,
        plastic_strain[0].reshape(6, BLOCKS, LANES),
        element_size.reshape(BLOCKS, LANES),
        yield_stress.reshape(BLOCKS, LANES),
        external_force[0].reshape(3, BLOCKS, LANES),
    )

    got, far_force, near_force = lax.optimization_barrier((got, far_force, near_force))
    back, force = call(
        master_kernel, 4, (shape(PEERS * SLOTS, 3 * LANES, dtype=BF16), shape(3, SEG, LANES)), 1 << 28
    )(got, rows, mortar, weight)
    returned = exchanged(back)
    slave_force = call(slave_kernel, 3, shape(3, SEG, LANES), 1 << 27)(returned, place, mortar)
    parity_late, slave_force = lax.optimization_barrier((parity, slave_force))
    residual, master_force = call(finish_kernel, 5, (shape(3, BLOCKS, LANES), shape(3, SEG, LANES)), 1 << 20)(
        parity_late, own_force, paired(far_force, 1), paired(near_force, 0), swapped(force)
    )
    return (
        residual.reshape(1, 3, BLOCKS * LANES),
        jnp.transpose(slave_force, (1, 0, 2))[None],
        jnp.transpose(master_force, (1, 0, 2))[None],
    )


def solution(mesh):
    return jax.shard_map(
        local,
        mesh=mesh,
        in_specs=(
            P("body", None, "dom"),
            P("body", None, "dom"),
            P("body", None, "dom"),
            P("body", "dom"),
            P("body", "dom"),
            P("body", None, "dom"),
            P("body", "dom", None, None),
            P("body", "dom", None),
            P("body", "dom", None),
            P("body", "dom"),
            P("body", "dom", None),
            P("body", "dom", None, None),
            P("body", "dom", None, None),
            P(),
            P(),
        ),
        out_specs=(
            P("body", None, "dom"),
            P("body", "dom", None, None),
            P("body", "dom", None, None),
        ),
        check_vma=False,
    )
```

```python
import jax
import jax.numpy as jnp
import numpy as np
from jax import lax
from jax.experimental import pallas as pl
from jax.experimental.pallas import tpu as pltpu
from jax.sharding import PartitionSpec as P


LANES = 128
HALO = 16
BLOCKS = 32
SLOTS = 8
PEERS = 64
SEG = 128
F32 = jnp.float32
BF16 = jnp.bfloat16
NT = (((1,), (1,)), ((), ()))
TN = (((0,), (0,)), ((), ()))
NN = (((1,), (0,)), ((), ()))


def dot(a, b, dims=NN):
    return lax.dot_general(a, b, dims, preferred_element_type=F32)


def iota(shape, dim, dtype=jnp.int32):
    return lax.broadcasted_iota(jnp.int32, shape, dim).astype(dtype)


def own_rows(m):
    return range(max(0, HALO - 8 * m), min(33, HALO + BLOCKS - 7 - 8 * m))


def reach_of(links, m, a):
    return links[pl.ds(64 * m + a, 8, stride=8), :] + iota((8, LANES), 1)


def gather_rows(disp, links, m, a, hs, base, got):
    reach = reach_of(links, m, a)
    hi, lo = reach >> 7, reach & 127
    chains = [list(got), [jnp.zeros((8, LANES), F32)] * 3]
    for n, h in enumerate(hs):
        here = hi == h
        chain = chains[n & 1]
        for i in range(3):
            rows = disp[i, 8 * m + h - base : 8 * m + h - base + 8, :]
            chain[i] = jnp.where(here, jnp.take_along_axis(rows, lo, axis=1), chain[i])
    return [x + y for x, y in zip(*chains)]


GROUP = 4


def gather_kernel(own, links, nodal):
    for m in range(BLOCKS // 8):

        @pl.loop(0, 8 // GROUP)
        def _(step):
            for c in range(GROUP):
                a = step * GROUP + c
                got = gather_rows(own, links, m, a, own_rows(m), HALO, [jnp.zeros((8, LANES), F32)] * 3)
                at = pl.multiple_of(a * BLOCKS + 8 * m, 8)
                for i in range(3):
                    nodal[i, pl.ds(at, 8), :] = got[i]


def element_kernel(parity, far, near, own, links, part, strain, edge_ref, yield_ref, ext, far_out, near_out, own_out,
                   disp, lo_s, hi_s, nodal_s, acc):
    odd = parity[0:1, :] == 1
    disp[:, 0:HALO, :] = jnp.where(odd, near[...], far[...])
    disp[:, HALO : HALO + BLOCKS, :] = own[...]
    disp[:, HALO + BLOCKS : 2 * HALO + BLOCKS, :] = jnp.where(odd, far[...], near[...])
    acc[...] = jnp.zeros_like(acc)
    block = iota((8, LANES), 0) * LANES
    for m in range(BLOCKS // 8):

        @pl.loop(0, 8 // GROUP)
        def _(step):
            for c in range(GROUP):
                a = step * GROUP + c
                at = pl.ds(pl.multiple_of(a * BLOCKS + 8 * m, 8), 8)
                rest = [h for h in range(33) if h not in own_rows(m)]
                got = gather_rows(disp, links, m, a, rest, 0, [part[i, at, :] for i in range(3)])
                for i in range(3):
                    nodal_s[i, at, :] = got[i]
                reach = reach_of(links, m, a) + block
                hi_s[at, :] = (reach >> 6).astype(F32)
                lo_s[at, :] = (reach & 63).astype(F32)

    @pl.loop(0, BLOCKS // 8)
    def _(m):
        at = lambda a: pl.ds(pl.multiple_of(a * BLOCKS + 8 * m, 8), 8)
        rows = at(0)
        edge = edge_ref[rows, :]
        scale = 0.25 / edge
        grad = [[None] * 3 for _ in range(3)]
        for i in range(3):
            u = [nodal_s[i, at(a), :] for a in range(8)]
            for j in range(3):
                plus = [u[a] for a in range(8) if a >> j & 1]
                minus = [u[a] for a in range(8) if not a >> j & 1]
                grad[i][j] = sum(p - q for p, q in zip(plus, minus)) * scale
        old = [strain[c, rows, :] for c in range(6)]
        exx = grad[0][0] - old[0]
        eyy = grad[1][1] - old[1]
        ezz = grad[2][2] - old[2]
        exy = 0.5 * (grad[0][1] + grad[1][0]) - old[3]
        eyz = 0.5 * (grad[1][2] + grad[2][1]) - old[4]
        ezx = 0.5 * (grad[2][0] + grad[0][2]) - old[5]
        trace = exx + eyy + ezz
        sxx = trace + exx
        syy = trace + eyy
        szz = trace + ezz
        mean = (sxx + syy + szz) / 3.0
        dxx, dyy, dzz = sxx - mean, syy - mean, szz - mean
        size = jnp.sqrt(dxx * dxx + dyy * dyy + dzz * dzz + 2.0 * (exy * exy + eyz * eyz + ezx * ezx))
        radius = np.float32(np.sqrt(2.0 / 3.0)) * yield_ref[rows, :]
        factor = radius / jnp.maximum(size, radius)
        area = 0.25 * edge * edge
        xy, yz, zx = area * factor * exy, area * factor * eyz, area * factor * ezx
        xx = area * (mean + factor * dxx)
        yy = area * (mean + factor * dyy)
        zz = area * (mean + factor * dzz)
        for i, (tx, ty, tz) in enumerate(((xx, xy, zx), (xy, yy, yz), (zx, yz, zz))):
            four = [tx + ty, ty - tx, tx - ty, -tx - ty]
            for a in range(8):
                pick = four[(0 if a & 1 else 1) if a & 2 else (2 if a & 1 else 3)]
                nodal_s[i, at(a), :] = pick + tz if a & 4 else pick - tz

    row = iota((16, LANES), 0, F32)
    tiles = [(row + 16.0 * t).astype(BF16) for t in range(5)]
    zero = jnp.zeros((16, LANES), BF16)
    one = jnp.ones((16, LANES), BF16)

    def wide(ref, *at):
        return jnp.broadcast_to(ref[at], (16, LANES)).astype(BF16)

    for m in range(BLOCKS // 8):
        sums = jnp.zeros((80, 3 * 64), F32)
        for s in range(8):
            left, right = [], []
            for a in range(8):
                at = slice(a * BLOCKS + 8 * m + s, a * BLOCKS + 8 * m + s + 1)
                hi = wide(hi_s, at, slice(None))
                lo = wide(lo_s, at, slice(None))
                left.append(jnp.concatenate([jnp.where(hi == t, one, zero) for t in tiles], axis=0))
                here = [lo == t for t in tiles[:4]]
                force = [wide(nodal_s, i, at, slice(None)) for i in range(3)]
                right.append(jnp.concatenate([jnp.where(h, f, zero) for f in force for h in here], axis=0))
            sums = sums + dot(jnp.concatenate(left, axis=1), jnp.concatenate(right, axis=1), NT)
        acc[0, 16 * m : 16 * m + 80, :] += sums[:, :LANES]
        acc[1, 16 * m : 16 * m + 80, :64] += sums[:, LANES:]
    for i in range(3):
        pair = [acc[i // 2, pl.ds(p, 2 * HALO + BLOCKS, stride=2), :] for p in range(2)]
        nodes = jnp.concatenate([x[:, 64 * (i % 2) : 64 * (i % 2) + 64] for x in pair], axis=1)
        low, high = nodes[0:HALO], nodes[HALO + BLOCKS :]
        far_out[i] = jnp.where(odd, high, low)
        near_out[i] = jnp.where(odd, low, high)
        own_out[i] = nodes[HALO : HALO + BLOCKS] - ext[i]


def finish_kernel(parity, own, far, near, force, out, force_out):
    odd = parity[0:1, :] == 1
    force_out[...] = force[...]
    out[:, 0:HALO, :] = own[:, 0:HALO, :] + jnp.where(odd, near[...], far[...])
    out[:, HALO:BLOCKS, :] = own[:, HALO:BLOCKS, :] + jnp.where(odd, far[...], near[...])


def pack_kernel(owner, where, active, disp, send, place):
    names = iota((PEERS, SEG), 0)
    earlier = jnp.where(iota((SEG, SEG), 0) < iota((SEG, SEG), 1), 1.0, 0.0).astype(BF16)
    ones = jnp.ones((SEG, SEG), BF16)
    hot = [owner[k : k + 1, :] == names for k in range(2)]
    hot16 = [jnp.where(h, 1.0, 0.0).astype(BF16) for h in hot]
    before = [dot(hot16[0], earlier), dot(hot16[1], earlier) + dot(hot16[0], ones)]
    slots = iota((PEERS * SLOTS, SEG), 0)
    sent = jnp.zeros((PEERS * SLOTS, SEG), F32)
    meta = jnp.zeros((PEERS * SLOTS, SEG), F32)
    for k in range(2):
        rank = jnp.sum(jnp.where(hot[k], before[k], 0.0), axis=0, keepdims=True)
        slot = owner[k : k + 1, :] * SLOTS + rank.astype(jnp.int32)
        mark = ((where[k : k + 1, :] + 1) * active[...]).astype(F32)
        here = slot == slots
        sent = jnp.where(here, 1.0, sent)
        meta = jnp.where(here, mark, meta)
    sent = sent.astype(BF16)
    place[...] = sent
    for c in range(3):
        send[:, c * LANES : (c + 1) * LANES] = dot(sent, disp[c]).astype(BF16)
    send[:, 3 * LANES :] = dot(meta.astype(BF16), ones).astype(BF16)


def rows_kernel(gap, normal, mdisp, coupling, quad_weight, rows, mortar, weight):
    mortar[...] = mortar_of(coupling)
    weight[...] = jnp.broadcast_to(quad_weight[...], weight.shape)
    total = gap[...]
    for c in range(3):
        n = normal[c]
        total = total + n * mdisp[c].astype(F32)
        rows[1 + c] = n
    rows[0] = total


def mortar_of(coupling):
    eye = jnp.where(iota((LANES, LANES), 0) == iota((LANES, LANES), 1), 1.0, 0.0)
    return (eye + coupling[...].astype(F32)).astype(BF16)


def split(x):
    top = x.astype(BF16)
    return top, (x - top.astype(F32)).astype(BF16)


def master_kernel(got, rows, mortar_ref, weight, back, force):
    mortar = mortar_ref[...]
    table = [split(rows[c]) for c in range(4)]
    name = iota((SEG, LANES), 1, F32) + 1.0
    totals = [jnp.zeros((SEG, LANES), F32)] * 3
    for part in range(PEERS * SLOTS // SEG):
        span = slice(part * SEG, (part + 1) * SEG)
        hot = jnp.where(got[span, 3 * LANES :].astype(F32) == name, 1.0, 0.0).astype(BF16)
        gap, n0, n1, n2 = (dot(hot, t) + dot(hot, b) for t, b in table)
        normal = (n0, n1, n2)
        for c in range(3):
            gap = gap - normal[c] * dot(got[span, c * LANES : (c + 1) * LANES], mortar)
        press = weight[0:1, :] * (2.0 * jnp.maximum(gap, 0.0))
        for c in range(3):
            top, low = split(press * normal[c])
            back[span, c * LANES : (c + 1) * LANES] = top
            totals[c] = totals[c] + dot(hot, top, TN) + dot(hot, low, TN)
    for c in range(3):
        force[c] = -totals[c]


def slave_kernel(got, place, mortar_ref, out):
    mortar = mortar_ref[...]
    for c in range(3):
        pair = dot(place[...], got[:, c * LANES : (c + 1) * LANES], TN).astype(BF16)
        out[c] = dot(pair, mortar, NT)


def shape(*dims, dtype=F32):
    return jax.ShapeDtypeStruct(dims, dtype)


VMEM = pl.BlockSpec(memory_space=pltpu.VMEM)


def call(kernel, ins, outs, cost, scratch=(), grant=8 << 20):
    return pl.pallas_call(
        kernel,
        out_shape=outs,
        in_specs=[VMEM] * ins if ins > 0 else [pl.BlockSpec()] * -ins,
        out_specs=jax.tree.map(lambda _: VMEM if ins > 0 else pl.BlockSpec(), outs),
        scratch_shapes=scratch,
        compiler_params=pltpu.CompilerParams(vmem_limit_bytes=grant),
        cost_estimate=pl.CostEstimate(flops=cost, bytes_accessed=1 << 20, transcendentals=0),
    )


def paired(block, first):
    route = [(i, i + 1) for i in range(first, PEERS - 1, 2)]
    return lax.ppermute(block, "dom", route + [(j, i) for i, j in route])


def swapped(block):
    return lax.ppermute(block, "body", [(0, 1), (1, 0)])


def exchanged(block):
    return lax.all_to_all(block, "dom", split_axis=0, concat_axis=0, tiled=True)


def local(
    displacement,
    connectivity,
    plastic_strain,
    element_size,
    yield_stress,
    external_force,
    slave_disp,
    pair_owner,
    pair_local,
    active,
    master_gap,
    master_normal,
    master_disp,
    coupling,
    quad_weight,
):
    seg_major = lambda x: jnp.transpose(x[0], (1, 0, 2))
    send, place = call(
        pack_kernel,
        -4,
        (shape(PEERS * SLOTS, 4 * LANES, dtype=BF16), shape(PEERS * SLOTS, SEG, dtype=BF16)),
        1 << 27,
        grant=60 << 20,
    )(pair_owner[0].T, pair_local[0].T, active, seg_major(slave_disp))
    got = exchanged(send)

    own = displacement[0].reshape(3, BLOCKS, LANES)
    odd = lax.axis_index("dom") & 1
    parity = jnp.full((8, LANES), odd, jnp.int32)
    first, last = own[:, :HALO], own[:, BLOCKS - HALO :]
    far = paired(jnp.where(odd == 1, last, first), 1)
    near = paired(jnp.where(odd == 1, first, last), 0)
    rows, mortar, weight = call(
        rows_kernel, 5, (shape(4, SEG, LANES), shape(LANES, LANES, dtype=BF16), shape(8, LANES)), 1 << 20
    )(master_gap[0], seg_major(master_normal), seg_major(master_disp), coupling, quad_weight.reshape(1, LANES))
    rows = swapped(rows)
    links = jnp.transpose(connectivity[0].reshape(8, BLOCKS, LANES), (1, 0, 2)).reshape(8 * BLOCKS, LANES)
    part = call(gather_kernel, 2, shape(3, 8 * BLOCKS, LANES), 1 << 30)(own, links)
    far_force, near_force, own_force = call(
        element_kernel,
        10,
        (shape(3, HALO, LANES), shape(3, HALO, LANES), shape(3, BLOCKS, LANES)),
        1 << 32,
        (
            pltpu.VMEM((3, 2 * HALO + BLOCKS + 8, LANES), F32),
            pltpu.VMEM((8 * BLOCKS, LANES), F32),
            pltpu.VMEM((8 * BLOCKS, LANES), F32),
            pltpu.VMEM((3, 8 * BLOCKS, LANES), F32),
            pltpu.VMEM((2, 4 * HALO + 2 * BLOCKS + 16, LANES), F32),
        ),
    )(
        parity,
        far,
        near,
        own,
        links,
        part,
        plastic_strain[0].reshape(6, BLOCKS, LANES),
        element_size.reshape(BLOCKS, LANES),
        yield_stress.reshape(BLOCKS, LANES),
        external_force[0].reshape(3, BLOCKS, LANES),
    )

    got, far_force, near_force = lax.optimization_barrier((got, far_force, near_force))
    back, force = call(
        master_kernel, 4, (shape(PEERS * SLOTS, 3 * LANES, dtype=BF16), shape(3, SEG, LANES)), 1 << 28
    )(got, rows, mortar, weight)
    returned = exchanged(back)
    slave_force = call(slave_kernel, 3, shape(3, SEG, LANES), 1 << 27)(returned, place, mortar)
    parity_late, slave_force = lax.optimization_barrier((parity, slave_force))
    residual, master_force = call(finish_kernel, 5, (shape(3, BLOCKS, LANES), shape(3, SEG, LANES)), 1 << 20)(
        parity_late, own_force, paired(far_force, 1), paired(near_force, 0), swapped(force)
    )
    return (
        residual.reshape(1, 3, BLOCKS * LANES),
        jnp.transpose(slave_force, (1, 0, 2))[None],
        jnp.transpose(master_force, (1, 0, 2))[None],
    )


def solution(mesh):
    return jax.shard_map(
        local,
        mesh=mesh,
        in_specs=(
            P("body", None, "dom"),
            P("body", None, "dom"),
            P("body", None, "dom"),
            P("body", "dom"),
            P("body", "dom"),
            P("body", None, "dom"),
            P("body", "dom", None, None),
            P("body", "dom", None),
            P("body", "dom", None),
            P("body", "dom"),
            P("body", "dom", None),
            P("body", "dom", None, None),
            P("body", "dom", None, None),
            P(),
            P(),
        ),
        out_specs=(
            P("body", None, "dom"),
            P("body", "dom", None, None),
            P("body", "dom", None, None),
        ),
        check_vma=False,
    )
```

```python
import jax
import jax.numpy as jnp
import numpy as np
from jax import lax
from jax.experimental import pallas as pl
from jax.experimental.pallas import tpu as pltpu
from jax.sharding import PartitionSpec as P


LANES = 128
HALO = 16
BLOCKS = 32
WINDOW = 48
SLOTS = 8
PEERS = 64
SEG = 128
F32 = jnp.float32
BF16 = jnp.bfloat16
NT = (((1,), (1,)), ((), ()))
TN = (((0,), (0,)), ((), ()))
NN = (((1,), (0,)), ((), ()))


def dot(a, b, dims=NN):
    return lax.dot_general(a, b, dims, preferred_element_type=F32)


def iota(shape, dim, dtype=jnp.int32):
    return lax.broadcasted_iota(jnp.int32, shape, dim).astype(dtype)


def own_rows(m):
    return range(max(0, HALO - 8 * m), min(33, HALO + BLOCKS - 7 - 8 * m))


def reach_of(links, m, a):
    return links[pl.ds(64 * m + a, 8, stride=8), :] + iota((8, LANES), 1)


def pack_pair(x, y, table):
    most = jnp.max(jnp.maximum(jnp.abs(x), jnp.abs(y)), axis=0, keepdims=True)
    most = jnp.maximum(jnp.max(most, axis=1, keepdims=True), 1e-30)
    scale = 32767.0 / most

    def whole(v):
        v = v * scale
        return (v + jnp.where(v < 0.0, -0.5, 0.5)).astype(jnp.int32)

    table[0 : x.shape[0], :] = (whole(x) << 16) | (whole(y) & 65535)
    return most / 32767.0


def gather_rows(table, third, unit, links, m, a, hs, base):
    reach = reach_of(links, m, a)
    hi, lo = reach >> 7, reach & 127
    pair, single = jnp.zeros((8, LANES), jnp.int32), jnp.zeros((8, LANES), F32)
    for h in hs:
        here = hi == h
        rows = slice(8 * m + h - base, 8 * m + h - base + 8)
        pair = jnp.where(here, jnp.take_along_axis(table[rows, :], lo, axis=1), pair)
        single = jnp.where(here, jnp.take_along_axis(third[2, rows, :], lo, axis=1), single)
    return [(pair >> 16).astype(F32) * unit, ((pair << 16) >> 16).astype(F32) * unit, single]


def gather_kernel(own, links, nodal, table):
    unit = pack_pair(own[0], own[1], table)
    for m in range(BLOCKS // 8):
        for a in range(8):
            got = gather_rows(table, own, unit, links, m, a, own_rows(m), HALO)
            at = a * BLOCKS + 8 * m
            for i in range(3):
                nodal[i, at : at + 8, :] = got[i]


def element_kernel(parity, far, near, own, links, part, strain, edge_ref, yield_ref, ext, far_out, near_out, own_out,
                   disp, table, lo_s, hi_s, force_s, acc):
    odd = parity[0:1, :] == 1
    disp[:, 0:HALO, :] = jnp.where(odd, near[...], far[...])
    disp[:, HALO : HALO + BLOCKS, :] = own[...]
    disp[:, HALO + BLOCKS : 2 * HALO + BLOCKS, :] = jnp.where(odd, far[...], near[...])
    acc[...] = jnp.zeros_like(acc)
    unit = pack_pair(disp[0, : 2 * HALO + BLOCKS], disp[1, : 2 * HALO + BLOCKS], table)
    block = iota((8, LANES), 0) * LANES
    for m in range(BLOCKS // 8):
        rest = [h for h in range(33) if h not in own_rows(m)]
        nodal = []
        for a in range(8):
            at = slice(a * BLOCKS + 8 * m, a * BLOCKS + 8 * m + 8)
            got = gather_rows(table, disp, unit, links, m, a, rest, 0)
            nodal.append([got[i] + part[i, at, :] for i in range(3)])
            reach = reach_of(links, m, a) + block
            hi_s[at, :] = (reach >> 7).astype(F32)
            lo_s[at, :] = (reach & 127).astype(F32)
        edge = edge_ref[8 * m : 8 * m + 8, :]
        scale = 0.25 / edge
        grad = [[None] * 3 for _ in range(3)]
        for i in range(3):
            u = [nodal[a][i] for a in range(8)]
            for j in range(3):
                plus = [u[a] for a in range(8) if a >> j & 1]
                minus = [u[a] for a in range(8) if not a >> j & 1]
                total = sum(p - q for p, q in zip(plus, minus))
                grad[i][j] = total * scale
        old = [strain[c, 8 * m : 8 * m + 8, :] for c in range(6)]
        exx = grad[0][0] - old[0]
        eyy = grad[1][1] - old[1]
        ezz = grad[2][2] - old[2]
        exy = 0.5 * (grad[0][1] + grad[1][0]) - old[3]
        eyz = 0.5 * (grad[1][2] + grad[2][1]) - old[4]
        ezx = 0.5 * (grad[2][0] + grad[0][2]) - old[5]
        trace = exx + eyy + ezz
        sxx = trace + exx
        syy = trace + eyy
        szz = trace + ezz
        mean = (sxx + syy + szz) / 3.0
        dxx, dyy, dzz = sxx - mean, syy - mean, szz - mean
        size = jnp.sqrt(dxx * dxx + dyy * dyy + dzz * dzz + 2.0 * (exy * exy + eyz * eyz + ezx * ezx))
        radius = np.float32(np.sqrt(2.0 / 3.0)) * yield_ref[8 * m : 8 * m + 8, :]
        factor = radius / jnp.maximum(size, radius)
        area = 0.25 * edge * edge
        xy, yz, zx = area * factor * exy, area * factor * eyz, area * factor * ezx
        xx = area * (mean + factor * dxx)
        yy = area * (mean + factor * dyy)
        zz = area * (mean + factor * dzz)
        for i, (tx, ty, tz) in enumerate(((xx, xy, zx), (xy, yy, yz), (zx, yz, zz))):
            four = [tx + ty, ty - tx, tx - ty, -tx - ty]
            for a in range(8):
                pick = four[(0 if a & 1 else 1) if a & 2 else (2 if a & 1 else 3)]
                f = pick + tz if a & 4 else pick - tz
                force_s[i, a * BLOCKS + 8 * m : a * BLOCKS + 8 * m + 8, :] = f
    row = iota((16, LANES), 0, F32)
    rows = [(row + 16.0 * t).astype(BF16) for t in range(8)]
    zero = jnp.zeros((16, LANES), BF16)
    one = jnp.ones((16, LANES), BF16)

    def wide(ref, *at):
        return jnp.broadcast_to(ref[at], (16, LANES)).astype(BF16)

    for m in range(BLOCKS // 8):
        sums = jnp.zeros((3 * WINDOW, LANES), F32)
        for s in range(8):
            left, right = [], []
            for a in range(8):
                at = slice(a * BLOCKS + 8 * m + s, a * BLOCKS + 8 * m + s + 1)
                hi = wide(hi_s, at, slice(None))
                lo = wide(lo_s, at, slice(None))
                here = [hi == rows[t] for t in range(WINDOW // 16)]
                parts = []
                for i in range(3):
                    f = wide(force_s, i, at, slice(None))
                    parts += [jnp.where(h, f, zero) for h in here]
                left.append(jnp.concatenate(parts, axis=0))
                right.append(jnp.concatenate([jnp.where(lo == r, one, zero) for r in rows], axis=0))
            sums = sums + dot(jnp.concatenate(left, axis=1), jnp.concatenate(right, axis=1), NT)
        for i in range(3):
            acc[i, 8 * m : 8 * m + WINDOW, :] += sums[i * WINDOW : (i + 1) * WINDOW]
    low, high = acc[:, 0:HALO, :], acc[:, HALO + BLOCKS : 2 * HALO + BLOCKS, :]
    far_out[...] = jnp.where(odd, high, low)
    near_out[...] = jnp.where(odd, low, high)
    own_out[...] = acc[:, HALO : HALO + BLOCKS, :] - ext[...]


def finish_kernel(parity, own, far, near, force, out, force_out):
    odd = parity[0:1, :] == 1
    force_out[...] = force[...]
    out[:, 0:HALO, :] = own[:, 0:HALO, :] + jnp.where(odd, near[...], far[...])
    out[:, HALO:BLOCKS, :] = own[:, HALO:BLOCKS, :] + jnp.where(odd, far[...], near[...])


def pack_kernel(owner, where, active, disp, send, place):
    names = iota((PEERS, SEG), 0)
    earlier = jnp.where(iota((SEG, SEG), 0) < iota((SEG, SEG), 1), 1.0, 0.0).astype(BF16)
    ones = jnp.ones((SEG, SEG), BF16)
    hot = [owner[k : k + 1, :] == names for k in range(2)]
    hot16 = [jnp.where(h, 1.0, 0.0).astype(BF16) for h in hot]
    before = [dot(hot16[0], earlier), dot(hot16[1], earlier) + dot(hot16[0], ones)]
    slots = iota((PEERS * SLOTS, SEG), 0)
    sent = jnp.zeros((PEERS * SLOTS, SEG), F32)
    meta = jnp.zeros((PEERS * SLOTS, SEG), F32)
    for k in range(2):
        rank = jnp.sum(jnp.where(hot[k], before[k], 0.0), axis=0, keepdims=True)
        slot = owner[k : k + 1, :] * SLOTS + rank.astype(jnp.int32)
        mark = ((where[k : k + 1, :] + 1) * active[...]).astype(F32)
        here = slot == slots
        sent = jnp.where(here, 1.0, sent)
        meta = jnp.where(here, mark, meta)
    sent = sent.astype(BF16)
    place[...] = sent
    for c in range(3):
        send[:, c * LANES : (c + 1) * LANES] = dot(sent, disp[c]).astype(BF16)
    send[:, 3 * LANES :] = dot(meta.astype(BF16), ones).astype(BF16)


def rows_kernel(gap, normal, mdisp, coupling, quad_weight, rows, mortar, weight):
    mortar[...] = mortar_of(coupling)
    weight[...] = jnp.broadcast_to(quad_weight[...], weight.shape)
    total = gap[...]
    for c in range(3):
        n = normal[c]
        total = total + n * mdisp[c].astype(F32)
        rows[1 + c] = n
    rows[0] = total


def mortar_of(coupling):
    eye = jnp.where(iota((LANES, LANES), 0) == iota((LANES, LANES), 1), 1.0, 0.0)
    return (eye + coupling[...].astype(F32)).astype(BF16)


def split(x):
    top = x.astype(BF16)
    return top, (x - top.astype(F32)).astype(BF16)


def master_kernel(got, rows, mortar_ref, weight, back, force):
    mortar = mortar_ref[...]
    table = [split(rows[c]) for c in range(4)]
    name = iota((SEG, LANES), 1, F32) + 1.0
    totals = [jnp.zeros((SEG, LANES), F32)] * 3
    for part in range(PEERS * SLOTS // SEG):
        span = slice(part * SEG, (part + 1) * SEG)
        hot = jnp.where(got[span, 3 * LANES :].astype(F32) == name, 1.0, 0.0).astype(BF16)
        gap, n0, n1, n2 = (dot(hot, t) + dot(hot, b) for t, b in table)
        normal = (n0, n1, n2)
        for c in range(3):
            gap = gap - normal[c] * dot(got[span, c * LANES : (c + 1) * LANES], mortar)
        press = weight[0:1, :] * (2.0 * jnp.maximum(gap, 0.0))
        for c in range(3):
            top, low = split(press * normal[c])
            back[span, c * LANES : (c + 1) * LANES] = top
            totals[c] = totals[c] + dot(hot, top, TN) + dot(hot, low, TN)
    for c in range(3):
        force[c] = -totals[c]


def slave_kernel(got, place, mortar_ref, out):
    mortar = mortar_ref[...]
    for c in range(3):
        pair = dot(place[...], got[:, c * LANES : (c + 1) * LANES], TN).astype(BF16)
        out[c] = dot(pair, mortar, NT)


def shape(*dims, dtype=F32):
    return jax.ShapeDtypeStruct(dims, dtype)


VMEM = pl.BlockSpec(memory_space=pltpu.VMEM)


def call(kernel, ins, outs, cost, scratch=(), grant=8 << 20):
    return pl.pallas_call(
        kernel,
        out_shape=outs,
        in_specs=[VMEM] * ins if ins > 0 else [pl.BlockSpec()] * -ins,
        out_specs=jax.tree.map(lambda _: VMEM if ins > 0 else pl.BlockSpec(), outs),
        scratch_shapes=scratch,
        compiler_params=pltpu.CompilerParams(vmem_limit_bytes=grant),
        cost_estimate=pl.CostEstimate(flops=cost, bytes_accessed=1 << 20, transcendentals=0),
    )


def paired(block, first):
    route = [(i, i + 1) for i in range(first, PEERS - 1, 2)]
    return lax.ppermute(block, "dom", route + [(j, i) for i, j in route])


def swapped(block):
    return lax.ppermute(block, "body", [(0, 1), (1, 0)])


def exchanged(block):
    return lax.all_to_all(block, "dom", split_axis=0, concat_axis=0, tiled=True)


def local(
    displacement,
    connectivity,
    plastic_strain,
    element_size,
    yield_stress,
    external_force,
    slave_disp,
    pair_owner,
    pair_local,
    active,
    master_gap,
    master_normal,
    master_disp,
    coupling,
    quad_weight,
):
    seg_major = lambda x: jnp.transpose(x[0], (1, 0, 2))
    send, place = call(
        pack_kernel,
        -4,
        (shape(PEERS * SLOTS, 4 * LANES, dtype=BF16), shape(PEERS * SLOTS, SEG, dtype=BF16)),
        1 << 27,
        grant=60 << 20,
    )(pair_owner[0].T, pair_local[0].T, active, seg_major(slave_disp))
    got = exchanged(send)

    own = displacement[0].reshape(3, BLOCKS, LANES)
    odd = lax.axis_index("dom") & 1
    parity = jnp.full((8, LANES), odd, jnp.int32)
    first, last = own[:, :HALO], own[:, BLOCKS - HALO :]
    far = paired(jnp.where(odd == 1, last, first), 1)
    near = paired(jnp.where(odd == 1, first, last), 0)
    rows, mortar, weight = call(
        rows_kernel, 5, (shape(4, SEG, LANES), shape(LANES, LANES, dtype=BF16), shape(8, LANES)), 1 << 20
    )(master_gap[0], seg_major(master_normal), seg_major(master_disp), coupling, quad_weight.reshape(1, LANES))
    rows = swapped(rows)
    links = jnp.transpose(connectivity[0].reshape(8, BLOCKS, LANES), (1, 0, 2)).reshape(8 * BLOCKS, LANES)
    part = call(
        gather_kernel, 2, shape(3, 8 * BLOCKS, LANES), 1 << 30, (pltpu.VMEM((BLOCKS, LANES), jnp.int32),)
    )(own, links)
    far_force, near_force, own_force = call(
        element_kernel,
        10,
        (shape(3, HALO, LANES), shape(3, HALO, LANES), shape(3, BLOCKS, LANES)),
        1 << 32,
        (
            pltpu.VMEM((3, 2 * HALO + BLOCKS + 8, LANES), F32),
            pltpu.VMEM((2 * HALO + BLOCKS + 8, LANES), jnp.int32),
            pltpu.VMEM((8 * BLOCKS, LANES), F32),
            pltpu.VMEM((8 * BLOCKS, LANES), F32),
            pltpu.VMEM((3, 8 * BLOCKS, LANES), F32),
            pltpu.VMEM((3, 2 * HALO + BLOCKS + 16, LANES), F32),
        ),
    )(
        parity,
        far,
        near,
        own,
        links,
        part,
        plastic_strain[0].reshape(6, BLOCKS, LANES),
        element_size.reshape(BLOCKS, LANES),
        yield_stress.reshape(BLOCKS, LANES),
        external_force[0].reshape(3, BLOCKS, LANES),
    )

    got, far_force, near_force = lax.optimization_barrier((got, far_force, near_force))
    back, force = call(
        master_kernel, 4, (shape(PEERS * SLOTS, 3 * LANES, dtype=BF16), shape(3, SEG, LANES)), 1 << 28
    )(got, rows, mortar, weight)
    returned = exchanged(back)
    slave_force = call(slave_kernel, 3, shape(3, SEG, LANES), 1 << 27)(returned, place, mortar)
    parity_late, slave_force = lax.optimization_barrier((parity, slave_force))
    residual, master_force = call(finish_kernel, 5, (shape(3, BLOCKS, LANES), shape(3, SEG, LANES)), 1 << 20)(
        parity_late, own_force, paired(far_force, 1), paired(near_force, 0), swapped(force)
    )
    return (
        residual.reshape(1, 3, BLOCKS * LANES),
        jnp.transpose(slave_force, (1, 0, 2))[None],
        jnp.transpose(master_force, (1, 0, 2))[None],
    )


def solution(mesh):
    return jax.shard_map(
        local,
        mesh=mesh,
        in_specs=(
            P("body", None, "dom"),
            P("body", None, "dom"),
            P("body", None, "dom"),
            P("body", "dom"),
            P("body", "dom"),
            P("body", None, "dom"),
            P("body", "dom", None, None),
            P("body", "dom", None),
            P("body", "dom", None),
            P("body", "dom"),
            P("body", "dom", None),
            P("body", "dom", None, None),
            P("body", "dom", None, None),
            P(),
            P(),
        ),
        out_specs=(
            P("body", None, "dom"),
            P("body", "dom", None, None),
            P("body", "dom", None, None),
        ),
        check_vma=False,
    )
```

```python
import jax
import jax.numpy as jnp
import numpy as np
from jax import lax
from jax.experimental import pallas as pl
from jax.experimental.pallas import tpu as pltpu
from jax.sharding import PartitionSpec as P


LANES = 128
HALO = 16
BLOCKS = 32
WINDOW = 48
SLOTS = 8
PEERS = 64
SEG = 128
F32 = jnp.float32
BF16 = jnp.bfloat16
NT = (((1,), (1,)), ((), ()))
TN = (((0,), (0,)), ((), ()))
NN = (((1,), (0,)), ((), ()))


def dot(a, b, dims=NN):
    return lax.dot_general(a, b, dims, preferred_element_type=F32)


def iota(shape, dim, dtype=jnp.int32):
    return lax.broadcasted_iota(jnp.int32, shape, dim).astype(dtype)


def own_rows(m):
    return range(max(0, HALO - 8 * m), min(33, HALO + BLOCKS - 7 - 8 * m))


def reach_of(links, m, a):
    return links[pl.ds(64 * m + a, 8, stride=8), :] + iota((8, LANES), 1)


def pack_pair(x, y, table):
    most = jnp.max(jnp.maximum(jnp.abs(x), jnp.abs(y)), axis=0, keepdims=True)
    most = jnp.maximum(jnp.max(most, axis=1, keepdims=True), 1e-30)
    scale = 32767.0 / most

    def whole(v):
        v = v * scale
        return (v + jnp.where(v < 0.0, -0.5, 0.5)).astype(jnp.int32)

    table[0 : x.shape[0], :] = (whole(x) << 16) | (whole(y) & 65535)
    return most / 32767.0


def gather_rows(table, third, unit, links, m, a, hs, base):
    reach = reach_of(links, m, a)
    hi, lo = reach >> 7, reach & 127
    pair, single = jnp.zeros((8, LANES), jnp.int32), jnp.zeros((8, LANES), F32)
    for h in hs:
        here = hi == h
        rows = slice(8 * m + h - base, 8 * m + h - base + 8)
        pair = jnp.where(here, jnp.take_along_axis(table[rows, :], lo, axis=1), pair)
        single = jnp.where(here, jnp.take_along_axis(third[2, rows, :], lo, axis=1), single)
    return [(pair >> 16).astype(F32) * unit, ((pair << 16) >> 16).astype(F32) * unit, single]


def gather_kernel(own, links, nodal, table):
    unit = pack_pair(own[0], own[1], table)
    for m in range(BLOCKS // 8):
        for a in range(8):
            got = gather_rows(table, own, unit, links, m, a, own_rows(m), HALO)
            at = a * BLOCKS + 8 * m
            for i in range(3):
                nodal[i, at : at + 8, :] = got[i]


def element_kernel(parity, far, near, own, links, part, strain, edge_ref, yield_ref, ext, far_out, near_out, own_out,
                   disp, table, lo_s, hi_s, force_s, acc):
    odd = parity[0:1, :] == 1
    disp[:, 0:HALO, :] = jnp.where(odd, near[...], far[...])
    disp[:, HALO : HALO + BLOCKS, :] = own[...]
    disp[:, HALO + BLOCKS : 2 * HALO + BLOCKS, :] = jnp.where(odd, far[...], near[...])
    acc[...] = jnp.zeros_like(acc)
    unit = pack_pair(disp[0, : 2 * HALO + BLOCKS], disp[1, : 2 * HALO + BLOCKS], table)
    block = iota((8, LANES), 0) * LANES
    for m in range(BLOCKS // 8):
        rest = [h for h in range(33) if h not in own_rows(m)]
        nodal = []
        for a in range(8):
            at = slice(a * BLOCKS + 8 * m, a * BLOCKS + 8 * m + 8)
            got = gather_rows(table, disp, unit, links, m, a, rest, 0)
            nodal.append([got[i] + part[i, at, :] for i in range(3)])
            reach = reach_of(links, m, a) + block
            hi_s[at, :] = (reach >> 7).astype(F32)
            lo_s[at, :] = (reach & 127).astype(F32)
        edge = edge_ref[8 * m : 8 * m + 8, :]
        scale = 0.25 / edge
        grad = [[None] * 3 for _ in range(3)]
        for i in range(3):
            u = [nodal[a][i] for a in range(8)]
            for j in range(3):
                plus = [u[a] for a in range(8) if a >> j & 1]
                minus = [u[a] for a in range(8) if not a >> j & 1]
                total = sum(p - q for p, q in zip(plus, minus))
                grad[i][j] = total * scale
        old = [strain[c, 8 * m : 8 * m + 8, :] for c in range(6)]
        exx = grad[0][0] - old[0]
        eyy = grad[1][1] - old[1]
        ezz = grad[2][2] - old[2]
        exy = 0.5 * (grad[0][1] + grad[1][0]) - old[3]
        eyz = 0.5 * (grad[1][2] + grad[2][1]) - old[4]
        ezx = 0.5 * (grad[2][0] + grad[0][2]) - old[5]
        trace = exx + eyy + ezz
        sxx = trace + exx
        syy = trace + eyy
        szz = trace + ezz
        mean = (sxx + syy + szz) / 3.0
        dxx, dyy, dzz = sxx - mean, syy - mean, szz - mean
        size = jnp.sqrt(dxx * dxx + dyy * dyy + dzz * dzz + 2.0 * (exy * exy + eyz * eyz + ezx * ezx))
        radius = np.float32(np.sqrt(2.0 / 3.0)) * yield_ref[8 * m : 8 * m + 8, :]
        factor = radius / jnp.maximum(size, radius)
        area = 0.25 * edge * edge
        xy, yz, zx = area * factor * exy, area * factor * eyz, area * factor * ezx
        xx = area * (mean + factor * dxx)
        yy = area * (mean + factor * dyy)
        zz = area * (mean + factor * dzz)
        for i, (tx, ty, tz) in enumerate(((xx, xy, zx), (xy, yy, yz), (zx, yz, zz))):
            four = [tx + ty, ty - tx, tx - ty, -tx - ty]
            for a in range(8):
                pick = four[(0 if a & 1 else 1) if a & 2 else (2 if a & 1 else 3)]
                f = pick + tz if a & 4 else pick - tz
                force_s[i, a * BLOCKS + 8 * m : a * BLOCKS + 8 * m + 8, :] = f
    row = iota((16, LANES), 0, F32)
    rows = [(row + 16.0 * t).astype(BF16) for t in range(8)]
    zero = jnp.zeros((16, LANES), BF16)
    one = jnp.ones((16, LANES), BF16)

    def wide(ref, *at):
        return jnp.broadcast_to(ref[at], (16, LANES)).astype(BF16)

    for m in range(BLOCKS // 8):
        sums = jnp.zeros((3 * WINDOW, LANES), F32)
        for s in range(8):
            left, right = [], []
            for a in range(8):
                at = slice(a * BLOCKS + 8 * m + s, a * BLOCKS + 8 * m + s + 1)
                hi = wide(hi_s, at, slice(None))
                lo = wide(lo_s, at, slice(None))
                here = [hi == rows[t] for t in range(WINDOW // 16)]
                parts = []
                for i in range(3):
                    f = wide(force_s, i, at, slice(None))
                    parts += [jnp.where(h, f, zero) for h in here]
                left.append(jnp.concatenate(parts, axis=0))
                right.append(jnp.concatenate([jnp.where(lo == r, one, zero) for r in rows], axis=0))
            sums = sums + dot(jnp.concatenate(left, axis=1), jnp.concatenate(right, axis=1), NT)
        for i in range(3):
            acc[i, 8 * m : 8 * m + WINDOW, :] += sums[i * WINDOW : (i + 1) * WINDOW]
    low, high = acc[:, 0:HALO, :], acc[:, HALO + BLOCKS : 2 * HALO + BLOCKS, :]
    far_out[...] = jnp.where(odd, high, low)
    near_out[...] = jnp.where(odd, low, high)
    own_out[...] = acc[:, HALO : HALO + BLOCKS, :] - ext[...]


def finish_kernel(parity, own, far, near, force, out, force_out):
    odd = parity[0:1, :] == 1
    force_out[...] = force[...]
    out[:, 0:HALO, :] = own[:, 0:HALO, :] + jnp.where(odd, near[...], far[...])
    out[:, HALO:BLOCKS, :] = own[:, HALO:BLOCKS, :] + jnp.where(odd, far[...], near[...])


def pack_kernel(owner, where, active, disp, send, slots, held, sem):
    names = iota((PEERS, SEG), 0)
    earlier = jnp.where(iota((SEG, SEG), 0) < iota((SEG, SEG), 1), 1.0, 0.0).astype(BF16)
    ones = jnp.ones((SEG, SEG), BF16)
    hot = [owner[k : k + 1, :] == names for k in range(2)]
    hot16 = [jnp.where(h, 1.0, 0.0).astype(BF16) for h in hot]
    before = [dot(hot16[0], earlier), dot(hot16[1], earlier) + dot(hot16[0], ones)]
    slot, mark = [], []
    for k in range(2):
        rank = jnp.sum(jnp.where(hot[k], before[k], 0.0), axis=0, keepdims=True)
        slot.append(owner[k : k + 1, :] * SLOTS + rank.astype(jnp.int32))
        mark.append(((where[k : k + 1, :] + 1) * active[...]).astype(F32))
        slots[k : k + 1, :] = slot[k]
    copies = []
    for part in range(PEERS * SLOTS // SEG):
        span = slice(part * SEG, (part + 1) * SEG)
        rows = iota((SEG, SEG), 0) + part * SEG
        here = [slot[k] == rows for k in range(2)]
        sent = jnp.where(here[0] | here[1], 1.0, 0.0).astype(BF16)
        meta = jnp.where(here[0], mark[0], jnp.where(here[1], mark[1], 0.0)).astype(BF16)
        for c in range(3):
            held[span, c * LANES : (c + 1) * LANES] = dot(sent, disp[c]).astype(BF16)
        held[span, 3 * LANES :] = dot(meta, ones).astype(BF16)
        copies.append(pltpu.make_async_copy(held.at[span], send.at[span], sem.at[part]))
        copies[-1].start()
    for copy in copies:
        copy.wait()


def rows_kernel(gap, normal, mdisp, coupling, quad_weight, slots, rows, mortar, weight, slots_out):
    slots_out[...] = slots[...]
    mortar[...] = mortar_of(coupling)
    weight[...] = jnp.broadcast_to(quad_weight[...], weight.shape)
    total = gap[...]
    for c in range(3):
        n = normal[c]
        total = total + n * mdisp[c].astype(F32)
        rows[1 + c] = n
    rows[0] = total


def mortar_of(coupling):
    eye = jnp.where(iota((LANES, LANES), 0) == iota((LANES, LANES), 1), 1.0, 0.0)
    return (eye + coupling[...].astype(F32)).astype(BF16)


def split(x):
    top = x.astype(BF16)
    return top, (x - top.astype(F32)).astype(BF16)


def master_kernel(got, rows, mortar_ref, weight, back, force, held, table, sem):
    mortar = mortar_ref[...]
    for c in range(4):
        table[0:SEG, c * LANES : (c + 1) * LANES], table[SEG:, c * LANES : (c + 1) * LANES] = split(rows[c])
    name = iota((SEG, LANES), 1, F32) + 1.0
    parts = range(PEERS * SLOTS // SEG)
    hots, copies = [], []
    for part in parts:
        span = slice(part * SEG, (part + 1) * SEG)
        hot = jnp.where(got[span, 3 * LANES :].astype(F32) == name, 1.0, 0.0).astype(BF16)
        hots.append(hot)
        found = dot(jnp.concatenate([hot, hot], axis=1), table[...])
        gap = found[:, :LANES]
        normal = [found[:, (1 + c) * LANES : (2 + c) * LANES] for c in range(3)]
        for c in range(3):
            gap = gap - normal[c] * dot(got[span, c * LANES : (c + 1) * LANES], mortar)
        press = weight[0:1, :] * (2.0 * jnp.maximum(gap, 0.0))
        for c in range(3):
            held[span, c * LANES : (c + 1) * LANES] = (press * normal[c]).astype(BF16)
        copies.append(pltpu.make_async_copy(held.at[span], back.at[span], sem.at[part]))
        copies[-1].start()
    total = dot(jnp.concatenate(hots, axis=0), held[...], TN)
    for c in range(3):
        force[c] = -total[:, c * LANES : (c + 1) * LANES]
    for copy in copies:
        copy.wait()


def slave_kernel(got, slots, mortar_ref, out, held, sem):
    mortar = mortar_ref[...]
    place = []
    for part in range(PEERS * SLOTS // SEG):
        rows = iota((SEG, SEG), 0) + part * SEG
        here = (slots[0:1, :] == rows) | (slots[1:2, :] == rows)
        place.append(jnp.where(here, 1.0, 0.0).astype(BF16))
    pair = dot(jnp.concatenate(place, axis=0), got[...], TN).astype(BF16)
    copies = []
    for c in range(3):
        held[c] = dot(pair[:, c * LANES : (c + 1) * LANES], mortar, NT)
        copies.append(pltpu.make_async_copy(held.at[c], out.at[c], sem.at[c]))
        copies[-1].start()
    for copy in copies:
        copy.wait()


def shape(*dims, dtype=F32):
    return jax.ShapeDtypeStruct(dims, dtype)


VMEM = pl.BlockSpec(memory_space=pltpu.VMEM)


HBM = pl.BlockSpec(memory_space=pl.ANY)


def call(kernel, ins, outs, cost, scratch=(), grant=8 << 20, places=None):
    return pl.pallas_call(
        kernel,
        out_shape=outs,
        in_specs=[VMEM] * ins if ins > 0 else [pl.BlockSpec()] * -ins,
        out_specs=jax.tree.map(lambda _: VMEM, outs) if places is None else places,
        scratch_shapes=scratch,
        compiler_params=pltpu.CompilerParams(vmem_limit_bytes=grant),
        cost_estimate=pl.CostEstimate(flops=cost, bytes_accessed=1 << 20, transcendentals=0),
    )


def paired(block, first):
    route = [(i, i + 1) for i in range(first, PEERS - 1, 2)]
    return lax.ppermute(block, "dom", route + [(j, i) for i, j in route])


def swapped(block):
    return lax.ppermute(block, "body", [(0, 1), (1, 0)])


def exchanged(block):
    return lax.all_to_all(block, "dom", split_axis=0, concat_axis=0, tiled=True)


def local(
    displacement,
    connectivity,
    plastic_strain,
    element_size,
    yield_stress,
    external_force,
    slave_disp,
    pair_owner,
    pair_local,
    active,
    master_gap,
    master_normal,
    master_disp,
    coupling,
    quad_weight,
):
    seg_major = lambda x: jnp.transpose(x[0], (1, 0, 2))
    send, slots = call(
        pack_kernel,
        -4,
        (shape(PEERS * SLOTS, 4 * LANES, dtype=BF16), shape(2, SEG, dtype=jnp.int32)),
        1 << 27,
        (pltpu.VMEM((PEERS * SLOTS, 4 * LANES), BF16), pltpu.SemaphoreType.DMA((4,))),
        grant=60 << 20,
        places=(HBM, pl.BlockSpec()),
    )(pair_owner[0].T, pair_local[0].T, active, seg_major(slave_disp))
    got = exchanged(send)

    own = displacement[0].reshape(3, BLOCKS, LANES)
    odd = lax.axis_index("dom") & 1
    parity = jnp.full((8, LANES), odd, jnp.int32)
    first, last = own[:, :HALO], own[:, BLOCKS - HALO :]
    far = paired(jnp.where(odd == 1, last, first), 1)
    near = paired(jnp.where(odd == 1, first, last), 0)
    rows, mortar, weight, slots = call(
        rows_kernel,
        6,
        (
            shape(4, SEG, LANES),
            shape(LANES, LANES, dtype=BF16),
            shape(8, LANES),
            shape(2, SEG, dtype=jnp.int32),
        ),
        1 << 20,
    )(master_gap[0], seg_major(master_normal), seg_major(master_disp), coupling, quad_weight.reshape(1, LANES), slots)
    rows = swapped(rows)
    links = jnp.transpose(connectivity[0].reshape(8, BLOCKS, LANES), (1, 0, 2)).reshape(8 * BLOCKS, LANES)
    part = call(
        gather_kernel, 2, shape(3, 8 * BLOCKS, LANES), 1 << 30, (pltpu.VMEM((BLOCKS, LANES), jnp.int32),)
    )(own, links)
    far_force, near_force, own_force = call(
        element_kernel,
        10,
        (shape(3, HALO, LANES), shape(3, HALO, LANES), shape(3, BLOCKS, LANES)),
        1 << 32,
        (
            pltpu.VMEM((3, 2 * HALO + BLOCKS + 8, LANES), F32),
            pltpu.VMEM((2 * HALO + BLOCKS + 8, LANES), jnp.int32),
            pltpu.VMEM((8 * BLOCKS, LANES), F32),
            pltpu.VMEM((8 * BLOCKS, LANES), F32),
            pltpu.VMEM((3, 8 * BLOCKS, LANES), F32),
            pltpu.VMEM((3, 2 * HALO + BLOCKS + 16, LANES), F32),
        ),
    )(
        parity,
        far,
        near,
        own,
        links,
        part,
        plastic_strain[0].reshape(6, BLOCKS, LANES),
        element_size.reshape(BLOCKS, LANES),
        yield_stress.reshape(BLOCKS, LANES),
        external_force[0].reshape(3, BLOCKS, LANES),
    )

    got, far_force, near_force = lax.optimization_barrier((got, far_force, near_force))
    back, force = call(
        master_kernel,
        4,
        (shape(PEERS * SLOTS, 3 * LANES, dtype=BF16), shape(3, SEG, LANES)),
        1 << 28,
        (
            pltpu.VMEM((PEERS * SLOTS, 3 * LANES), BF16),
            pltpu.VMEM((2 * SEG, 4 * LANES), BF16),
            pltpu.SemaphoreType.DMA((4,)),
        ),
        places=(HBM, VMEM),
    )(got, rows, mortar, weight)
    returned = exchanged(back)
    slave_force = call(
        slave_kernel,
        3,
        shape(3, SEG, LANES),
        1 << 27,
        (pltpu.VMEM((3, SEG, LANES), F32), pltpu.SemaphoreType.DMA((3,))),
        places=HBM,
    )(returned, slots, mortar)
    residual, master_force = call(finish_kernel, 5, (shape(3, BLOCKS, LANES), shape(3, SEG, LANES)), 1 << 20)(
        parity, own_force, paired(far_force, 1), paired(near_force, 0), swapped(force)
    )
    return (
        residual.reshape(1, 3, BLOCKS * LANES),
        jnp.transpose(slave_force, (1, 0, 2))[None],
        jnp.transpose(master_force, (1, 0, 2))[None],
    )


def solution(mesh):
    return jax.shard_map(
        local,
        mesh=mesh,
        in_specs=(
            P("body", None, "dom"),
            P("body", None, "dom"),
            P("body", None, "dom"),
            P("body", "dom"),
            P("body", "dom"),
            P("body", None, "dom"),
            P("body", "dom", None, None),
            P("body", "dom", None),
            P("body", "dom", None),
            P("body", "dom"),
            P("body", "dom", None),
            P("body", "dom", None, None),
            P("body", "dom", None, None),
            P(),
            P(),
        ),
        out_specs=(
            P("body", None, "dom"),
            P("body", "dom", None, None),
            P("body", "dom", None, None),
        ),
        check_vma=False,
    )
```

```python
import jax
import jax.numpy as jnp
import numpy as np
from jax import lax
from jax.experimental import pallas as pl
from jax.experimental.pallas import tpu as pltpu
from jax.sharding import PartitionSpec as P


LANES = 128
HALO = 16
BLOCKS = 32
WINDOW = 48
SLOTS = 8
PEERS = 64
SEG = 128
F32 = jnp.float32
BF16 = jnp.bfloat16
NT = (((1,), (1,)), ((), ()))
TN = (((0,), (0,)), ((), ()))
NN = (((1,), (0,)), ((), ()))


def dot(a, b, dims=NN):
    return lax.dot_general(a, b, dims, preferred_element_type=F32)


def iota(shape, dim, dtype=jnp.int32):
    return lax.broadcasted_iota(jnp.int32, shape, dim).astype(dtype)


def own_rows(m):
    return range(max(0, HALO - 8 * m), min(33, HALO + BLOCKS - 7 - 8 * m))


def reach_of(links, m, a):
    return links[pl.ds(64 * m + a, 8, stride=8), :] + iota((8, LANES), 1)


def pack_pair(x, y, table):
    most = jnp.max(jnp.maximum(jnp.abs(x), jnp.abs(y)), axis=0, keepdims=True)
    most = jnp.maximum(jnp.max(most, axis=1, keepdims=True), 1e-30)
    scale = 32767.0 / most

    def whole(v):
        v = v * scale
        return (v + jnp.where(v < 0.0, -0.5, 0.5)).astype(jnp.int32)

    table[0 : x.shape[0], :] = (whole(x) << 16) | (whole(y) & 65535)
    return most / 32767.0


def gather_rows(table, third, unit, links, m, a, hs, base):
    reach = reach_of(links, m, a)
    hi, lo = reach >> 7, reach & 127
    pair, single = jnp.zeros((8, LANES), jnp.int32), jnp.zeros((8, LANES), F32)
    for h in hs:
        here = hi == h
        rows = slice(8 * m + h - base, 8 * m + h - base + 8)
        pair = jnp.where(here, jnp.take_along_axis(table[rows, :], lo, axis=1), pair)
        single = jnp.where(here, jnp.take_along_axis(third[2, rows, :], lo, axis=1), single)
    return [(pair >> 16).astype(F32) * unit, ((pair << 16) >> 16).astype(F32) * unit, single]


def gather_kernel(own, links, nodal, table):
    unit = pack_pair(own[0], own[1], table)
    for m in range(BLOCKS // 8):
        for a in range(8):
            got = gather_rows(table, own, unit, links, m, a, own_rows(m), HALO)
            at = a * BLOCKS + 8 * m
            for i in range(3):
                nodal[i, at : at + 8, :] = got[i]


def element_kernel(parity, far, near, own, links, part, strain, edge_ref, yield_ref, ext, far_out, near_out, own_out,
                   disp, table, lo_s, hi_s, force_s, acc):
    odd = parity[0:1, :] == 1
    disp[:, 0:HALO, :] = jnp.where(odd, near[...], far[...])
    disp[:, HALO : HALO + BLOCKS, :] = own[...]
    disp[:, HALO + BLOCKS : 2 * HALO + BLOCKS, :] = jnp.where(odd, far[...], near[...])
    acc[...] = jnp.zeros_like(acc)
    unit = pack_pair(disp[0, : 2 * HALO + BLOCKS], disp[1, : 2 * HALO + BLOCKS], table)
    block = iota((8, LANES), 0) * LANES
    for m in range(BLOCKS // 8):
        rest = [h for h in range(33) if h not in own_rows(m)]
        nodal = []
        for a in range(8):
            at = slice(a * BLOCKS + 8 * m, a * BLOCKS + 8 * m + 8)
            got = gather_rows(table, disp, unit, links, m, a, rest, 0)
            nodal.append([got[i] + part[i, at, :] for i in range(3)])
            reach = reach_of(links, m, a) + block
            hi_s[at, :] = (reach >> 7).astype(F32)
            lo_s[at, :] = (reach & 127).astype(F32)
        edge = edge_ref[8 * m : 8 * m + 8, :]
        scale = 0.25 / edge
        grad = [[None] * 3 for _ in range(3)]
        for i in range(3):
            u = [nodal[a][i] for a in range(8)]
            for j in range(3):
                plus = [u[a] for a in range(8) if a >> j & 1]
                minus = [u[a] for a in range(8) if not a >> j & 1]
                total = sum(p - q for p, q in zip(plus, minus))
                grad[i][j] = total * scale
        old = [strain[c, 8 * m : 8 * m + 8, :] for c in range(6)]
        exx = grad[0][0] - old[0]
        eyy = grad[1][1] - old[1]
        ezz = grad[2][2] - old[2]
        exy = 0.5 * (grad[0][1] + grad[1][0]) - old[3]
        eyz = 0.5 * (grad[1][2] + grad[2][1]) - old[4]
        ezx = 0.5 * (grad[2][0] + grad[0][2]) - old[5]
        trace = exx + eyy + ezz
        sxx = trace + exx
        syy = trace + eyy
        szz = trace + ezz
        mean = (sxx + syy + szz) / 3.0
        dxx, dyy, dzz = sxx - mean, syy - mean, szz - mean
        size = jnp.sqrt(dxx * dxx + dyy * dyy + dzz * dzz + 2.0 * (exy * exy + eyz * eyz + ezx * ezx))
        radius = np.float32(np.sqrt(2.0 / 3.0)) * yield_ref[8 * m : 8 * m + 8, :]
        factor = radius / jnp.maximum(size, radius)
        area = 0.25 * edge * edge
        xy, yz, zx = area * factor * exy, area * factor * eyz, area * factor * ezx
        xx = area * (mean + factor * dxx)
        yy = area * (mean + factor * dyy)
        zz = area * (mean + factor * dzz)
        for i, (tx, ty, tz) in enumerate(((xx, xy, zx), (xy, yy, yz), (zx, yz, zz))):
            four = [tx + ty, ty - tx, tx - ty, -tx - ty]
            for a in range(8):
                pick = four[(0 if a & 1 else 1) if a & 2 else (2 if a & 1 else 3)]
                f = pick + tz if a & 4 else pick - tz
                force_s[i, a * BLOCKS + 8 * m : a * BLOCKS + 8 * m + 8, :] = f
    row = iota((16, LANES), 0, F32)
    rows = [(row + 16.0 * t).astype(BF16) for t in range(8)]
    zero = jnp.zeros((16, LANES), BF16)
    one = jnp.ones((16, LANES), BF16)

    def wide(ref, *at):
        return jnp.broadcast_to(ref[at], (16, LANES)).astype(BF16)

    for m in range(BLOCKS // 8):
        sums = jnp.zeros((3 * WINDOW, LANES), F32)
        for s in range(8):
            left, right = [], []
            for a in range(8):
                at = slice(a * BLOCKS + 8 * m + s, a * BLOCKS + 8 * m + s + 1)
                hi = wide(hi_s, at, slice(None))
                lo = wide(lo_s, at, slice(None))
                here = [hi == rows[t] for t in range(WINDOW // 16)]
                parts = []
                for i in range(3):
                    f = wide(force_s, i, at, slice(None))
                    parts += [jnp.where(h, f, zero) for h in here]
                left.append(jnp.concatenate(parts, axis=0))
                right.append(jnp.concatenate([jnp.where(lo == r, one, zero) for r in rows], axis=0))
            sums = sums + dot(jnp.concatenate(left, axis=1), jnp.concatenate(right, axis=1), NT)
        for i in range(3):
            acc[i, 8 * m : 8 * m + WINDOW, :] += sums[i * WINDOW : (i + 1) * WINDOW]
    low, high = acc[:, 0:HALO, :], acc[:, HALO + BLOCKS : 2 * HALO + BLOCKS, :]
    far_out[...] = jnp.where(odd, high, low)
    near_out[...] = jnp.where(odd, low, high)
    own_out[...] = acc[:, HALO : HALO + BLOCKS, :] - ext[...]


def finish_kernel(parity, own, far, near, force, out, force_out):
    odd = parity[0:1, :] == 1
    force_out[...] = force[...]
    out[:, 0:HALO, :] = own[:, 0:HALO, :] + jnp.where(odd, near[...], far[...])
    out[:, HALO:BLOCKS, :] = own[:, HALO:BLOCKS, :] + jnp.where(odd, far[...], near[...])


def pack_kernel(owner, where, active, disp, send, slots):
    names = iota((PEERS, SEG), 0)
    earlier = jnp.where(iota((SEG, SEG), 0) < iota((SEG, SEG), 1), 1.0, 0.0).astype(BF16)
    ones = jnp.ones((SEG, SEG), BF16)
    hot = [owner[k : k + 1, :] == names for k in range(2)]
    hot16 = [jnp.where(h, 1.0, 0.0).astype(BF16) for h in hot]
    before = [dot(hot16[0], earlier), dot(hot16[1], earlier) + dot(hot16[0], ones)]
    rows = iota((PEERS * SLOTS, SEG), 0)
    sent = jnp.zeros((PEERS * SLOTS, SEG), F32)
    meta = jnp.zeros((PEERS * SLOTS, SEG), F32)
    for k in range(2):
        rank = jnp.sum(jnp.where(hot[k], before[k], 0.0), axis=0, keepdims=True)
        slot = owner[k : k + 1, :] * SLOTS + rank.astype(jnp.int32)
        slots[k : k + 1, :] = slot
        mark = ((where[k : k + 1, :] + 1) * active[...]).astype(F32)
        here = slot == rows
        sent = jnp.where(here, 1.0, sent)
        meta = jnp.where(here, mark, meta)
    sent = sent.astype(BF16)
    for c in range(3):
        send[:, c * LANES : (c + 1) * LANES] = dot(sent, disp[c]).astype(BF16)
    send[:, 3 * LANES :] = dot(meta.astype(BF16), ones).astype(BF16)


def rows_kernel(gap, normal, mdisp, coupling, quad_weight, slots, rows, mortar, weight, slots_out):
    slots_out[...] = slots[...]
    mortar[...] = mortar_of(coupling)
    weight[...] = jnp.broadcast_to(quad_weight[...], weight.shape)
    total = gap[...]
    for c in range(3):
        n = normal[c]
        total = total + n * mdisp[c].astype(F32)
        rows[1 + c] = n
    rows[0] = total


def mortar_of(coupling):
    eye = jnp.where(iota((LANES, LANES), 0) == iota((LANES, LANES), 1), 1.0, 0.0)
    return (eye + coupling[...].astype(F32)).astype(BF16)


def split(x):
    top = x.astype(BF16)
    return top, (x - top.astype(F32)).astype(BF16)


def master_kernel(got, rows, mortar_ref, weight, back, force, held, table, sem):
    mortar = mortar_ref[...]
    for c in range(4):
        table[0:SEG, c * LANES : (c + 1) * LANES], table[SEG:, c * LANES : (c + 1) * LANES] = split(rows[c])
    name = iota((SEG, LANES), 1, F32) + 1.0
    parts = range(PEERS * SLOTS // SEG)
    hots, copies = [], []
    for part in parts:
        span = slice(part * SEG, (part + 1) * SEG)
        hot = jnp.where(got[span, 3 * LANES :].astype(F32) == name, 1.0, 0.0).astype(BF16)
        hots.append(hot)
        found = dot(jnp.concatenate([hot, hot], axis=1), table[...])
        gap = found[:, :LANES]
        normal = [found[:, (1 + c) * LANES : (2 + c) * LANES] for c in range(3)]
        for c in range(3):
            gap = gap - normal[c] * dot(got[span, c * LANES : (c + 1) * LANES], mortar)
        press = weight[0:1, :] * (2.0 * jnp.maximum(gap, 0.0))
        for c in range(3):
            held[span, c * LANES : (c + 1) * LANES] = (press * normal[c]).astype(BF16)
        copies.append(pltpu.make_async_copy(held.at[span], back.at[span], sem.at[part]))
        copies[-1].start()
    total = dot(jnp.concatenate(hots, axis=0), held[...], TN)
    for c in range(3):
        force[c] = -total[:, c * LANES : (c + 1) * LANES]
    for copy in copies:
        copy.wait()


def slave_kernel(got, slots, mortar_ref, out, held, sem):
    mortar = mortar_ref[...]
    place = []
    for part in range(PEERS * SLOTS // SEG):
        rows = iota((SEG, SEG), 0) + part * SEG
        here = (slots[0:1, :] == rows) | (slots[1:2, :] == rows)
        place.append(jnp.where(here, 1.0, 0.0).astype(BF16))
    pair = dot(jnp.concatenate(place, axis=0), got[...], TN).astype(BF16)
    copies = []
    for c in range(3):
        held[c] = dot(pair[:, c * LANES : (c + 1) * LANES], mortar, NT)
        copies.append(pltpu.make_async_copy(held.at[c], out.at[c], sem.at[c]))
        copies[-1].start()
    for copy in copies:
        copy.wait()


def shape(*dims, dtype=F32):
    return jax.ShapeDtypeStruct(dims, dtype)


VMEM = pl.BlockSpec(memory_space=pltpu.VMEM)


HBM = pl.BlockSpec(memory_space=pl.ANY)


def call(kernel, ins, outs, cost, scratch=(), grant=8 << 20, places=None):
    return pl.pallas_call(
        kernel,
        out_shape=outs,
        in_specs=[VMEM] * ins if ins > 0 else [pl.BlockSpec()] * -ins,
        out_specs=jax.tree.map(lambda _: VMEM, outs) if places is None else places,
        scratch_shapes=scratch,
        compiler_params=pltpu.CompilerParams(vmem_limit_bytes=grant),
        cost_estimate=pl.CostEstimate(flops=cost, bytes_accessed=1 << 20, transcendentals=0),
    )


def paired(block, first):
    route = [(i, i + 1) for i in range(first, PEERS - 1, 2)]
    return lax.ppermute(block, "dom", route + [(j, i) for i, j in route])


def swapped(block):
    return lax.ppermute(block, "body", [(0, 1), (1, 0)])


def exchanged(block):
    return lax.all_to_all(block, "dom", split_axis=0, concat_axis=0, tiled=True)


def local(
    displacement,
    connectivity,
    plastic_strain,
    element_size,
    yield_stress,
    external_force,
    slave_disp,
    pair_owner,
    pair_local,
    active,
    master_gap,
    master_normal,
    master_disp,
    coupling,
    quad_weight,
):
    seg_major = lambda x: jnp.transpose(x[0], (1, 0, 2))
    send, slots = call(
        pack_kernel,
        -4,
        (shape(PEERS * SLOTS, 4 * LANES, dtype=BF16), shape(2, SEG, dtype=jnp.int32)),
        1 << 27,
        grant=60 << 20,
        places=(pl.BlockSpec(), pl.BlockSpec()),
    )(pair_owner[0].T, pair_local[0].T, active, seg_major(slave_disp))
    got = exchanged(send)

    own = displacement[0].reshape(3, BLOCKS, LANES)
    odd = lax.axis_index("dom") & 1
    parity = jnp.full((8, LANES), odd, jnp.int32)
    first, last = own[:, :HALO], own[:, BLOCKS - HALO :]
    far = paired(jnp.where(odd == 1, last, first), 1)
    near = paired(jnp.where(odd == 1, first, last), 0)
    rows, mortar, weight, slots = call(
        rows_kernel,
        6,
        (
            shape(4, SEG, LANES),
            shape(LANES, LANES, dtype=BF16),
            shape(8, LANES),
            shape(2, SEG, dtype=jnp.int32),
        ),
        1 << 20,
    )(master_gap[0], seg_major(master_normal), seg_major(master_disp), coupling, quad_weight.reshape(1, LANES), slots)
    rows = swapped(rows)
    links = jnp.transpose(connectivity[0].reshape(8, BLOCKS, LANES), (1, 0, 2)).reshape(8 * BLOCKS, LANES)
    part = call(
        gather_kernel, 2, shape(3, 8 * BLOCKS, LANES), 1 << 30, (pltpu.VMEM((BLOCKS, LANES), jnp.int32),)
    )(own, links)
    far_force, near_force, own_force = call(
        element_kernel,
        10,
        (shape(3, HALO, LANES), shape(3, HALO, LANES), shape(3, BLOCKS, LANES)),
        1 << 32,
        (
            pltpu.VMEM((3, 2 * HALO + BLOCKS + 8, LANES), F32),
            pltpu.VMEM((2 * HALO + BLOCKS + 8, LANES), jnp.int32),
            pltpu.VMEM((8 * BLOCKS, LANES), F32),
            pltpu.VMEM((8 * BLOCKS, LANES), F32),
            pltpu.VMEM((3, 8 * BLOCKS, LANES), F32),
            pltpu.VMEM((3, 2 * HALO + BLOCKS + 16, LANES), F32),
        ),
    )(
        parity,
        far,
        near,
        own,
        links,
        part,
        plastic_strain[0].reshape(6, BLOCKS, LANES),
        element_size.reshape(BLOCKS, LANES),
        yield_stress.reshape(BLOCKS, LANES),
        external_force[0].reshape(3, BLOCKS, LANES),
    )

    got, far_force, near_force = lax.optimization_barrier((got, far_force, near_force))
    back, force = call(
        master_kernel,
        4,
        (shape(PEERS * SLOTS, 3 * LANES, dtype=BF16), shape(3, SEG, LANES)),
        1 << 28,
        (
            pltpu.VMEM((PEERS * SLOTS, 3 * LANES), BF16),
            pltpu.VMEM((2 * SEG, 4 * LANES), BF16),
            pltpu.SemaphoreType.DMA((4,)),
        ),
        places=(HBM, VMEM),
    )(got, rows, mortar, weight)
    returned = exchanged(back)
    slave_force = call(
        slave_kernel,
        3,
        shape(3, SEG, LANES),
        1 << 27,
        (pltpu.VMEM((3, SEG, LANES), F32), pltpu.SemaphoreType.DMA((3,))),
        places=HBM,
    )(returned, slots, mortar)
    residual, master_force = call(finish_kernel, 5, (shape(3, BLOCKS, LANES), shape(3, SEG, LANES)), 1 << 20)(
        parity, own_force, paired(far_force, 1), paired(near_force, 0), swapped(force)
    )
    return (
        residual.reshape(1, 3, BLOCKS * LANES),
        jnp.transpose(slave_force, (1, 0, 2))[None],
        jnp.transpose(master_force, (1, 0, 2))[None],
    )


def solution(mesh):
    return jax.shard_map(
        local,
        mesh=mesh,
        in_specs=(
            P("body", None, "dom"),
            P("body", None, "dom"),
            P("body", None, "dom"),
            P("body", "dom"),
            P("body", "dom"),
            P("body", None, "dom"),
            P("body", "dom", None, None),
            P("body", "dom", None),
            P("body", "dom", None),
            P("body", "dom"),
            P("body", "dom", None),
            P("body", "dom", None, None),
            P("body", "dom", None, None),
            P(),
            P(),
        ),
        out_specs=(
            P("body", None, "dom"),
            P("body", "dom", None, None),
            P("body", "dom", None, None),
        ),
        check_vma=False,
    )
```

```python
import jax
import jax.numpy as jnp
import numpy as np
from jax import lax
from jax.experimental import pallas as pl
from jax.experimental.pallas import tpu as pltpu
from jax.sharding import PartitionSpec as P


LANES = 128
HALO = 16
BLOCKS = 32
WINDOW = 48
SLOTS = 8
PEERS = 64
SEG = 128
F32 = jnp.float32
BF16 = jnp.bfloat16
NT = (((1,), (1,)), ((), ()))
TN = (((0,), (0,)), ((), ()))
NN = (((1,), (0,)), ((), ()))


def dot(a, b, dims=NN):
    return lax.dot_general(a, b, dims, preferred_element_type=F32)


def iota(shape, dim, dtype=jnp.int32):
    return lax.broadcasted_iota(jnp.int32, shape, dim).astype(dtype)


def own_rows(m):
    return range(max(0, HALO - 8 * m), min(33, HALO + BLOCKS - 7 - 8 * m))


def reach_of(links, m, a):
    return links[pl.ds(64 * m + a, 8, stride=8), :] + iota((8, LANES), 1)


def pack_pair(x, y, table):
    most = jnp.max(jnp.maximum(jnp.abs(x), jnp.abs(y)), axis=0, keepdims=True)
    most = jnp.maximum(jnp.max(most, axis=1, keepdims=True), 1e-30)
    scale = 32767.0 / most

    def whole(v):
        v = v * scale
        return (v + jnp.where(v < 0.0, -0.5, 0.5)).astype(jnp.int32)

    table[0 : x.shape[0], :] = (whole(x) << 16) | (whole(y) & 65535)
    return most / 32767.0


def gather_rows(table, third, unit, links, m, a, hs, base):
    reach = reach_of(links, m, a)
    hi, lo = reach >> 7, reach & 127
    pair, single = jnp.zeros((8, LANES), jnp.int32), jnp.zeros((8, LANES), F32)
    for h in hs:
        here = hi == h
        rows = slice(8 * m + h - base, 8 * m + h - base + 8)
        pair = jnp.where(here, jnp.take_along_axis(table[rows, :], lo, axis=1), pair)
        single = jnp.where(here, jnp.take_along_axis(third[2, rows, :], lo, axis=1), single)
    return [(pair >> 16).astype(F32) * unit, ((pair << 16) >> 16).astype(F32) * unit, single]


def gather_kernel(own, links, nodal, table):
    unit = pack_pair(own[0], own[1], table)
    for m in range(BLOCKS // 8):
        for a in range(8):
            got = gather_rows(table, own, unit, links, m, a, own_rows(m), HALO)
            at = a * BLOCKS + 8 * m
            for i in range(3):
                nodal[i, at : at + 8, :] = got[i]


def element_kernel(parity, far, near, own, links, part, strain, edge_ref, yield_ref, ext, far_out, near_out, own_out,
                   disp, table, lo_s, hi_s, force_s, acc):
    odd = parity[0:1, :] == 1
    near_halo, far_halo = near[...].astype(F32), far[...].astype(F32)
    disp[:, 0:HALO, :] = jnp.where(odd, near_halo, far_halo)
    disp[:, HALO : HALO + BLOCKS, :] = own[...]
    disp[:, HALO + BLOCKS : 2 * HALO + BLOCKS, :] = jnp.where(odd, far_halo, near_halo)
    acc[...] = jnp.zeros_like(acc)
    unit = pack_pair(disp[0, : 2 * HALO + BLOCKS], disp[1, : 2 * HALO + BLOCKS], table)
    block = iota((8, LANES), 0) * LANES
    for m in range(BLOCKS // 8):
        rest = [h for h in range(33) if h not in own_rows(m)]
        nodal = []
        for a in range(8):
            at = slice(a * BLOCKS + 8 * m, a * BLOCKS + 8 * m + 8)
            got = gather_rows(table, disp, unit, links, m, a, rest, 0)
            nodal.append([got[i] + part[i, at, :] for i in range(3)])
            reach = reach_of(links, m, a) + block
            hi_s[at, :] = (reach >> 7).astype(F32)
            lo_s[at, :] = (reach & 127).astype(F32)
        edge = edge_ref[8 * m : 8 * m + 8, :]
        scale = 0.25 / edge
        grad = [[None] * 3 for _ in range(3)]
        for i in range(3):
            u = [nodal[a][i] for a in range(8)]
            for j in range(3):
                plus = [u[a] for a in range(8) if a >> j & 1]
                minus = [u[a] for a in range(8) if not a >> j & 1]
                total = sum(p - q for p, q in zip(plus, minus))
                grad[i][j] = total * scale
        old = [strain[c, 8 * m : 8 * m + 8, :] for c in range(6)]
        exx = grad[0][0] - old[0]
        eyy = grad[1][1] - old[1]
        ezz = grad[2][2] - old[2]
        exy = 0.5 * (grad[0][1] + grad[1][0]) - old[3]
        eyz = 0.5 * (grad[1][2] + grad[2][1]) - old[4]
        ezx = 0.5 * (grad[2][0] + grad[0][2]) - old[5]
        trace = exx + eyy + ezz
        sxx = trace + exx
        syy = trace + eyy
        szz = trace + ezz
        mean = (sxx + syy + szz) / 3.0
        dxx, dyy, dzz = sxx - mean, syy - mean, szz - mean
        size = jnp.sqrt(dxx * dxx + dyy * dyy + dzz * dzz + 2.0 * (exy * exy + eyz * eyz + ezx * ezx))
        radius = np.float32(np.sqrt(2.0 / 3.0)) * yield_ref[8 * m : 8 * m + 8, :]
        factor = radius / jnp.maximum(size, radius)
        area = 0.25 * edge * edge
        xy, yz, zx = area * factor * exy, area * factor * eyz, area * factor * ezx
        xx = area * (mean + factor * dxx)
        yy = area * (mean + factor * dyy)
        zz = area * (mean + factor * dzz)
        for i, (tx, ty, tz) in enumerate(((xx, xy, zx), (xy, yy, yz), (zx, yz, zz))):
            four = [tx + ty, ty - tx, tx - ty, -tx - ty]
            for a in range(8):
                pick = four[(0 if a & 1 else 1) if a & 2 else (2 if a & 1 else 3)]
                f = pick + tz if a & 4 else pick - tz
                force_s[i, a * BLOCKS + 8 * m : a * BLOCKS + 8 * m + 8, :] = f
    row = iota((16, LANES), 0, F32)
    rows = [(row + 16.0 * t).astype(BF16) for t in range(8)]
    zero = jnp.zeros((16, LANES), BF16)
    one = jnp.ones((16, LANES), BF16)

    def wide(ref, *at):
        return jnp.broadcast_to(ref[at], (16, LANES)).astype(BF16)

    for m in range(BLOCKS // 8):
        sums = jnp.zeros((3 * WINDOW, LANES), F32)
        for s in range(8):
            left, right = [], []
            for a in range(8):
                at = slice(a * BLOCKS + 8 * m + s, a * BLOCKS + 8 * m + s + 1)
                hi = wide(hi_s, at, slice(None))
                lo = wide(lo_s, at, slice(None))
                here = [hi == rows[t] for t in range(WINDOW // 16)]
                parts = []
                for i in range(3):
                    f = wide(force_s, i, at, slice(None))
                    parts += [jnp.where(h, f, zero) for h in here]
                left.append(jnp.concatenate(parts, axis=0))
                right.append(jnp.concatenate([jnp.where(lo == r, one, zero) for r in rows], axis=0))
            sums = sums + dot(jnp.concatenate(left, axis=1), jnp.concatenate(right, axis=1), NT)
        for i in range(3):
            acc[i, 8 * m : 8 * m + WINDOW, :] += sums[i * WINDOW : (i + 1) * WINDOW]
    low, high = acc[:, 0:HALO, :], acc[:, HALO + BLOCKS : 2 * HALO + BLOCKS, :]
    far_out[...] = jnp.where(odd, high, low).astype(BF16)
    near_out[...] = jnp.where(odd, low, high).astype(BF16)
    own_out[...] = acc[:, HALO : HALO + BLOCKS, :] - ext[...]


def finish_kernel(parity, own, far, near, force, out, force_out):
    odd = parity[0:1, :] == 1
    force_out[...] = force[...]
    near_sum, far_sum = near[...].astype(F32), far[...].astype(F32)
    out[:, 0:HALO, :] = own[:, 0:HALO, :] + jnp.where(odd, near_sum, far_sum)
    out[:, HALO:BLOCKS, :] = own[:, HALO:BLOCKS, :] + jnp.where(odd, far_sum, near_sum)


def pack_kernel(owner, where, active, disp, send, slots):
    names = iota((PEERS, SEG), 0)
    earlier = jnp.where(iota((SEG, SEG), 0) < iota((SEG, SEG), 1), 1.0, 0.0).astype(BF16)
    ones = jnp.ones((SEG, SEG), BF16)
    hot = [owner[k : k + 1, :] == names for k in range(2)]
    hot16 = [jnp.where(h, 1.0, 0.0).astype(BF16) for h in hot]
    before = [dot(hot16[0], earlier), dot(hot16[1], earlier) + dot(hot16[0], ones)]
    rows = iota((PEERS * SLOTS, SEG), 0)
    sent = jnp.zeros((PEERS * SLOTS, SEG), F32)
    meta = jnp.zeros((PEERS * SLOTS, SEG), F32)
    for k in range(2):
        rank = jnp.sum(jnp.where(hot[k], before[k], 0.0), axis=0, keepdims=True)
        slot = owner[k : k + 1, :] * SLOTS + rank.astype(jnp.int32)
        slots[k : k + 1, :] = slot
        mark = ((where[k : k + 1, :] + 1) * active[...]).astype(F32)
        here = slot == rows
        sent = jnp.where(here, 1.0, sent)
        meta = jnp.where(here, mark, meta)
    sent = sent.astype(BF16)
    for c in range(3):
        send[:, c * LANES : (c + 1) * LANES] = dot(sent, disp[c]).astype(BF16)
    send[:, 3 * LANES :] = dot(meta.astype(BF16), ones).astype(BF16)


def rows_kernel(gap, normal, mdisp, coupling, links, slots, quad_weight, rows, mortar, slots_out, weight):
    weight[...] = jnp.broadcast_to(quad_weight[...], weight.shape)
    slots_out[...] = slots[...]
    mortar[...] = mortar_of(coupling)
    total = gap[...]
    for c in range(3):
        n = normal[c]
        total = total + n * mdisp[c].astype(F32)
        rows[1 + c] = n
    rows[0] = total


def mortar_of(coupling):
    eye = jnp.where(iota((LANES, LANES), 0) == iota((LANES, LANES), 1), 1.0, 0.0)
    return (eye + coupling[...].astype(F32)).astype(BF16)


def split(x):
    top = x.astype(BF16)
    return top, (x - top.astype(F32)).astype(BF16)


def master_kernel(got, rows, mortar_ref, weight, back, force, held, table, sem):
    mortar = mortar_ref[...]
    for c in range(4):
        table[0:SEG, c * LANES : (c + 1) * LANES], table[SEG:, c * LANES : (c + 1) * LANES] = split(rows[c])
    name = iota((SEG, LANES), 1, F32) + 1.0
    parts = range(PEERS * SLOTS // SEG)
    hots, copies = [], []
    for part in parts:
        span = slice(part * SEG, (part + 1) * SEG)
        hot = jnp.where(got[span, 3 * LANES :].astype(F32) == name, 1.0, 0.0).astype(BF16)
        hots.append(hot)
        found = dot(jnp.concatenate([hot, hot], axis=1), table[...])
        gap = found[:, :LANES]
        normal = [found[:, (1 + c) * LANES : (2 + c) * LANES] for c in range(3)]
        for c in range(3):
            gap = gap - normal[c] * dot(got[span, c * LANES : (c + 1) * LANES], mortar)
        press = weight[0:1, :] * (2.0 * jnp.maximum(gap, 0.0))
        for c in range(3):
            held[span, c * LANES : (c + 1) * LANES] = (press * normal[c]).astype(BF16)
        copies.append(pltpu.make_async_copy(held.at[span], back.at[span], sem.at[part]))
        copies[-1].start()
    total = dot(jnp.concatenate(hots, axis=0), held[...], TN)
    for c in range(3):
        force[c] = -total[:, c * LANES : (c + 1) * LANES]
    for copy in copies:
        copy.wait()


def slave_kernel(got, slots, mortar_ref, out, held, sem):
    mortar = mortar_ref[...]
    place = []
    for part in range(PEERS * SLOTS // SEG):
        rows = iota((SEG, SEG), 0) + part * SEG
        here = (slots[0:1, :] == rows) | (slots[1:2, :] == rows)
        place.append(jnp.where(here, 1.0, 0.0).astype(BF16))
    pair = dot(jnp.concatenate(place, axis=0), got[...], TN).astype(BF16)
    copies = []
    for c in range(3):
        held[c] = dot(pair[:, c * LANES : (c + 1) * LANES], mortar, NT)
        copies.append(pltpu.make_async_copy(held.at[c], out.at[c], sem.at[c]))
        copies[-1].start()
    for copy in copies:
        copy.wait()


def shape(*dims, dtype=F32):
    return jax.ShapeDtypeStruct(dims, dtype)


VMEM = pl.BlockSpec(memory_space=pltpu.VMEM)


HBM = pl.BlockSpec(memory_space=pl.ANY)


def call(kernel, ins, outs, cost, scratch=(), grant=8 << 20, places=None):
    return pl.pallas_call(
        kernel,
        out_shape=outs,
        in_specs=[VMEM] * ins if ins > 0 else [pl.BlockSpec()] * -ins,
        out_specs=jax.tree.map(lambda _: VMEM, outs) if places is None else places,
        scratch_shapes=scratch,
        compiler_params=pltpu.CompilerParams(vmem_limit_bytes=grant),
        cost_estimate=pl.CostEstimate(flops=cost, bytes_accessed=1 << 20, transcendentals=0),
    )


def paired(block, first):
    route = [(i, i + 1) for i in range(first, PEERS - 1, 2)]
    return lax.ppermute(block, "dom", route + [(j, i) for i, j in route])


def swapped(block):
    return lax.ppermute(block, "body", [(0, 1), (1, 0)])


def exchanged(block):
    return lax.all_to_all(block, "dom", split_axis=0, concat_axis=0, tiled=True)


def local(
    displacement,
    connectivity,
    plastic_strain,
    element_size,
    yield_stress,
    external_force,
    slave_disp,
    pair_owner,
    pair_local,
    active,
    master_gap,
    master_normal,
    master_disp,
    coupling,
    quad_weight,
):
    seg_major = lambda x: jnp.transpose(x[0], (1, 0, 2))
    send, slots = call(
        pack_kernel,
        -4,
        (shape(PEERS * SLOTS, 4 * LANES, dtype=BF16), shape(2, SEG, dtype=jnp.int32)),
        1 << 27,
        grant=60 << 20,
        places=(pl.BlockSpec(), pl.BlockSpec()),
    )(pair_owner[0].T, pair_local[0].T, active, seg_major(slave_disp))
    got = exchanged(send)

    own = displacement[0].reshape(3, BLOCKS, LANES)
    odd = lax.axis_index("dom") & 1
    parity = jnp.full((8, LANES), odd, jnp.int32)
    first, last = own[:, :HALO], own[:, BLOCKS - HALO :]
    far = paired(jnp.where(odd == 1, last, first).astype(BF16), 1)
    near = paired(jnp.where(odd == 1, first, last).astype(BF16), 0)
    links = jnp.transpose(connectivity[0].reshape(8, BLOCKS, LANES), (1, 0, 2)).reshape(8 * BLOCKS, LANES)
    rows, mortar, slots, weight = call(
        rows_kernel,
        7,
        (
            shape(4, SEG, LANES),
            shape(LANES, LANES, dtype=BF16),
            shape(2, SEG, dtype=jnp.int32),
            shape(8, LANES),
        ),
        1 << 20,
    )(
        master_gap[0],
        seg_major(master_normal),
        seg_major(master_disp),
        coupling,
        links,
        slots,
        quad_weight.reshape(1, LANES),
    )
    rows = swapped(rows)
    part = call(
        gather_kernel, 2, shape(3, 8 * BLOCKS, LANES), 1 << 30, (pltpu.VMEM((BLOCKS, LANES), jnp.int32),)
    )(own, links)
    far_force, near_force, own_force = call(
        element_kernel,
        10,
        (
            shape(3, HALO, LANES, dtype=BF16),
            shape(3, HALO, LANES, dtype=BF16),
            shape(3, BLOCKS, LANES),
        ),
        1 << 32,
        (
            pltpu.VMEM((3, 2 * HALO + BLOCKS + 8, LANES), F32),
            pltpu.VMEM((2 * HALO + BLOCKS + 8, LANES), jnp.int32),
            pltpu.VMEM((8 * BLOCKS, LANES), F32),
            pltpu.VMEM((8 * BLOCKS, LANES), F32),
            pltpu.VMEM((3, 8 * BLOCKS, LANES), F32),
            pltpu.VMEM((3, 2 * HALO + BLOCKS + 16, LANES), F32),
        ),
    )(
        parity,
        far,
        near,
        own,
        links,
        part,
        plastic_strain[0].reshape(6, BLOCKS, LANES),
        element_size.reshape(BLOCKS, LANES),
        yield_stress.reshape(BLOCKS, LANES),
        external_force[0].reshape(3, BLOCKS, LANES),
    )

    got, far_force, near_force = lax.optimization_barrier((got, far_force, near_force))
    back, force = call(
        master_kernel,
        4,
        (shape(PEERS * SLOTS, 3 * LANES, dtype=BF16), shape(3, SEG, LANES)),
        1 << 28,
        (
            pltpu.VMEM((PEERS * SLOTS, 3 * LANES), BF16),
            pltpu.VMEM((2 * SEG, 4 * LANES), BF16),
            pltpu.SemaphoreType.DMA((4,)),
        ),
        places=(HBM, VMEM),
    )(got, rows, mortar, weight)
    returned = exchanged(back)
    slave_force = call(
        slave_kernel,
        3,
        shape(3, SEG, LANES),
        1 << 27,
        (pltpu.VMEM((3, SEG, LANES), F32), pltpu.SemaphoreType.DMA((3,))),
        places=HBM,
    )(returned, slots, mortar)
    residual, master_force = call(finish_kernel, 5, (shape(3, BLOCKS, LANES), shape(3, SEG, LANES)), 1 << 20)(
        parity, own_force, paired(far_force, 1), paired(near_force, 0), swapped(force)
    )
    return (
        residual.reshape(1, 3, BLOCKS * LANES),
        jnp.transpose(slave_force, (1, 0, 2))[None],
        jnp.transpose(master_force, (1, 0, 2))[None],
    )


def solution(mesh):
    return jax.shard_map(
        local,
        mesh=mesh,
        in_specs=(
            P("body", None, "dom"),
            P("body", None, "dom"),
            P("body", None, "dom"),
            P("body", "dom"),
            P("body", "dom"),
            P("body", None, "dom"),
            P("body", "dom", None, None),
            P("body", "dom", None),
            P("body", "dom", None),
            P("body", "dom"),
            P("body", "dom", None),
            P("body", "dom", None, None),
            P("body", "dom", None, None),
            P(),
            P(),
        ),
        out_specs=(
            P("body", None, "dom"),
            P("body", "dom", None, None),
            P("body", "dom", None, None),
        ),
        check_vma=False,
    )
```

```python
import jax
import jax.numpy as jnp
import numpy as np
from jax import lax
from jax.experimental import pallas as pl
from jax.experimental.pallas import tpu as pltpu
from jax.sharding import PartitionSpec as P


LANES = 128
HALO = 16
BLOCKS = 32
WINDOW = 48
SLOTS = 8
PEERS = 64
SEG = 128
F32 = jnp.float32
BF16 = jnp.bfloat16
NT = (((1,), (1,)), ((), ()))
TN = (((0,), (0,)), ((), ()))
NN = (((1,), (0,)), ((), ()))


def dot(a, b, dims=NN):
    return lax.dot_general(a, b, dims, preferred_element_type=F32)


def iota(shape, dim, dtype=jnp.int32):
    return lax.broadcasted_iota(jnp.int32, shape, dim).astype(dtype)


def own_rows(m):
    return range(max(0, HALO - 8 * m), min(33, HALO + BLOCKS - 7 - 8 * m))


def reach_of(links, m, a):
    return links[pl.ds(64 * m + a, 8, stride=8), :] + iota((8, LANES), 1)


def pack_pair(x, y, table):
    most = jnp.max(jnp.maximum(jnp.abs(x), jnp.abs(y)), axis=0, keepdims=True)
    most = jnp.maximum(jnp.max(most, axis=1, keepdims=True), 1e-30)
    scale = 32767.0 / most

    def whole(v):
        v = v * scale
        return (v + jnp.where(v < 0.0, -0.5, 0.5)).astype(jnp.int32)

    table[0 : x.shape[0], :] = (whole(x) << 16) | (whole(y) & 65535)
    return most / 32767.0


def gather_rows(table, third, unit, links, m, a, hs, base):
    reach = reach_of(links, m, a)
    hi, lo = reach >> 7, reach & 127
    pair, single = jnp.zeros((8, LANES), jnp.int32), jnp.zeros((8, LANES), F32)
    for h in hs:
        here = hi == h
        rows = slice(8 * m + h - base, 8 * m + h - base + 8)
        pair = jnp.where(here, jnp.take_along_axis(table[rows, :], lo, axis=1), pair)
        single = jnp.where(here, jnp.take_along_axis(third[2, rows, :], lo, axis=1), single)
    return [(pair >> 16).astype(F32) * unit, ((pair << 16) >> 16).astype(F32) * unit, single]


def gather_kernel(own, links, nodal, table):
    unit = pack_pair(own[0], own[1], table)
    for m in range(BLOCKS // 8):
        for a in range(8):
            got = gather_rows(table, own, unit, links, m, a, own_rows(m), HALO)
            at = a * BLOCKS + 8 * m
            for i in range(3):
                nodal[i, at : at + 8, :] = got[i]


def element_kernel(parity, far, near, own, links, part, strain, edge_ref, yield_ref, ext, far_out, near_out, own_out,
                   disp, table, lo_s, hi_s, force_s, acc):
    odd = parity[0:1, :] == 1
    near_halo, far_halo = near[...].astype(F32), far[...].astype(F32)
    disp[:, 0:HALO, :] = jnp.where(odd, near_halo, far_halo)
    disp[:, HALO : HALO + BLOCKS, :] = own[...]
    disp[:, HALO + BLOCKS : 2 * HALO + BLOCKS, :] = jnp.where(odd, far_halo, near_halo)
    acc[...] = jnp.zeros_like(acc)
    unit = pack_pair(disp[0, : 2 * HALO + BLOCKS], disp[1, : 2 * HALO + BLOCKS], table)
    block = iota((8, LANES), 0) * LANES
    for m in range(BLOCKS // 8):
        rest = [h for h in range(33) if h not in own_rows(m)]
        nodal = []
        for a in range(8):
            at = slice(a * BLOCKS + 8 * m, a * BLOCKS + 8 * m + 8)
            got = gather_rows(table, disp, unit, links, m, a, rest, 0)
            nodal.append([got[i] + part[i, at, :] for i in range(3)])
            reach = reach_of(links, m, a) + block
            hi_s[at, :] = (reach >> 7).astype(F32)
            lo_s[at, :] = (reach & 127).astype(F32)
        edge = edge_ref[8 * m : 8 * m + 8, :]
        scale = 0.25 / edge
        grad = [[None] * 3 for _ in range(3)]
        for i in range(3):
            u = [nodal[a][i] for a in range(8)]
            for j in range(3):
                plus = [u[a] for a in range(8) if a >> j & 1]
                minus = [u[a] for a in range(8) if not a >> j & 1]
                total = sum(p - q for p, q in zip(plus, minus))
                grad[i][j] = total * scale
        old = [strain[c, 8 * m : 8 * m + 8, :] for c in range(6)]
        exx = grad[0][0] - old[0]
        eyy = grad[1][1] - old[1]
        ezz = grad[2][2] - old[2]
        exy = 0.5 * (grad[0][1] + grad[1][0]) - old[3]
        eyz = 0.5 * (grad[1][2] + grad[2][1]) - old[4]
        ezx = 0.5 * (grad[2][0] + grad[0][2]) - old[5]
        trace = exx + eyy + ezz
        sxx = trace + exx
        syy = trace + eyy
        szz = trace + ezz
        mean = (sxx + syy + szz) / 3.0
        dxx, dyy, dzz = sxx - mean, syy - mean, szz - mean
        size = jnp.sqrt(dxx * dxx + dyy * dyy + dzz * dzz + 2.0 * (exy * exy + eyz * eyz + ezx * ezx))
        radius = np.float32(np.sqrt(2.0 / 3.0)) * yield_ref[8 * m : 8 * m + 8, :]
        factor = radius / jnp.maximum(size, radius)
        area = 0.25 * edge * edge
        xy, yz, zx = area * factor * exy, area * factor * eyz, area * factor * ezx
        xx = area * (mean + factor * dxx)
        yy = area * (mean + factor * dyy)
        zz = area * (mean + factor * dzz)
        for i, (tx, ty, tz) in enumerate(((xx, xy, zx), (xy, yy, yz), (zx, yz, zz))):
            four = [tx + ty, ty - tx, tx - ty, -tx - ty]
            for a in range(8):
                pick = four[(0 if a & 1 else 1) if a & 2 else (2 if a & 1 else 3)]
                f = pick + tz if a & 4 else pick - tz
                force_s[i, a * BLOCKS + 8 * m : a * BLOCKS + 8 * m + 8, :] = f
    row = iota((16, LANES), 0, F32)
    rows = [(row + 16.0 * t).astype(BF16) for t in range(8)]
    zero = jnp.zeros((16, LANES), BF16)
    one = jnp.ones((16, LANES), BF16)

    def wide(ref, *at):
        return jnp.broadcast_to(ref[at], (16, LANES)).astype(BF16)

    for m in range(BLOCKS // 8):
        sums = jnp.zeros((3 * WINDOW, LANES), F32)
        for s in range(8):
            left, right = [], []
            for a in range(8):
                at = slice(a * BLOCKS + 8 * m + s, a * BLOCKS + 8 * m + s + 1)
                hi = wide(hi_s, at, slice(None))
                lo = wide(lo_s, at, slice(None))
                here = [hi == rows[t] for t in range(WINDOW // 16)]
                parts = []
                for i in range(3):
                    f = wide(force_s, i, at, slice(None))
                    parts += [jnp.where(h, f, zero) for h in here]
                left.append(jnp.concatenate(parts, axis=0))
                right.append(jnp.concatenate([jnp.where(lo == r, one, zero) for r in rows], axis=0))
            sums = sums + dot(jnp.concatenate(left, axis=1), jnp.concatenate(right, axis=1), NT)
        for i in range(3):
            acc[i, 8 * m : 8 * m + WINDOW, :] += sums[i * WINDOW : (i + 1) * WINDOW]
    low, high = acc[:, 0:HALO, :], acc[:, HALO + BLOCKS : 2 * HALO + BLOCKS, :]
    far_out[...] = jnp.where(odd, high, low).astype(BF16)
    near_out[...] = jnp.where(odd, low, high).astype(BF16)
    own_out[...] = acc[:, HALO : HALO + BLOCKS, :] - ext[...]


def finish_kernel(parity, own, far, near, force, out, force_out):
    odd = parity[0:1, :] == 1
    force_out[...] = force[...]
    near_sum, far_sum = near[...].astype(F32), far[...].astype(F32)
    out[:, 0:HALO, :] = own[:, 0:HALO, :] + jnp.where(odd, near_sum, far_sum)
    out[:, HALO:BLOCKS, :] = own[:, HALO:BLOCKS, :] + jnp.where(odd, far_sum, near_sum)


def pack_kernel(owner_hbm, where_hbm, active_hbm, disp_hbm, send, slots, owner, where, active, disp, sem):
    ends = ((owner_hbm, owner), (where_hbm, where), (active_hbm, active), (disp_hbm, disp))
    copies = [pltpu.make_async_copy(source, target, sem.at[n]) for n, (source, target) in enumerate(ends)]
    for copy in copies:
        copy.start()
    names = iota((PEERS, SEG), 0)
    earlier = jnp.where(iota((SEG, SEG), 0) < iota((SEG, SEG), 1), 1.0, 0.0).astype(BF16)
    ones = jnp.ones((SEG, SEG), BF16)
    copies[0].wait()
    hot = [owner[k : k + 1, :] == names for k in range(2)]
    hot16 = [jnp.where(h, 1.0, 0.0).astype(BF16) for h in hot]
    before = [dot(hot16[0], earlier), dot(hot16[1], earlier) + dot(hot16[0], ones)]
    rows = iota((PEERS * SLOTS, SEG), 0)
    copies[1].wait()
    copies[2].wait()
    sent = jnp.zeros((PEERS * SLOTS, SEG), F32)
    meta = jnp.zeros((PEERS * SLOTS, SEG), F32)
    for k in range(2):
        rank = jnp.sum(jnp.where(hot[k], before[k], 0.0), axis=0, keepdims=True)
        slot = owner[k : k + 1, :] * SLOTS + rank.astype(jnp.int32)
        slots[k : k + 1, :] = slot
        mark = ((where[k : k + 1, :] + 1) * active[...]).astype(F32)
        here = slot == rows
        sent = jnp.where(here, 1.0, sent)
        meta = jnp.where(here, mark, meta)
    sent = sent.astype(BF16)
    copies[3].wait()
    for c in range(3):
        send[:, c * LANES : (c + 1) * LANES] = dot(sent, disp[c]).astype(BF16)
    send[:, 3 * LANES :] = dot(meta.astype(BF16), ones).astype(BF16)


def rows_kernel(gap, normal, mdisp, coupling, links, slots, quad_weight, rows, mortar, slots_out, weight):
    weight[...] = jnp.broadcast_to(quad_weight[...], weight.shape)
    slots_out[...] = slots[...]
    mortar[...] = mortar_of(coupling)
    total = gap[...]
    for c in range(3):
        n = normal[c]
        total = total + n * mdisp[c].astype(F32)
        rows[1 + c] = n
    rows[0] = total


def mortar_of(coupling):
    eye = jnp.where(iota((LANES, LANES), 0) == iota((LANES, LANES), 1), 1.0, 0.0)
    return (eye + coupling[...].astype(F32)).astype(BF16)


def split(x):
    top = x.astype(BF16)
    return top, (x - top.astype(F32)).astype(BF16)


def master_kernel(got, rows, mortar_ref, weight, back, force, held, table, sem):
    mortar = mortar_ref[...]
    for c in range(4):
        table[0:SEG, c * LANES : (c + 1) * LANES], table[SEG:, c * LANES : (c + 1) * LANES] = split(rows[c])
    name = iota((SEG, LANES), 1, F32) + 1.0
    parts = range(PEERS * SLOTS // SEG)
    hots, copies = [], []
    for part in parts:
        span = slice(part * SEG, (part + 1) * SEG)
        hot = jnp.where(got[span, 3 * LANES :].astype(F32) == name, 1.0, 0.0).astype(BF16)
        hots.append(hot)
        found = dot(jnp.concatenate([hot, hot], axis=1), table[...])
        gap = found[:, :LANES]
        normal = [found[:, (1 + c) * LANES : (2 + c) * LANES] for c in range(3)]
        for c in range(3):
            gap = gap - normal[c] * dot(got[span, c * LANES : (c + 1) * LANES], mortar)
        press = weight[0:1, :] * (2.0 * jnp.maximum(gap, 0.0))
        for c in range(3):
            held[span, c * LANES : (c + 1) * LANES] = (press * normal[c]).astype(BF16)
        copies.append(pltpu.make_async_copy(held.at[span], back.at[span], sem.at[part]))
        copies[-1].start()
    total = dot(jnp.concatenate(hots, axis=0), held[...], TN)
    for c in range(3):
        force[c] = -total[:, c * LANES : (c + 1) * LANES]
    for copy in copies:
        copy.wait()


def slave_kernel(got, slots, mortar_ref, out, held, sem):
    mortar = mortar_ref[...]
    place = []
    for part in range(PEERS * SLOTS // SEG):
        rows = iota((SEG, SEG), 0) + part * SEG
        here = (slots[0:1, :] == rows) | (slots[1:2, :] == rows)
        place.append(jnp.where(here, 1.0, 0.0).astype(BF16))
    pair = dot(jnp.concatenate(place, axis=0), got[...], TN).astype(BF16)
    copies = []
    for c in range(3):
        held[c] = dot(pair[:, c * LANES : (c + 1) * LANES], mortar, NT)
        copies.append(pltpu.make_async_copy(held.at[c], out.at[c], sem.at[c]))
        copies[-1].start()
    for copy in copies:
        copy.wait()


def shape(*dims, dtype=F32):
    return jax.ShapeDtypeStruct(dims, dtype)


VMEM = pl.BlockSpec(memory_space=pltpu.VMEM)


HBM = pl.BlockSpec(memory_space=pl.ANY)


def call(kernel, ins, outs, cost, scratch=(), grant=8 << 20, places=None):
    return pl.pallas_call(
        kernel,
        out_shape=outs,
        in_specs=[VMEM] * ins if ins > 0 else [HBM] * -ins,
        out_specs=jax.tree.map(lambda _: VMEM, outs) if places is None else places,
        scratch_shapes=scratch,
        compiler_params=pltpu.CompilerParams(vmem_limit_bytes=grant),
        cost_estimate=pl.CostEstimate(flops=cost, bytes_accessed=1 << 20, transcendentals=0),
    )


def paired(block, first):
    route = [(i, i + 1) for i in range(first, PEERS - 1, 2)]
    return lax.ppermute(block, "dom", route + [(j, i) for i, j in route])


def swapped(block):
    return lax.ppermute(block, "body", [(0, 1), (1, 0)])


def exchanged(block):
    return lax.all_to_all(block, "dom", split_axis=0, concat_axis=0, tiled=True)


def local(
    displacement,
    connectivity,
    plastic_strain,
    element_size,
    yield_stress,
    external_force,
    slave_disp,
    pair_owner,
    pair_local,
    active,
    master_gap,
    master_normal,
    master_disp,
    coupling,
    quad_weight,
):
    seg_major = lambda x: jnp.transpose(x[0], (1, 0, 2))
    send, slots = call(
        pack_kernel,
        -4,
        (shape(PEERS * SLOTS, 4 * LANES, dtype=BF16), shape(2, SEG, dtype=jnp.int32)),
        1 << 27,
        (
            pltpu.VMEM((2, SEG), jnp.int32),
            pltpu.VMEM((2, SEG), jnp.int32),
            pltpu.VMEM((1, SEG), jnp.int32),
            pltpu.VMEM((3, SEG, LANES), BF16),
            pltpu.SemaphoreType.DMA((4,)),
        ),
        grant=60 << 20,
        places=(pl.BlockSpec(), pl.BlockSpec()),
    )(pair_owner[0].T, pair_local[0].T, active, seg_major(slave_disp))
    got = exchanged(send)

    own = displacement[0].reshape(3, BLOCKS, LANES)
    odd = lax.axis_index("dom") & 1
    parity = jnp.full((8, LANES), odd, jnp.int32)
    first, last = own[:, :HALO], own[:, BLOCKS - HALO :]
    far = paired(jnp.where(odd == 1, last, first).astype(BF16), 1)
    near = paired(jnp.where(odd == 1, first, last).astype(BF16), 0)
    links = jnp.transpose(connectivity[0].reshape(8, BLOCKS, LANES), (1, 0, 2)).reshape(8 * BLOCKS, LANES)
    rows, mortar, slots, weight = call(
        rows_kernel,
        7,
        (
            shape(4, SEG, LANES),
            shape(LANES, LANES, dtype=BF16),
            shape(2, SEG, dtype=jnp.int32),
            shape(8, LANES),
        ),
        1 << 20,
    )(
        master_gap[0],
        seg_major(master_normal),
        seg_major(master_disp),
        coupling,
        links,
        slots,
        quad_weight.reshape(1, LANES),
    )
    rows = swapped(rows)
    part = call(
        gather_kernel, 2, shape(3, 8 * BLOCKS, LANES), 1 << 30, (pltpu.VMEM((BLOCKS, LANES), jnp.int32),)
    )(own, links)
    far_force, near_force, own_force = call(
        element_kernel,
        10,
        (
            shape(3, HALO, LANES, dtype=BF16),
            shape(3, HALO, LANES, dtype=BF16),
            shape(3, BLOCKS, LANES),
        ),
        1 << 32,
        (
            pltpu.VMEM((3, 2 * HALO + BLOCKS + 8, LANES), F32),
            pltpu.VMEM((2 * HALO + BLOCKS + 8, LANES), jnp.int32),
            pltpu.VMEM((8 * BLOCKS, LANES), F32),
            pltpu.VMEM((8 * BLOCKS, LANES), F32),
            pltpu.VMEM((3, 8 * BLOCKS, LANES), F32),
            pltpu.VMEM((3, 2 * HALO + BLOCKS + 16, LANES), F32),
        ),
    )(
        parity,
        far,
        near,
        own,
        links,
        part,
        plastic_strain[0].reshape(6, BLOCKS, LANES),
        element_size.reshape(BLOCKS, LANES),
        yield_stress.reshape(BLOCKS, LANES),
        external_force[0].reshape(3, BLOCKS, LANES),
    )

    got, far_force, near_force = lax.optimization_barrier((got, far_force, near_force))
    back, force = call(
        master_kernel,
        4,
        (shape(PEERS * SLOTS, 3 * LANES, dtype=BF16), shape(3, SEG, LANES)),
        1 << 28,
        (
            pltpu.VMEM((PEERS * SLOTS, 3 * LANES), BF16),
            pltpu.VMEM((2 * SEG, 4 * LANES), BF16),
            pltpu.SemaphoreType.DMA((4,)),
        ),
        places=(HBM, VMEM),
    )(got, rows, mortar, weight)
    returned = exchanged(back)
    slave_force = call(
        slave_kernel,
        3,
        shape(3, SEG, LANES),
        1 << 27,
        (pltpu.VMEM((3, SEG, LANES), F32), pltpu.SemaphoreType.DMA((3,))),
        places=HBM,
    )(returned, slots, mortar)
    residual, master_force = call(finish_kernel, 5, (shape(3, BLOCKS, LANES), shape(3, SEG, LANES)), 1 << 20)(
        parity, own_force, paired(far_force, 1), paired(near_force, 0), swapped(force)
    )
    return (
        residual.reshape(1, 3, BLOCKS * LANES),
        jnp.transpose(slave_force, (1, 0, 2))[None],
        jnp.transpose(master_force, (1, 0, 2))[None],
    )


def solution(mesh):
    return jax.shard_map(
        local,
        mesh=mesh,
        in_specs=(
            P("body", None, "dom"),
            P("body", None, "dom"),
            P("body", None, "dom"),
            P("body", "dom"),
            P("body", "dom"),
            P("body", None, "dom"),
            P("body", "dom", None, None),
            P("body", "dom", None),
            P("body", "dom", None),
            P("body", "dom"),
            P("body", "dom", None),
            P("body", "dom", None, None),
            P("body", "dom", None, None),
            P(),
            P(),
        ),
        out_specs=(
            P("body", None, "dom"),
            P("body", "dom", None, None),
            P("body", "dom", None, None),
        ),
        check_vma=False,
    )
```

```python
import jax
import jax.numpy as jnp
import numpy as np
from jax import lax
from jax.experimental import pallas as pl
from jax.experimental.pallas import tpu as pltpu
from jax.sharding import PartitionSpec as P


LANES = 128
HALO = 16
BLOCKS = 32
WINDOW = 48
SLOTS = 8
PEERS = 64
STRIDE, INVERSE = 27, 19
SEG = 128
F32 = jnp.float32
BF16 = jnp.bfloat16
NT = (((1,), (1,)), ((), ()))
TN = (((0,), (0,)), ((), ()))
NN = (((1,), (0,)), ((), ()))


def dot(a, b, dims=NN):
    return lax.dot_general(a, b, dims, preferred_element_type=F32)


def iota(shape, dim, dtype=jnp.int32):
    return lax.broadcasted_iota(jnp.int32, shape, dim).astype(dtype)


def own_rows(m):
    return range(max(0, HALO - 8 * m), min(33, HALO + BLOCKS - 7 - 8 * m))


def reach_of(links, m, a):
    return links[pl.ds(64 * m + a, 8, stride=8), :] + iota((8, LANES), 1)


def pack_pair(x, y, table):
    most = jnp.max(jnp.maximum(jnp.abs(x), jnp.abs(y)), axis=0, keepdims=True)
    most = jnp.maximum(jnp.max(most, axis=1, keepdims=True), 1e-30)
    scale = 32767.0 / most

    def whole(v):
        v = v * scale
        return (v + jnp.where(v < 0.0, -0.5, 0.5)).astype(jnp.int32)

    table[0 : x.shape[0], :] = (whole(x) << 16) | (whole(y) & 65535)
    return most / 32767.0


def gather_rows(table, third, unit, links, m, a, hs, base):
    reach = reach_of(links, m, a)
    hi, lo = reach >> 7, reach & 127
    pair, single = jnp.zeros((8, LANES), jnp.int32), jnp.zeros((8, LANES), F32)
    for h in hs:
        here = hi == h
        rows = slice(8 * m + h - base, 8 * m + h - base + 8)
        pair = jnp.where(here, jnp.take_along_axis(table[rows, :], lo, axis=1), pair)
        single = jnp.where(here, jnp.take_along_axis(third[2, rows, :], lo, axis=1), single)
    return [(pair >> 16).astype(F32) * unit, ((pair << 16) >> 16).astype(F32) * unit, single]


def gather_kernel(own, links, nodal, table):
    unit = pack_pair(own[0], own[1], table)
    for m in range(BLOCKS // 8):
        for a in range(8):
            got = gather_rows(table, own, unit, links, m, a, own_rows(m), HALO)
            at = a * BLOCKS + 8 * m
            for i in range(3):
                nodal[i, at : at + 8, :] = got[i]


def element_kernel(parity, far, near, own, links, part, strain, edge_ref, yield_ref, ext, far_out, near_out, own_out,
                   disp, table, lo_s, hi_s, force_s, acc):
    odd = parity[0:1, :] == 1
    near_halo, far_halo = near[...].astype(F32), far[...].astype(F32)
    disp[:, 0:HALO, :] = jnp.where(odd, near_halo, far_halo)
    disp[:, HALO : HALO + BLOCKS, :] = own[...]
    disp[:, HALO + BLOCKS : 2 * HALO + BLOCKS, :] = jnp.where(odd, far_halo, near_halo)
    acc[...] = jnp.zeros_like(acc)
    unit = pack_pair(disp[0, : 2 * HALO + BLOCKS], disp[1, : 2 * HALO + BLOCKS], table)
    block = iota((8, LANES), 0) * LANES
    for m in range(BLOCKS // 8):
        rest = [h for h in range(33) if h not in own_rows(m)]
        nodal = []
        for a in range(8):
            at = slice(a * BLOCKS + 8 * m, a * BLOCKS + 8 * m + 8)
            got = gather_rows(table, disp, unit, links, m, a, rest, 0)
            nodal.append([got[i] + part[i, at, :] for i in range(3)])
            reach = reach_of(links, m, a) + block
            hi_s[at, :] = (reach >> 7).astype(F32)
            lo_s[at, :] = (reach & 127).astype(F32)
        edge = edge_ref[8 * m : 8 * m + 8, :]
        scale = 0.25 / edge
        grad = [[None] * 3 for _ in range(3)]
        for i in range(3):
            u = [nodal[a][i] for a in range(8)]
            for j in range(3):
                plus = [u[a] for a in range(8) if a >> j & 1]
                minus = [u[a] for a in range(8) if not a >> j & 1]
                total = sum(p - q for p, q in zip(plus, minus))
                grad[i][j] = total * scale
        old = [strain[c, 8 * m : 8 * m + 8, :] for c in range(6)]
        exx = grad[0][0] - old[0]
        eyy = grad[1][1] - old[1]
        ezz = grad[2][2] - old[2]
        exy = 0.5 * (grad[0][1] + grad[1][0]) - old[3]
        eyz = 0.5 * (grad[1][2] + grad[2][1]) - old[4]
        ezx = 0.5 * (grad[2][0] + grad[0][2]) - old[5]
        trace = exx + eyy + ezz
        sxx = trace + exx
        syy = trace + eyy
        szz = trace + ezz
        mean = (sxx + syy + szz) / 3.0
        dxx, dyy, dzz = sxx - mean, syy - mean, szz - mean
        size = jnp.sqrt(dxx * dxx + dyy * dyy + dzz * dzz + 2.0 * (exy * exy + eyz * eyz + ezx * ezx))
        radius = np.float32(np.sqrt(2.0 / 3.0)) * yield_ref[8 * m : 8 * m + 8, :]
        factor = radius / jnp.maximum(size, radius)
        area = 0.25 * edge * edge
        xy, yz, zx = area * factor * exy, area * factor * eyz, area * factor * ezx
        xx = area * (mean + factor * dxx)
        yy = area * (mean + factor * dyy)
        zz = area * (mean + factor * dzz)
        for i, (tx, ty, tz) in enumerate(((xx, xy, zx), (xy, yy, yz), (zx, yz, zz))):
            four = [tx + ty, ty - tx, tx - ty, -tx - ty]
            for a in range(8):
                pick = four[(0 if a & 1 else 1) if a & 2 else (2 if a & 1 else 3)]
                f = pick + tz if a & 4 else pick - tz
                force_s[i, a * BLOCKS + 8 * m : a * BLOCKS + 8 * m + 8, :] = f
    row = iota((16, LANES), 0, F32)
    rows = [(row + 16.0 * t).astype(BF16) for t in range(8)]
    zero = jnp.zeros((16, LANES), BF16)
    one = jnp.ones((16, LANES), BF16)

    def wide(ref, *at):
        return jnp.broadcast_to(ref[at], (16, LANES)).astype(BF16)

    for m in range(BLOCKS // 8):
        sums = jnp.zeros((3 * WINDOW, LANES), F32)
        for s in range(8):
            left, right = [], []
            for a in range(8):
                at = slice(a * BLOCKS + 8 * m + s, a * BLOCKS + 8 * m + s + 1)
                hi = wide(hi_s, at, slice(None))
                lo = wide(lo_s, at, slice(None))
                here = [hi == rows[t] for t in range(WINDOW // 16)]
                parts = []
                for i in range(3):
                    f = wide(force_s, i, at, slice(None))
                    parts += [jnp.where(h, f, zero) for h in here]
                left.append(jnp.concatenate(parts, axis=0))
                right.append(jnp.concatenate([jnp.where(lo == r, one, zero) for r in rows], axis=0))
            sums = sums + dot(jnp.concatenate(left, axis=1), jnp.concatenate(right, axis=1), NT)
        for i in range(3):
            acc[i, 8 * m : 8 * m + WINDOW, :] += sums[i * WINDOW : (i + 1) * WINDOW]
    low, high = acc[:, 0:HALO, :], acc[:, HALO + BLOCKS : 2 * HALO + BLOCKS, :]
    far_out[...] = jnp.where(odd, high, low).astype(BF16)
    near_out[...] = jnp.where(odd, low, high).astype(BF16)
    own_out[...] = acc[:, HALO : HALO + BLOCKS, :] - ext[...]


def finish_kernel(parity, own, far, near, force, out, force_out):
    odd = parity[0:1, :] == 1
    force_out[...] = force[...]
    near_sum, far_sum = near[...].astype(F32), far[...].astype(F32)
    out[:, 0:HALO, :] = own[:, 0:HALO, :] + jnp.where(odd, near_sum, far_sum)
    out[:, HALO:BLOCKS, :] = own[:, HALO:BLOCKS, :] + jnp.where(odd, far_sum, near_sum)


def pack_kernel(owner_hbm, where_hbm, active_hbm, disp_hbm, send, slots, owner, where, active, disp, sem):
    ends = ((owner_hbm, owner), (where_hbm, where), (active_hbm, active), (disp_hbm, disp))
    copies = [pltpu.make_async_copy(source, target, sem.at[n]) for n, (source, target) in enumerate(ends)]
    for copy in copies:
        copy.start()
    names = iota((PEERS, SEG), 0)
    earlier = jnp.where(iota((SEG, SEG), 0) < iota((SEG, SEG), 1), 1.0, 0.0).astype(BF16)
    ones = jnp.ones((SEG, SEG), BF16)
    copies[0].wait()
    hot = [owner[k : k + 1, :] == names for k in range(2)]
    hot16 = [jnp.where(h, 1.0, 0.0).astype(BF16) for h in hot]
    before = [dot(hot16[0], earlier), dot(hot16[1], earlier) + dot(hot16[0], ones)]
    rows = iota((PEERS * SLOTS, SEG), 0)
    copies[1].wait()
    copies[2].wait()
    sent = jnp.zeros((PEERS * SLOTS, SEG), F32)
    meta = jnp.zeros((PEERS * SLOTS, SEG), F32)
    for k in range(2):
        rank = jnp.sum(jnp.where(hot[k], before[k], 0.0), axis=0, keepdims=True)
        slot = (owner[k : k + 1, :] * INVERSE & (PEERS - 1)) * SLOTS + rank.astype(jnp.int32)
        slots[k : k + 1, :] = slot
        mark = ((where[k : k + 1, :] + 1) * active[...]).astype(F32)
        here = slot == rows
        sent = jnp.where(here, 1.0, sent)
        meta = jnp.where(here, mark, meta)
    sent = sent.astype(BF16)
    copies[3].wait()
    for c in range(3):
        send[:, c * LANES : (c + 1) * LANES] = dot(sent, disp[c]).astype(BF16)
    send[:, 3 * LANES :] = dot(meta.astype(BF16), ones).astype(BF16)


def rows_kernel(gap, normal, mdisp, coupling, links, slots, quad_weight, rows, mortar, slots_out, weight):
    weight[...] = jnp.broadcast_to(quad_weight[...], weight.shape)
    slots_out[...] = slots[...]
    mortar[...] = mortar_of(coupling)
    total = gap[...]
    for c in range(3):
        n = normal[c]
        total = total + n * mdisp[c].astype(F32)
        rows[1 + c] = n
    rows[0] = total


def mortar_of(coupling):
    eye = jnp.where(iota((LANES, LANES), 0) == iota((LANES, LANES), 1), 1.0, 0.0)
    return (eye + coupling[...].astype(F32)).astype(BF16)


def split(x):
    top = x.astype(BF16)
    return top, (x - top.astype(F32)).astype(BF16)


def master_kernel(got, rows, mortar_ref, weight, back, force, held, table, sem):
    mortar = mortar_ref[...]
    for c in range(4):
        table[0:SEG, c * LANES : (c + 1) * LANES], table[SEG:, c * LANES : (c + 1) * LANES] = split(rows[c])
    name = iota((SEG, LANES), 1, F32) + 1.0
    parts = range(PEERS * SLOTS // SEG)
    hots, copies = [], []
    for part in parts:
        span = slice(part * SEG, (part + 1) * SEG)
        hot = jnp.where(got[span, 3 * LANES :].astype(F32) == name, 1.0, 0.0).astype(BF16)
        hots.append(hot)
        found = dot(jnp.concatenate([hot, hot], axis=1), table[...])
        gap = found[:, :LANES]
        normal = [found[:, (1 + c) * LANES : (2 + c) * LANES] for c in range(3)]
        for c in range(3):
            gap = gap - normal[c] * dot(got[span, c * LANES : (c + 1) * LANES], mortar)
        press = weight[0:1, :] * (2.0 * jnp.maximum(gap, 0.0))
        for c in range(3):
            held[span, c * LANES : (c + 1) * LANES] = (press * normal[c]).astype(BF16)
        copies.append(pltpu.make_async_copy(held.at[span], back.at[span], sem.at[part]))
        copies[-1].start()
    total = dot(jnp.concatenate(hots, axis=0), held[...], TN)
    for c in range(3):
        force[c] = -total[:, c * LANES : (c + 1) * LANES]
    for copy in copies:
        copy.wait()


def slave_kernel(got, slots, mortar_ref, out, held, sem):
    mortar = mortar_ref[...]
    place = []
    for part in range(PEERS * SLOTS // SEG):
        rows = iota((SEG, SEG), 0) + part * SEG
        here = (slots[0:1, :] == rows) | (slots[1:2, :] == rows)
        place.append(jnp.where(here, 1.0, 0.0).astype(BF16))
    pair = dot(jnp.concatenate(place, axis=0), got[...], TN).astype(BF16)
    copies = []
    for c in range(3):
        held[c] = dot(pair[:, c * LANES : (c + 1) * LANES], mortar, NT)
        copies.append(pltpu.make_async_copy(held.at[c], out.at[c], sem.at[c]))
        copies[-1].start()
    for copy in copies:
        copy.wait()


def shape(*dims, dtype=F32):
    return jax.ShapeDtypeStruct(dims, dtype)


VMEM = pl.BlockSpec(memory_space=pltpu.VMEM)


HBM = pl.BlockSpec(memory_space=pl.ANY)


def call(kernel, ins, outs, cost, scratch=(), grant=8 << 20, places=None):
    return pl.pallas_call(
        kernel,
        out_shape=outs,
        in_specs=[VMEM] * ins if ins > 0 else [HBM] * -ins,
        out_specs=jax.tree.map(lambda _: VMEM, outs) if places is None else places,
        scratch_shapes=scratch,
        compiler_params=pltpu.CompilerParams(vmem_limit_bytes=grant),
        cost_estimate=pl.CostEstimate(flops=cost, bytes_accessed=1 << 20, transcendentals=0),
    )


def paired(block, first):
    route = [(i, i + 1) for i in range(first, PEERS - 1, 2)]
    return lax.ppermute(block, "dom", route + [(j, i) for i, j in route])


def swapped(block):
    return lax.ppermute(block, "body", [(0, 1), (1, 0)])


def exchanged(block):
    order = [STRIDE * i % PEERS for i in range(PEERS)]
    return lax.all_to_all(
        block, "dom", split_axis=0, concat_axis=0, axis_index_groups=[order], tiled=True
    )


def local(
    displacement,
    connectivity,
    plastic_strain,
    element_size,
    yield_stress,
    external_force,
    slave_disp,
    pair_owner,
    pair_local,
    active,
    master_gap,
    master_normal,
    master_disp,
    coupling,
    quad_weight,
):
    seg_major = lambda x: jnp.transpose(x[0], (1, 0, 2))
    send, slots = call(
        pack_kernel,
        -4,
        (shape(PEERS * SLOTS, 4 * LANES, dtype=BF16), shape(2, SEG, dtype=jnp.int32)),
        1 << 27,
        (
            pltpu.VMEM((2, SEG), jnp.int32),
            pltpu.VMEM((2, SEG), jnp.int32),
            pltpu.VMEM((1, SEG), jnp.int32),
            pltpu.VMEM((3, SEG, LANES), BF16),
            pltpu.SemaphoreType.DMA((4,)),
        ),
        grant=60 << 20,
        places=(pl.BlockSpec(), pl.BlockSpec()),
    )(pair_owner[0].T, pair_local[0].T, active, seg_major(slave_disp))
    got = exchanged(send)

    own = displacement[0].reshape(3, BLOCKS, LANES)
    odd = lax.axis_index("dom") & 1
    parity = jnp.full((8, LANES), odd, jnp.int32)
    first, last = own[:, :HALO], own[:, BLOCKS - HALO :]
    far = paired(jnp.where(odd == 1, last, first).astype(BF16), 1)
    near = paired(jnp.where(odd == 1, first, last).astype(BF16), 0)
    links = jnp.transpose(connectivity[0].reshape(8, BLOCKS, LANES), (1, 0, 2)).reshape(8 * BLOCKS, LANES)
    rows, mortar, slots, weight = call(
        rows_kernel,
        7,
        (
            shape(4, SEG, LANES),
            shape(LANES, LANES, dtype=BF16),
            shape(2, SEG, dtype=jnp.int32),
            shape(8, LANES),
        ),
        1 << 20,
    )(
        master_gap[0],
        seg_major(master_normal),
        seg_major(master_disp),
        coupling,
        links,
        slots,
        quad_weight.reshape(1, LANES),
    )
    rows = swapped(rows)
    part = call(
        gather_kernel, 2, shape(3, 8 * BLOCKS, LANES), 1 << 30, (pltpu.VMEM((BLOCKS, LANES), jnp.int32),)
    )(own, links)
    far_force, near_force, own_force = call(
        element_kernel,
        10,
        (
            shape(3, HALO, LANES, dtype=BF16),
            shape(3, HALO, LANES, dtype=BF16),
            shape(3, BLOCKS, LANES),
        ),
        1 << 32,
        (
            pltpu.VMEM((3, 2 * HALO + BLOCKS + 8, LANES), F32),
            pltpu.VMEM((2 * HALO + BLOCKS + 8, LANES), jnp.int32),
            pltpu.VMEM((8 * BLOCKS, LANES), F32),
            pltpu.VMEM((8 * BLOCKS, LANES), F32),
            pltpu.VMEM((3, 8 * BLOCKS, LANES), F32),
            pltpu.VMEM((3, 2 * HALO + BLOCKS + 16, LANES), F32),
        ),
    )(
        parity,
        far,
        near,
        own,
        links,
        part,
        plastic_strain[0].reshape(6, BLOCKS, LANES),
        element_size.reshape(BLOCKS, LANES),
        yield_stress.reshape(BLOCKS, LANES),
        external_force[0].reshape(3, BLOCKS, LANES),
    )

    got, far_force, near_force = lax.optimization_barrier((got, far_force, near_force))
    back, force = call(
        master_kernel,
        4,
        (shape(PEERS * SLOTS, 3 * LANES, dtype=BF16), shape(3, SEG, LANES)),
        1 << 28,
        (
            pltpu.VMEM((PEERS * SLOTS, 3 * LANES), BF16),
            pltpu.VMEM((2 * SEG, 4 * LANES), BF16),
            pltpu.SemaphoreType.DMA((4,)),
        ),
        places=(HBM, VMEM),
    )(got, rows, mortar, weight)
    returned = exchanged(back)
    slave_force = call(
        slave_kernel,
        3,
        shape(3, SEG, LANES),
        1 << 27,
        (pltpu.VMEM((3, SEG, LANES), F32), pltpu.SemaphoreType.DMA((3,))),
        places=HBM,
    )(returned, slots, mortar)
    residual, master_force = call(finish_kernel, 5, (shape(3, BLOCKS, LANES), shape(3, SEG, LANES)), 1 << 20)(
        parity, own_force, paired(far_force, 1), paired(near_force, 0), swapped(force)
    )
    return (
        residual.reshape(1, 3, BLOCKS * LANES),
        jnp.transpose(slave_force, (1, 0, 2))[None],
        jnp.transpose(master_force, (1, 0, 2))[None],
    )


def solution(mesh):
    return jax.shard_map(
        local,
        mesh=mesh,
        in_specs=(
            P("body", None, "dom"),
            P("body", None, "dom"),
            P("body", None, "dom"),
            P("body", "dom"),
            P("body", "dom"),
            P("body", None, "dom"),
            P("body", "dom", None, None),
            P("body", "dom", None),
            P("body", "dom", None),
            P("body", "dom"),
            P("body", "dom", None),
            P("body", "dom", None, None),
            P("body", "dom", None, None),
            P(),
            P(),
        ),
        out_specs=(
            P("body", None, "dom"),
            P("body", "dom", None, None),
            P("body", "dom", None, None),
        ),
        check_vma=False,
    )
```
